32 devices in a mesh: dp: 8 (over y, x, core), fsdp: 4 (over z).
Axes of the slice: x: 2, y: 2, z: 4, core: 2. Of those that a mesh axis runs over, the one named last changes fastest.
Arguments:
- patches: bfloat16 [32768, 768], P(('dp', 'fsdp')), may hold values from -6 to 6
- picture_ids: int32 [32768], P(('dp', 'fsdp')), may hold values from 0 to 10, as said below
- norm1_gain: bfloat16 [768], P(('dp', 'fsdp')), may hold values from 0.5 to 1.5
- norm1_bias: bfloat16 [768], P(('dp', 'fsdp')), may hold values from -1.75 to 1.75
- qkv_weight: bfloat16 [768, 2304], P(('dp', 'fsdp')), may hold values from -0.21875 to 0.21875
- query_shift: bfloat16 [768], P(('dp', 'fsdp')), may hold values from -3 to 3
- value_shift: bfloat16 [768], P(('dp', 'fsdp')), may hold values from -3 to 3
- query_gain: bfloat16 [768], P(('dp', 'fsdp')), may hold values from 0.5 to 1.5
- query_bias: bfloat16 [768], P(('dp', 'fsdp')), may hold values from -3 to 3
- key_gain: bfloat16 [768], P(('dp', 'fsdp')), may hold values from 0.5 to 1.5
- out_weight: bfloat16 [768, 768], P(('dp', 'fsdp')), may hold values from -6 to 6
- out_bias: bfloat16 [768], P(('dp', 'fsdp')), may hold values from -1.75 to 1.75
- norm2_gain: bfloat16 [768], P(('dp', 'fsdp')), may hold values from 0.5 to 1.5
- norm2_bias: bfloat16 [768], P(('dp', 'fsdp')), may hold values from -1.75 to 1.75
- up_weight: bfloat16 [768, 3072], P(('dp', 'fsdp')), may hold values from -0.21875 to 0.21875
- up_bias: bfloat16 [3072], P(('dp', 'fsdp')), may hold values from -3 to 3
- down_weight: bfloat16 [3072, 768], P(('dp', 'fsdp')), may hold values from -0.109375 to 0.109375
- down_bias: bfloat16 [768], P(('dp', 'fsdp')), may hold values from -1.75 to 1.75
- out_grad: bfloat16 [32768, 768], P(('dp', 'fsdp')), may hold values from -6 to 6
Outputs:
- mixed_out: bfloat16 [32768, 768], P(('dp', 'fsdp'))
- patches_grad: float32 [32768, 768], P(('dp', 'fsdp'))
- norm1_gain_grad: float32 [768], P(('dp', 'fsdp'))
- norm1_bias_grad: float32 [768], P(('dp', 'fsdp'))
- qkv_weight_grad: float32 [768, 2304], P(('dp', 'fsdp'))
- query_shift_grad: float32 [768], P(('dp', 'fsdp'))
- value_shift_grad: float32 [768], P(('dp', 'fsdp'))
- query_gain_grad: float32 [768], P(('dp', 'fsdp'))
- query_bias_grad: float32 [768], P(('dp', 'fsdp'))
- key_gain_grad: float32 [768], P(('dp', 'fsdp'))
- out_weight_grad: float32 [768, 768], P(('dp', 'fsdp'))
- out_bias_grad: float32 [768], P(('dp', 'fsdp'))
- norm2_gain_grad: float32 [768], P(('dp', 'fsdp'))
- norm2_bias_grad: float32 [768], P(('dp', 'fsdp'))
- up_weight_grad: float32 [768, 3072], P(('dp', 'fsdp'))
- up_bias_grad: float32 [3072], P(('dp', 'fsdp'))
- down_weight_grad: float32 [3072, 768], P(('dp', 'fsdp'))
- down_bias_grad: float32 [768], P(('dp', 'fsdp'))
The draws below stay inside these ranges and needn't reach their ends.
Inputs may be any that keep to these rules, and one draw needn't show every extreme that they name: `picture_ids`: within each packed row of 1024 consecutive slots the pictures are numbered 1, 2, 3 and so on in order, each covering 100 to 1024 consecutive slots; zero marks padding, which only follows a row's last picture; rows 0, 4, 8 and so on begin with a picture of exactly 1024 slots; rows 1, 5, 9 and so on hold 1024 // 100 pictures of exactly 100 slots.
All inputs are finite; a program needn't handle non-finite values.
Results may differ from the reference program's by a relative error of at most 0.0099.
Values may be sent and summed in bfloat16 or wider, within the bound.
No kernel may reach another device: no remote copies, remote signals or barrier semaphores. Data moves between devices by JAX's collectives and lax.ppermute only.
A program may use at most 256 MiB of HBM per device.

```python
import math
import jax
import jax.numpy as jnp
from jax import lax

D = 768
HEADS = 12
HD = 64
FF = 3072
ROW = 1024
PIC_MIN = 100
PIC_MAX = 1024
TOKENS = 32768


def draw_picture_ids(key, part):
    row_count = TOKENS // ROW
    slots = ROW // PIC_MIN + 1
    lengths = jax.random.randint(key, (row_count, slots), PIC_MIN, PIC_MAX + 1)
    row_index = jnp.arange(row_count)
    first_len = jnp.where(row_index % 4 == 0, PIC_MAX, lengths[:, 0])
    lengths = lengths.at[:, 0].set(first_len)
    lengths = jnp.where((row_index % 4 == 1)[:, None], PIC_MIN, lengths)
    ends = jnp.cumsum(lengths, axis=1)
    kept = ends <= ROW
    filled = jnp.max(jnp.where(kept, ends, 0), axis=1)
    places = jnp.arange(ROW)
    before = jnp.sum(((ends[:, None, :] <= places[None, :, None]) & kept[:, None, :]).astype(jnp.int32), axis=2)
    numbers = jnp.where(places[None, :] < filled[:, None], before + 1, 0)
    return numbers.reshape(TOKENS).astype(jnp.int32)


def raised(array, own_key, source, target, parts, factor):
    owner, partner = [(jnp.arange(array.shape[position]) // (array.shape[position] // parts)).reshape([-1 if axis == position else 1 for axis in range(array.ndim)]) for position in (source, target)]
    chosen = jax.random.permutation(own_key, parts)[partner]
    strong = (owner == chosen) | (owner == (partner + parts // 2) % parts)
    return jnp.where(strong, factor * array, array)


def level_of(key, dims, shards, low, largest):
    def one(position, blocks):
        draws = jax.random.uniform(jax.random.fold_in(jax.random.fold_in(key, 6), position), (blocks,), jnp.float32, low / len(shards), largest / len(shards))
        return jnp.repeat(jnp.exp(draws), dims[position] // blocks).reshape((-1,) + (1,) * (len(dims) - position - 1))

    loudness = one(*shards[0])
    for cut in shards[1:]:
        loudness = loudness * one(*cut)
    return loudness


def gaussian(key, extent, deviation, limit, shards=(), dtype=jnp.bfloat16):
    values = jax.random.normal(key, extent, jnp.float32) * deviation
    if len(shards) > 0:
        values = level_of(key, extent, shards, -0.22, 0.18) * values
    return jnp.clip(values, min=-limit, max=limit).astype(dtype)


def noise_with(key, shape, width, limit, cuts, heavy, kind=jnp.bfloat16):
    values = width * jax.random.normal(key, shape, jnp.float32)
    if cuts:
        values = values * level_of(key, shape, cuts, -0.22, 0.18)
    return jnp.clip(raised(values, jax.random.fold_in(key, 3), *heavy), -limit, limit).astype(kind)


def setup_inputs(seed: int = 0) -> dict:
    seeds = jax.random.split(jax.random.key(seed), 20)
    patches = noise_with(seeds[0], (TOKENS, D), 1.0, 6.0, ((0, 32),), (0, 1, 32, 2.75))
    picture_ids = draw_picture_ids(jax.random.fold_in(seeds[19], 71), 0)
    norm1_gain = jnp.clip(1.0 + 0.1 * jax.random.normal(seeds[2], (D,), jnp.float32), 0.5, 1.5).astype(jnp.bfloat16)
    norm1_bias = gaussian(seeds[3], (D,), 0.3, 1.75, ((0, 32),))
    qkv_weight = gaussian(seeds[4], (D, 3 * D), D ** -0.5, 0.21875, ((0, 32),))
    query_shift = gaussian(seeds[5], (D,), 0.5, 3.0, ((0, 32),))
    value_shift = gaussian(seeds[6], (D,), 0.5, 3.0, ((0, 32),))
    query_gain = jnp.clip(1.0 + 0.1 * jax.random.normal(seeds[7], (D,), jnp.float32), 0.5, 1.5).astype(jnp.bfloat16)
    query_bias = gaussian(seeds[8], (D,), 0.5, 3.0, ((0, 32),))
    key_gain = jnp.clip(1.0 + 0.1 * jax.random.normal(seeds[9], (D,), jnp.float32), 0.5, 1.5).astype(jnp.bfloat16)
    out_weight = gaussian(seeds[10], (D, D), (max(1, 2 * D // (PIC_MIN + PIC_MAX))) ** -0.5, 6.0, ((0, 32),))
    out_bias = gaussian(seeds[11], (D,), 0.3, 1.75, ((0, 32),))
    norm2_gain = jnp.clip(1.0 + 0.1 * jax.random.normal(seeds[12], (D,), jnp.float32), 0.5, 1.5).astype(jnp.bfloat16)
    norm2_bias = gaussian(seeds[13], (D,), 0.3, 1.75, ((0, 32),))
    up_weight = gaussian(seeds[14], (D, FF), D ** -0.5, 0.21875, ((0, 32),))
    up_bias = gaussian(seeds[15], (FF,), 0.5, 3.0, ((0, 32),))
    down_weight = gaussian(seeds[16], (FF, D), FF ** -0.5, 0.109375, ((0, 32),))
    down_bias = gaussian(seeds[17], (D,), 0.3, 1.75, ((0, 32),))
    out_grad = gaussian(seeds[18], (TOKENS, D), 1.0, 6.0, ((0, 32),))
    return dict(patches=patches, picture_ids=picture_ids, norm1_gain=norm1_gain, norm1_bias=norm1_bias, qkv_weight=qkv_weight, query_shift=query_shift, value_shift=value_shift, query_gain=query_gain, query_bias=query_bias, key_gain=key_gain, out_weight=out_weight, out_bias=out_bias, norm2_gain=norm2_gain, norm2_bias=norm2_bias, up_weight=up_weight, up_bias=up_bias, down_weight=down_weight, down_bias=down_bias, out_grad=out_grad)


EPSILON = 1e-06
NEG_FILL = -1000000000.0

@jax.custom_vjp
def low(v):
    return lax.optimization_barrier(v.astype(jnp.bfloat16)).astype(jnp.float32)

@jax.custom_vjp
def low_back(v):
    return v

def low_keep(v):
    return (low(v), None)

def low_pass(kept, grad):
    return (grad,)

def back_keep(v):
    return (v, None)

def back_low(kept, grad):
    return (low(grad),)
low.defvjp(low_keep, low_pass)
low_back.defvjp(back_keep, back_low)

def product(left, right):
    return jnp.dot(left, right, precision=lax.Precision.HIGHEST)

def layer_norm(values, gains, biases):
    average = lax.optimization_barrier(jnp.mean(values, axis=-1, keepdims=True))
    centred = values - average
    variance = lax.optimization_barrier(jnp.mean(centred * centred, axis=-1, keepdims=True))
    return centred * lax.rsqrt(variance + EPSILON) * gains + biases

def head_norm(values, gains, biases):
    tok_count = values.shape[0]
    shaped = values.reshape(tok_count, HEADS, HD)
    normed = layer_norm(shaped, gains.reshape(HEADS, HD), biases.reshape(HEADS, HD))
    return normed.reshape(tok_count, HEADS * HD)

def gelu_tanh(values):
    return jax.nn.gelu(values, approximate=True)

def allowed_pairs(pic_ids):
    length = pic_ids.shape[0]
    rows_at = lax.broadcasted_iota(jnp.int32, (length, length), 0)
    cols_at = lax.broadcasted_iota(jnp.int32, (length, length), 1)
    same_pic = (pic_ids[:, None] == pic_ids[None, :]) & (pic_ids[None, :] != 0)
    return same_pic | (rows_at == cols_at)

def forward(tokens, pic_ids, weights):
    gain_one, bias_one, w_qkv, q_shift, v_shift, q_gain, q_bias, k_gain, w_out, b_out, gain_two, bias_two, w_up, b_up, w_down, b_down = weights
    group_rows = tokens.shape[0]
    flat_tokens = tokens.reshape(group_rows * ROW, D)
    hidden_one = low(layer_norm(flat_tokens, gain_one, bias_one))
    shift_row = jnp.concatenate([q_shift, jnp.zeros_like(q_shift), v_shift])
    qkv_all = low_back(product(hidden_one, w_qkv) + shift_row)
    queries = low(head_norm(qkv_all[:, :D], q_gain, q_bias)).reshape(group_rows, ROW, HEADS, HD)
    keys_all = low(head_norm(qkv_all[:, D:2 * D], k_gain, jnp.zeros_like(k_gain))).reshape(group_rows, ROW, HEADS, HD)
    values_all = low(qkv_all[:, 2 * D:]).reshape(group_rows, ROW, HEADS, HD)
    scores = jnp.einsum('gqhd,gkhd->ghqk', queries, keys_all, precision=lax.Precision.HIGHEST) * HD ** (-0.5)
    scores = low_back(scores)
    allowed = jax.vmap(allowed_pairs)(pic_ids)[:, None]
    probs = low(jax.nn.softmax(jnp.where(allowed, scores, NEG_FILL), axis=-1))
    attended = jnp.einsum('ghqk,gkhd->gqhd', probs, values_all, precision=lax.Precision.HIGHEST)
    attended = low(low_back(attended.reshape(group_rows * ROW, D)))
    middle = flat_tokens + low_back(product(attended, w_out) + b_out)
    hidden_two = low(layer_norm(middle, gain_two, bias_two))
    hidden_pre = low_back(product(hidden_two, w_up) + b_up)
    hidden_act = low(gelu_tanh(hidden_pre))
    result = middle + low_back(product(hidden_act, w_down) + b_down)
    return result.reshape(group_rows, ROW, D)

def add_pair(earlier, update):
    return earlier + update

def reference(patches, picture_ids, norm1_gain, norm1_bias, qkv_weight, query_shift, value_shift, query_gain, query_bias, key_gain, out_weight, out_bias, norm2_gain, norm2_bias, up_weight, up_bias, down_weight, down_bias, out_grad):
    params = tuple((tensor.astype(jnp.float32) for tensor in (norm1_gain, norm1_bias, qkv_weight, query_shift, value_shift, query_gain, query_bias, key_gain, out_weight, out_bias, norm2_gain, norm2_bias, up_weight, up_bias, down_weight, down_bias)))
    row_total = TOKENS // ROW
    group_rows = math.gcd(row_total, max(1, 4096 // ROW))
    blocks = row_total // group_rows
    token_groups = patches.astype(jnp.float32).reshape(blocks, group_rows, ROW, D)
    id_groups = picture_ids.reshape(blocks, group_rows, ROW)
    grad_groups = out_grad.astype(jnp.float32).reshape(blocks, group_rows, ROW, D)

    def one_group(totals, pieces):
        group_tokens, group_ids, group_grads = pieces

        def apply_layer(tokens, weights):
            return forward(tokens, group_ids, weights)
        outputs, pullback = jax.vjp(apply_layer, group_tokens, params)
        token_grad, weight_grads = pullback(group_grads)
        totals = tuple((add_pair(earlier, update) for earlier, update in zip(totals, weight_grads)))
        return (totals, (outputs.astype(jnp.bfloat16), token_grad))
    zeros = tuple((jnp.zeros_like(tensor) for tensor in params))
    totals, (mixed, grads_in) = lax.scan(one_group, zeros, (token_groups, id_groups, grad_groups))
    return (mixed.reshape(TOKENS, D), grads_in.reshape(TOKENS, D), totals[0], totals[1], totals[2], totals[3], totals[4], totals[5], totals[6], totals[7], totals[8], totals[9], totals[10], totals[11], totals[12], totals[13], totals[14], totals[15])
```

```python
import functools
import math
import jax
import jax.numpy as jnp
from jax import lax
from jax.experimental import pallas as pl
from jax.experimental.pallas import tpu as pltpu
from jax.sharding import Mesh, PartitionSpec as P

HEADS = 12
HD = 64
ROW = 1024
EPSILON = 1e-06
BF = jnp.bfloat16
F32 = jnp.float32
EXP_SCALE = HD**-0.5 * math.log2(math.e)
VMEM_LIMIT = 56 << 20
LANES = 128


def nn(left, right):
    return jnp.dot(left, right, preferred_element_type=F32)


def nt(left, right):
    return lax.dot_general(left, right, (((1,), (1,)), ((), ())), preferred_element_type=F32)


def tn(left, right):
    return lax.dot_general(left, right, (((0,), (0,)), ((), ())), preferred_element_type=F32)


def call(body, grid, in_specs, out_specs, out_shape, scratch, flops, name):
    def run(*args):
        moved = sum(a.size * a.dtype.itemsize for a in args)
        moved += sum(math.prod(o.shape) * o.dtype.itemsize for o in out_shape)
        return pl.pallas_call(
            body,
            grid=grid,
            in_specs=in_specs,
            out_specs=out_specs,
            out_shape=out_shape,
            scratch_shapes=scratch,
            compiler_params=pltpu.CompilerParams(vmem_limit_bytes=VMEM_LIMIT),
            cost_estimate=pl.CostEstimate(flops=flops, bytes_accessed=moved, transcendentals=0),
            name=name,
        )(*args)

    return run


def shape(dims, kind):
    return jax.ShapeDtypeStruct(dims, kind)


def chunk_at(step, size):
    return pl.ds(pl.multiple_of(step * size, size), size)


def block_mean(size):
    rows_at = lax.broadcasted_iota(jnp.int32, (size, size), 0)
    cols_at = lax.broadcasted_iota(jnp.int32, (size, size), 1)
    return jnp.where(rows_at // HD == cols_at // HD, 1.0 / HD, 0.0).astype(BF)


def normed(values):
    average = jnp.mean(values, axis=-1, keepdims=True)
    centred = values - average
    variance = jnp.mean(centred * centred, axis=-1, keepdims=True)
    scale = lax.rsqrt(variance + EPSILON)
    return centred * scale, scale


def norm_back(hat, scale, grads):
    first = jnp.mean(grads, axis=-1, keepdims=True)
    second = jnp.mean(grads * hat, axis=-1, keepdims=True)
    return scale * (grads - first - hat * second)


def column_sum(values):
    return jnp.sum(values, axis=0, keepdims=True)


def project_body(x, gain, bias, wq, wk, wv, q_shift, v_shift, q_gain, q_bias, k_gain,
                 a1, q, k, v, q_hat, k_hat, q_scale, k_scale):
    tokens = x.shape[0]
    step = 256

    @pl.when(pl.program_id(0) == 0)
    def _():
        def first(t, carry):
            rows = chunk_at(t, step)
            hat, scale = normed(x[rows, :].astype(F32))
            a1[rows, :] = (hat * gain[...] + bias[...]).astype(BF)
            return carry

        lax.fori_loop(0, tokens // step, first, 0)

    means = block_mean(wq.shape[1])

    def one(t, carry):
        rows = chunk_at(t, step)
        source = a1[rows, :]

        def head_norm(pre, out, hat_out, scale_out, gains, biases):
            high = pre.astype(BF)
            low = (pre - high.astype(F32)).astype(BF)
            centred = pre - (nn(high, means) + nn(low, means))
            variance = nn((centred * centred).astype(BF), means)
            scale = lax.rsqrt(variance + EPSILON)
            hat = centred * scale
            shifted = hat * gains
            out[rows, :] = (shifted if biases is None else shifted + biases).astype(BF)
            hat_out[rows, :] = hat.astype(BF)
            scale_out[rows, :] = scale.astype(BF)

        head_norm(nn(source, wq[...]) + q_shift[...], q, q_hat, q_scale, q_gain[...], q_bias[...])
        head_norm(nn(source, wk[...]), k, k_hat, k_scale, k_gain[...], None)
        v[rows, :] = (nn(source, wv[...]) + v_shift[...]).astype(BF)
        return carry

    lax.fori_loop(0, tokens // step, one, 0)


def project(x, gain, bias, w_qkv, q_shift, v_shift, q_gain, q_bias, k_gain):
    tokens, width = x.shape
    cols = 256
    parts = width // cols
    whole = pl.BlockSpec((tokens, width), lambda j: (0, 0))
    wide = pl.BlockSpec((1, width), lambda j: (0, 0))
    row = pl.BlockSpec((1, cols), lambda j: (0, j))
    out = pl.BlockSpec((tokens, cols), lambda j: (0, j))
    weights = [
        pl.BlockSpec((width, cols), functools.partial(lambda j, n: (0, j + n), n=n * parts))
        for n in range(3)
    ]
    return call(
        project_body,
        (parts,),
        [whole, wide, wide] + weights + [row] * 5,
        [whole] + [out] * 7,
        [shape((tokens, width), BF)] * 8,
        [],
        6 * tokens * width * width,
        "project",
    )(x, gain, bias, w_qkv, w_qkv, w_qkv, q_shift, v_shift, q_gain, q_bias, k_gain)


def half(values, head):
    lane = lax.broadcasted_iota(jnp.int32, values.shape, 1)
    return jnp.where((lane < HD) if head == 0 else (lane >= HD), values, jnp.zeros_like(values))


def three_parts(values, lane):
    high = values.astype(BF).astype(F32)
    rest = values - high
    middle = rest.astype(BF).astype(F32)
    low = rest - middle
    return jnp.where(
        lane == 12, high, jnp.where(lane == 13, middle, jnp.where(lane == 14, low, 0.0))
    )


def picture_lanes(pic_ids):
    lane = lax.broadcasted_iota(jnp.int32, (pic_ids.shape[0], LANES), 1)
    same = (pic_ids[:, None] == lane + 1) & (lane < 10)
    for_q = jnp.where(same | (lane == 10), 32.0, 0.0).astype(BF)
    ones = jnp.where((lane >= 12) & (lane < 15), 1.0, 0.0)
    for_k = jnp.where(same, 64.0, jnp.where(lane == 10, -64.0, ones)).astype(BF)
    padding = jnp.broadcast_to((pic_ids == 0)[:, None], lane.shape).astype(F32)
    return for_q, for_k, padding


def attend_body(step, q, k, v, extra_q, extra_k, padding, att, extra_back):
    values = jnp.concatenate([v[...], jnp.ones((ROW, LANES), BF)], axis=1)
    keys = [jnp.concatenate([half(k[...], h), extra_k[...]], axis=1) for h in (0, 1)]

    def one(t, carry):
        rows = chunk_at(t, step)
        queries = jnp.concatenate([q[rows, :], extra_q[rows, :]], axis=1)
        pad = padding[rows, :]
        lane = lax.broadcasted_iota(jnp.int32, (step, LANES), 1)
        results = []
        for h in (0, 1):
            powers = jnp.exp2(nt(queries, keys[h]) * EXP_SCALE).astype(BF)
            out = nn(powers, values)
            total = out[:, LANES:] + pad
            results.append((out[:, :LANES] + pad * v[rows, :].astype(F32)) / total)
            row_term = three_parts(jnp.log(total) * -(HD**0.5), lane)
            extra_back[h, rows, :] = (extra_q[rows, :].astype(F32) + row_term).astype(BF)
        att[rows, :] = jnp.where(lane < HD, results[0], results[1]).astype(BF)
        return carry

    lax.fori_loop(0, ROW // step, one, 0)


def attend(q, k, v, extra_q, extra_k, padding):
    tokens, width = q.shape
    pairs = width // LANES
    block = pl.BlockSpec((ROW, LANES), lambda r, p: (r, p))
    fixed = pl.BlockSpec((ROW, LANES), lambda r, p: (r, 0))
    return call(
        functools.partial(attend_body, 512),
        (tokens // ROW, pairs),
        [block] * 3 + [fixed] * 3,
        [block, pl.BlockSpec((2, ROW, LANES), lambda r, p: (p, r, 0))],
        [shape((tokens, width), BF), shape((2 * pairs, tokens, LANES), BF)],
        [],
        16 * tokens * ROW * width,
        "attend",
    )(q, k, v, extra_q, extra_k, padding)


def attend_back_body(step, q, k, v, go, att, extra_q, extra_k, padding, q_hat, k_hat, q_scale,
                     k_scale, q_gain, k_gain, gq, gk, gv, sums, total):
    lane = lax.broadcasted_iota(jnp.int32, (ROW, LANES), 1)
    rows_at = lax.broadcasted_iota(jnp.int32, (LANES, LANES), 0)
    cols_at = lax.broadcasted_iota(jnp.int32, (LANES, LANES), 1)
    terms = go[...].astype(F32) * att[...].astype(F32)
    high = terms.astype(BF)
    low = (terms - high.astype(F32)).astype(BF)
    three = (lane >= 12) & (lane < 15)
    v_extra = jnp.where(three, 1.0, 0.0).astype(BF)[:step]
    queries, grads, go_half, q_half = [], [], [], []
    for h in (0, 1):
        mine = (rows_at < HD) if h == 0 else (rows_at >= HD)
        pick = jnp.where(mine & (cols_at >= 12) & (cols_at < 15), 1.0, 0.0).astype(BF)
        delta = nn(high, pick) + nn(low, pick)
        grads.append(jnp.concatenate([go[...], three_parts(-delta, lane).astype(BF)], axis=1))
        queries.append(jnp.concatenate([q[...], extra_q[h]], axis=1))
        go_half.append(half(go[...], h))
        q_half.append(half(q[...], h))
    total[...] = jnp.zeros_like(total)
    means = block_mean(LANES)

    def head_norm_back(incoming, hat, scale, gains):
        inner = incoming * gains
        first = nn(inner.astype(BF), means)
        second = nn((inner * hat).astype(BF), means)
        return scale * (inner - first - hat * second)

    def one(t, carry):
        k_sum, v_sum = carry
        rows = chunk_at(t, step)
        grad_v, grad_k = 0.0, 0.0
        for h in (0, 1):
            key = half(k[rows, :], h)
            scores = nt(jnp.concatenate([key, extra_k[rows, :]], axis=1), queries[h])
            pulled = nt(jnp.concatenate([half(v[rows, :], h), v_extra], axis=1), grads[h])
            probs = jnp.exp2(scores * EXP_SCALE)
            grad_scores = (probs * pulled).astype(BF)
            grad_v += nn(probs.astype(BF), go_half[h])
            grad_k += nn(grad_scores, q_half[h])
            total[...] += tn(key, grad_scores)
        out_v = (grad_v + padding[rows, :] * go[rows, :].astype(F32)).astype(BF)
        gv[rows, :] = out_v
        grad_k = grad_k * HD**-0.5
        hat = k_hat[rows, :].astype(F32)
        back = head_norm_back(grad_k, hat, k_scale[rows, :].astype(F32), k_gain[...])
        gk[rows, :] = back.astype(BF)
        return k_sum + column_sum(grad_k * hat), v_sum + column_sum(out_v.astype(F32))

    zero = jnp.zeros((1, LANES), F32)
    k_sum, v_sum = lax.fori_loop(0, ROW // step, one, (zero, zero))
    gain_sum, bias_sum, shift_sum = zero, zero, zero
    for t in range(ROW // 256):
        rows = slice(t * 256, t * 256 + 256)
        grad_q = total[:, rows].T * HD**-0.5
        hat = q_hat[rows, :].astype(F32)
        back = head_norm_back(grad_q, hat, q_scale[rows, :].astype(F32), q_gain[...]).astype(BF)
        gq[rows, :] = back
        gain_sum += column_sum(grad_q * hat)
        bias_sum += column_sum(grad_q)
        shift_sum += column_sum(back.astype(F32))
    sums[...] = jnp.concatenate(
        [shift_sum, v_sum, gain_sum, bias_sum, k_sum, zero, zero, zero], axis=0
    )


def attend_back(q, k, v, go, att, extra_q, extra_k, padding, q_hat, k_hat, q_scale, k_scale,
                q_gain, k_gain):
    tokens, width = q.shape
    packed = tokens // ROW
    block = pl.BlockSpec((ROW, LANES), lambda r, p: (r, p))
    fixed = pl.BlockSpec((ROW, LANES), lambda r, p: (r, 0))
    row = pl.BlockSpec((1, LANES), lambda r, p: (0, p))
    return call(
        functools.partial(attend_back_body, 512),
        (packed, width // LANES),
        [block] * 5
        + [pl.BlockSpec((2, ROW, LANES), lambda r, p: (p, r, 0)), fixed, fixed]
        + [block] * 4
        + [row] * 2,
        [block] * 3 + [pl.BlockSpec((8, LANES), lambda r, p: (r, p))],
        [shape((tokens, width), BF)] * 3 + [shape((8 * packed, width), F32)],
        [pltpu.VMEM((LANES, ROW), F32)],
        40 * tokens * ROW * width,
        "attend_back",
    )(q, k, v, go, att, extra_q, extra_k, padding, q_hat, k_hat, q_scale, k_scale, q_gain, k_gain)


def mix_body(att, w_out, b_out, x, gain, bias, x2, a2):
    middle = x[...].astype(F32) + (nn(att[...], w_out[...]) + b_out[...])
    x2[...] = middle
    a2[...] = (normed(middle)[0] * gain[...] + bias[...]).astype(BF)


def mix(att, w_out, b_out, x, gain, bias):
    tokens, width = x.shape
    step = 256
    block = pl.BlockSpec((step, width), lambda t: (t, 0))
    row = pl.BlockSpec((1, width), lambda t: (0, 0))
    return call(
        mix_body,
        (tokens // step,),
        [block, pl.BlockSpec((width, width), lambda t: (0, 0)), row, block, row, row],
        [block, block],
        [shape((tokens, width), F32), shape((tokens, width), BF)],
        [],
        2 * tokens * width * width,
        "mix",
    )(att, w_out, b_out, x, gain, bias)


SLOPE = math.sqrt(2.0 / math.pi)
CUBE = 0.044715


def gelu_pair(values):
    square = values * values
    bent = jnp.tanh(SLOPE * (values + CUBE * (square * values)))
    share = 0.5 * (1.0 + bent)
    slope = share + (0.5 * SLOPE) * values * (1.0 - bent * bent) * (1.0 + (3 * CUBE) * square)
    return values * share, slope


def hidden_body(step, a2, og, up, down, b_up, y, ga, w_down, w_up, sum_up, turned, act, grad):
    tokens = a2.shape[0]

    @pl.when(pl.program_id(0) == 0)
    def _():
        turned[...] = a2[...].T
        y[...] = jnp.zeros_like(y)
        ga[...] = jnp.zeros_like(ga)

    def one(t, carry):
        rows = chunk_at(t, step)
        value, slope = gelu_pair(nn(a2[rows, :], up[...]) + b_up[...])
        value = value.astype(BF)
        act[rows, :] = value
        y[rows, :] += nn(value, down[...])
        pulled = (nt(og[rows, :], down[...]) * slope).astype(BF)
        grad[rows, :] = pulled
        ga[rows, :] += nt(pulled, up[...])
        return carry + column_sum(pulled.astype(F32))

    sum_up[...] = lax.fori_loop(0, tokens // step, one, jnp.zeros(sum_up.shape, F32))
    for part in range(0, act.shape[1], 256):
        cols = slice(part, part + 256)
        w_down[cols, :] = tn(act[:, cols], og[...]).astype(BF)
    for part in range(0, turned.shape[0], 256):
        rows = slice(part, part + 256)
        w_up[rows, :] = nn(turned[rows, :], grad[...]).astype(BF)


def hidden(a2, og, up, down, b_up):
    tokens, width = a2.shape
    units = up.shape[1]
    block = 512
    fixed = pl.BlockSpec((tokens, width), lambda j: (0, 0))
    cols = pl.BlockSpec((width, block), lambda j: (0, j))
    rows = pl.BlockSpec((block, width), lambda j: (j, 0))
    row = pl.BlockSpec((1, block), lambda j: (0, j))
    return call(
        functools.partial(hidden_body, 256),
        (units // block,),
        [fixed, fixed, cols, rows, row],
        [fixed, fixed, rows, cols, row],
        [
            shape((tokens, width), F32),
            shape((tokens, width), F32),
            shape((units, width), BF),
            shape((width, units), BF),
            shape((1, units), F32),
        ],
        [
            pltpu.VMEM((width, tokens), BF),
            pltpu.VMEM((tokens, block), BF),
            pltpu.VMEM((tokens, block), BF),
        ],
        12 * tokens * width * units,
        "hidden",
    )(a2, og, up, down, b_up)


def close_body(y, ga, x2, og, b_down, gain, mixed, gx2, gy, sums):
    middle = x2[...]
    outer = og[...].astype(F32)
    mixed[...] = (middle + (y[...] + b_down[...])).astype(BF)
    hat, scale = normed(middle)
    incoming = ga[...]
    total = outer + norm_back(hat, scale, incoming * gain[...])
    gx2[...] = total
    rounded = total.astype(BF)
    gy[...] = rounded
    new = jnp.concatenate(
        [
            column_sum(incoming * hat),
            column_sum(incoming),
            column_sum(rounded.astype(F32)),
            column_sum(outer),
            jnp.zeros((4, outer.shape[1]), F32),
        ],
        axis=0,
    )

    @pl.when(pl.program_id(0) == 0)
    def _():
        sums[...] = new

    @pl.when(pl.program_id(0) > 0)
    def _():
        sums[...] += new


def close(y, ga, x2, og, b_down, gain):
    tokens, width = y.shape
    step = 256
    block = pl.BlockSpec((step, width), lambda t: (t, 0))
    row = pl.BlockSpec((1, width), lambda t: (0, 0))
    return call(
        close_body,
        (tokens // step,),
        [block] * 4 + [row] * 2,
        [block] * 3 + [pl.BlockSpec((8, width), lambda t: (0, 0))],
        [
            shape((tokens, width), BF),
            shape((tokens, width), F32),
            shape((tokens, width), BF),
            shape((8, width), F32),
        ],
        [],
        40 * tokens * width,
        "close",
    )(y, ga, x2, og, b_down, gain)


def mix_back_body(gy, att, w_out, go, w_grad):
    go[...] = nt(gy[...], w_out[...]).astype(BF)
    w_grad[...] = tn(att[...], gy[...]).astype(BF)


def mix_back(gy, att, w_out):
    tokens, width = gy.shape
    cols = 256
    narrow = pl.BlockSpec((tokens, cols), lambda j: (0, j))
    rows = pl.BlockSpec((cols, width), lambda j: (j, 0))
    return call(
        mix_back_body,
        (width // cols,),
        [pl.BlockSpec((tokens, width), lambda j: (0, 0)), narrow, rows],
        [narrow, rows],
        [shape((tokens, width), BF), shape((width, width), BF)],
        [],
        4 * tokens * width * width,
        "mix_back",
    )(gy, att, w_out)


def project_grad_body(a1, gq, gk, gv, out_q, out_k, out_v, turned):
    @pl.when(pl.program_id(0) == 0)
    def _():
        turned[...] = a1[...].T

    for source, out in ((gq, out_q), (gk, out_k), (gv, out_v)):
        out[...] = nn(turned[...], source[...]).astype(BF)


def project_grad(a1, gq, gk, gv):
    tokens, width = a1.shape
    cols = 256
    narrow = pl.BlockSpec((tokens, cols), lambda j: (0, j))
    out = pl.BlockSpec((width, cols), lambda j: (0, j))
    return call(
        project_grad_body,
        (width // cols,),
        [pl.BlockSpec((tokens, width), lambda j: (0, 0))] + [narrow] * 3,
        [out] * 3,
        [shape((width, width), BF)] * 3,
        [pltpu.VMEM((width, tokens), BF)],
        6 * tokens * width * width,
        "project_grad",
    )(a1, gq, gk, gv)


def project_back_body(gq, gk, gv, w_qkv, x, gx2, gain, out, sums):
    width = x.shape[1]
    incoming = nt(gq[...], w_qkv[:, :width])
    incoming += nt(gk[...], w_qkv[:, width : 2 * width])
    incoming += nt(gv[...], w_qkv[:, 2 * width :])
    hat, scale = normed(x[...].astype(F32))
    out[...] = gx2[...] + norm_back(hat, scale, incoming * gain[...])
    new = jnp.concatenate(
        [column_sum(incoming * hat), column_sum(incoming), jnp.zeros((6, width), F32)], axis=0
    )

    @pl.when(pl.program_id(0) == 0)
    def _():
        sums[...] = new

    @pl.when(pl.program_id(0) > 0)
    def _():
        sums[...] += new


def project_back(gq, gk, gv, w_qkv, x, gx2, gain):
    tokens, width = x.shape
    step = 256
    block = pl.BlockSpec((step, width), lambda t: (t, 0))
    return call(
        project_back_body,
        (tokens // step,),
        [block] * 3
        + [pl.BlockSpec((width, 3 * width), lambda t: (0, 0)), block, block]
        + [pl.BlockSpec((1, width), lambda t: (0, 0))],
        [block, pl.BlockSpec((8, width), lambda t: (0, 0))],
        [shape((tokens, width), F32), shape((8, width), F32)],
        [],
        6 * tokens * width * width,
        "project_back",
    )(gq, gk, gv, w_qkv, x, gx2, gain)


AXES = ("dp", "fsdp")


def gather(shard):
    return lax.all_gather(shard, AXES, axis=0, tiled=True)


def spread(grad):
    return lax.psum_scatter(grad, AXES, scatter_dimension=0, tiled=True)


def pack_columns(vectors, rows):
    columns = [v.reshape(rows, -1) for v in vectors]
    joined = jnp.concatenate(columns, axis=1)
    return jnp.pad(joined, ((0, 0), (0, LANES - joined.shape[1])))


def on_device(patches, picture_ids, norm1_gain, norm1_bias, qkv_weight, query_shift, value_shift,
              query_gain, query_bias, key_gain, out_weight, out_bias, norm2_gain, norm2_bias,
              up_weight, up_bias, down_weight, down_bias, out_grad):
    width = patches.shape[1]
    rows = qkv_weight.shape[0]
    small = pack_columns(
        [norm1_gain, norm1_bias, query_shift, value_shift, query_gain, query_bias, key_gain,
         out_bias, norm2_gain, norm2_bias, down_bias, up_bias],
        rows,
    )
    first = gather(jnp.concatenate([qkv_weight, small], axis=1))
    w_qkv = first[:, : 3 * width]
    vectors = first[:, 3 * width :]
    b_up = vectors[:, 11:15].reshape(1, -1).astype(F32)
    vectors = vectors.T.astype(F32)
    (gain_one, bias_one, q_shift, v_shift, q_gain, q_bias, k_gain, b_out, gain_two, bias_two,
     b_down) = [vectors[n : n + 1] for n in range(11)]
    w_out = gather(out_weight)
    w_up = gather(up_weight)
    w_down = gather(down_weight)

    extra_q, extra_k, padding = picture_lanes(picture_ids)
    a1, q, k, v, q_hat, k_hat, q_scale, k_scale = project(
        patches, gain_one, bias_one, w_qkv, q_shift, v_shift, q_gain, q_bias, k_gain
    )
    att, extra_back = attend(q, k, v, extra_q, extra_k, padding)
    x2, a2 = mix(att, w_out, b_out, patches, gain_two, bias_two)
    y, ga, down_grad, up_grad, up_sum = hidden(a2, out_grad, w_up, w_down, b_up)
    down_out = spread(down_grad)
    up_out = spread(up_grad)
    mixed, gx2, gy, sums_two = close(y, ga, x2, out_grad, b_down, gain_two)
    go, out_w_grad = mix_back(gy, att, w_out)
    out_out = spread(out_w_grad)
    gq, gk, gv, sums_att = attend_back(
        q, k, v, go, att, extra_back, extra_k, padding, q_hat, k_hat, q_scale, k_scale, q_gain,
        k_gain,
    )
    sums_att = sums_att.reshape(-1, 8, width).sum(axis=0)
    qkv_grads = project_grad(a1, gq, gk, gv)
    patches_grad, sums_one = project_back(gq, gk, gv, w_qkv, patches, gx2, gain_one)
    sums = jnp.concatenate([sums_one[:2], sums_att[:5], sums_two[:4]], axis=0)
    columns = jnp.concatenate([sums.T, up_sum.reshape(width, -1)], axis=1)
    columns = jnp.pad(columns, ((0, 0), (0, LANES - columns.shape[1]))).astype(BF)
    last = spread(jnp.concatenate([*qkv_grads, columns], axis=1)).astype(F32)
    qkv_out = last[:, : 3 * width]
    final = last[:, 3 * width :]
    (gain_one_out, bias_one_out, q_shift_out, v_shift_out, q_gain_out, q_bias_out, k_gain_out,
     gain_two_out, bias_two_out, out_bias_out, down_bias_out) = [final[:, n] for n in range(11)]
    return (
        mixed, patches_grad, gain_one_out, bias_one_out, qkv_out, q_shift_out, v_shift_out,
        q_gain_out, q_bias_out, k_gain_out, out_out.astype(F32), out_bias_out, gain_two_out,
        bias_two_out, up_out.astype(F32), final[:, 11:15].reshape(-1), down_out.astype(F32),
        down_bias_out,
    )


def solution(mesh):
    flat = P(AXES)
    wide = P(AXES, None)
    in_specs = (wide, flat, flat, flat, wide, flat, flat, flat, flat, flat, wide, flat, flat, flat,
                wide, flat, wide, flat, wide)
    out_specs = (wide, wide, flat, flat, wide, flat, flat, flat, flat, flat, wide, flat, flat, flat,
                 wide, flat, wide, flat)
    return jax.shard_map(
        on_device, mesh=mesh, in_specs=in_specs, out_specs=out_specs, check_vma=False
    )
```

```python
import functools
import math
import jax
import jax.numpy as jnp
from jax import lax
from jax.experimental import pallas as pl
from jax.experimental.pallas import tpu as pltpu
from jax.sharding import Mesh, PartitionSpec as P

HEADS = 12
HD = 64
ROW = 1024
EPSILON = 1e-06
BF = jnp.bfloat16
F32 = jnp.float32
EXP_SCALE = HD**-0.5 * math.log2(math.e)
VMEM_LIMIT = 56 << 20
LANES = 128


def nn(left, right):
    return jnp.dot(left, right, preferred_element_type=F32)


def nt(left, right):
    return lax.dot_general(left, right, (((1,), (1,)), ((), ())), preferred_element_type=F32)


def tn(left, right):
    return lax.dot_general(left, right, (((0,), (0,)), ((), ())), preferred_element_type=F32)


def call(body, grid, in_specs, out_specs, out_shape, scratch, flops, name):
    def run(*args):
        moved = sum(a.size * a.dtype.itemsize for a in args)
        moved += sum(math.prod(o.shape) * o.dtype.itemsize for o in out_shape)
        return pl.pallas_call(
            body,
            grid=grid,
            in_specs=in_specs,
            out_specs=out_specs,
            out_shape=out_shape,
            scratch_shapes=scratch,
            compiler_params=pltpu.CompilerParams(vmem_limit_bytes=VMEM_LIMIT),
            cost_estimate=pl.CostEstimate(flops=flops, bytes_accessed=moved, transcendentals=0),
            name=name,
        )(*args)

    return run


def shape(dims, kind):
    return jax.ShapeDtypeStruct(dims, kind)


def chunk_at(step, size):
    return pl.ds(pl.multiple_of(step * size, size), size)


def block_mean(size):
    rows_at = lax.broadcasted_iota(jnp.int32, (size, size), 0)
    cols_at = lax.broadcasted_iota(jnp.int32, (size, size), 1)
    return jnp.where(rows_at // HD == cols_at // HD, 1.0 / HD, 0.0).astype(BF)


def normed(values):
    average = jnp.mean(values, axis=-1, keepdims=True)
    centred = values - average
    variance = jnp.mean(centred * centred, axis=-1, keepdims=True)
    scale = lax.rsqrt(variance + EPSILON)
    return centred * scale, scale


def norm_back(hat, scale, grads):
    first = jnp.mean(grads, axis=-1, keepdims=True)
    second = jnp.mean(grads * hat, axis=-1, keepdims=True)
    return scale * (grads - first - hat * second)


def column_sum(values):
    return jnp.sum(values, axis=0, keepdims=True)


def project_body(x, gain, bias, weights, q_shift, v_shift, q_gain, q_bias, k_gain,
                 a1, q, k, v, q_hat, k_hat, q_scale, k_scale):
    tokens = x.shape[0]
    step = 256

    @pl.when(pl.program_id(0) == 0)
    def _():
        def first(t, carry):
            rows = chunk_at(t, step)
            hat, scale = normed(x[rows, :].astype(F32))
            a1[rows, :] = (hat * gain[...] + bias[...]).astype(BF)
            return carry

        lax.fori_loop(0, tokens // step, first, 0)

    cols = weights.shape[1] // 3
    means = block_mean(cols)

    def one(t, carry):
        rows = chunk_at(t, step)
        source = a1[rows, :]

        def head_norm(pre, out, hat_out, scale_out, gains, biases):
            high = pre.astype(BF)
            low = (pre - high.astype(F32)).astype(BF)
            centred = pre - (nn(high, means) + nn(low, means))
            variance = nn((centred * centred).astype(BF), means)
            scale = lax.rsqrt(variance + EPSILON)
            hat = centred * scale
            shifted = hat * gains
            out[rows, :] = (shifted if biases is None else shifted + biases).astype(BF)
            hat_out[rows, :] = hat.astype(BF)
            scale_out[rows, :] = scale.astype(BF)

        head_norm(nn(source, weights[:, :cols]) + q_shift[...], q, q_hat, q_scale, q_gain[...], q_bias[...])
        head_norm(nn(source, weights[:, cols : 2 * cols]), k, k_hat, k_scale, k_gain[...], None)
        v[rows, :] = (nn(source, weights[:, 2 * cols :]) + v_shift[...]).astype(BF)
        return carry

    lax.fori_loop(0, tokens // step, one, 0)


def project(x, gain, bias, weights, q_shift, v_shift, q_gain, q_bias, k_gain):
    tokens, width = x.shape
    cols = 256
    parts = width // cols
    whole = pl.BlockSpec((tokens, width), lambda j: (0, 0))
    wide = pl.BlockSpec((1, width), lambda j: (0, 0))
    row = pl.BlockSpec((1, cols), lambda j: (0, j))
    out = pl.BlockSpec((tokens, cols), lambda j: (0, j))
    return call(
        project_body,
        (parts,),
        [whole, wide, wide, pl.BlockSpec((width, 3 * cols), lambda j: (0, j))] + [row] * 5,
        [whole] + [out] * 7,
        [shape((tokens, width), BF)] * 8,
        [],
        6 * tokens * width * width,
        "project",
    )(x, gain, bias, weights, q_shift, v_shift, q_gain, q_bias, k_gain)


def half(values, head):
    lane = lax.broadcasted_iota(jnp.int32, values.shape, 1)
    return jnp.where((lane < HD) if head == 0 else (lane >= HD), values, jnp.zeros_like(values))


def three_parts(values, lane):
    high = values.astype(BF).astype(F32)
    rest = values - high
    middle = rest.astype(BF).astype(F32)
    low = rest - middle
    return jnp.where(
        lane == 12, high, jnp.where(lane == 13, middle, jnp.where(lane == 14, low, 0.0))
    )


def picture_lanes(pic_ids):
    lane = lax.broadcasted_iota(jnp.int32, (pic_ids.shape[0], LANES), 1)
    same = (pic_ids[:, None] == lane + 1) & (lane < 10)
    for_q = jnp.where(same | (lane == 10), 32.0, 0.0).astype(BF)
    ones = jnp.where((lane >= 12) & (lane < 15), 1.0, 0.0)
    for_k = jnp.where(same, 64.0, jnp.where(lane == 10, -64.0, ones)).astype(BF)
    padding = jnp.broadcast_to((pic_ids == 0)[:, None], lane.shape).astype(F32)
    return for_q, for_k, padding


def attend_body(step, q, k, v, extra_q, extra_k, padding, att, extra_back):
    values = jnp.concatenate([v[...], jnp.ones((ROW, LANES), BF)], axis=1)
    keys = [jnp.concatenate([half(k[...], h), extra_k[...]], axis=1) for h in (0, 1)]

    def one(t, carry):
        rows = chunk_at(t, step)
        queries = jnp.concatenate([q[rows, :], extra_q[rows, :]], axis=1)
        pad = padding[rows, :]
        lane = lax.broadcasted_iota(jnp.int32, (step, LANES), 1)
        results = []
        for h in (0, 1):
            powers = jnp.exp2(nt(queries, keys[h]) * EXP_SCALE).astype(BF)
            out = nn(powers, values)
            total = out[:, LANES:] + pad
            results.append((out[:, :LANES] + pad * v[rows, :].astype(F32)) / total)
            row_term = three_parts(jnp.log(total) * -(HD**0.5), lane)
            extra_back[h, rows, :] = (extra_q[rows, :].astype(F32) + row_term).astype(BF)
        att[rows, :] = jnp.where(lane < HD, results[0], results[1]).astype(BF)
        return carry

    lax.fori_loop(0, ROW // step, one, 0)


def attend(q, k, v, extra_q, extra_k, padding):
    tokens, width = q.shape
    pairs = width // LANES
    block = pl.BlockSpec((ROW, LANES), lambda r, p: (r, p))
    fixed = pl.BlockSpec((ROW, LANES), lambda r, p: (r, 0))
    return call(
        functools.partial(attend_body, 512),
        (tokens // ROW, pairs),
        [block] * 3 + [fixed] * 3,
        [block, pl.BlockSpec((2, ROW, LANES), lambda r, p: (p, r, 0))],
        [shape((tokens, width), BF), shape((2 * pairs, tokens, LANES), BF)],
        [],
        16 * tokens * ROW * width,
        "attend",
    )(q, k, v, extra_q, extra_k, padding)


def attend_back_body(step, q, k, v, go, att, extra_q, extra_k, padding, q_hat, k_hat, q_scale,
                     k_scale, q_gain, k_gain, packed, sums, total):
    offset = lax.rem(pl.program_id(1), 2) * LANES
    q_at, k_at, v_at = [pl.ds(pl.multiple_of(offset + n, LANES), LANES) for n in (0, 256, 512)]
    lane = lax.broadcasted_iota(jnp.int32, (ROW, LANES), 1)
    rows_at = lax.broadcasted_iota(jnp.int32, (LANES, LANES), 0)
    cols_at = lax.broadcasted_iota(jnp.int32, (LANES, LANES), 1)
    terms = go[...].astype(F32) * att[...].astype(F32)
    high = terms.astype(BF)
    low = (terms - high.astype(F32)).astype(BF)
    three = (lane >= 12) & (lane < 15)
    v_extra = jnp.where(three, 1.0, 0.0).astype(BF)[:step]
    queries, grads, go_half, q_half = [], [], [], []
    for h in (0, 1):
        mine = (rows_at < HD) if h == 0 else (rows_at >= HD)
        pick = jnp.where(mine & (cols_at >= 12) & (cols_at < 15), 1.0, 0.0).astype(BF)
        delta = nn(high, pick) + nn(low, pick)
        grads.append(jnp.concatenate([go[...], three_parts(-delta, lane).astype(BF)], axis=1))
        queries.append(jnp.concatenate([q[...], extra_q[h]], axis=1))
        go_half.append(half(go[...], h))
        q_half.append(half(q[...], h))
    total[...] = jnp.zeros_like(total)
    means = block_mean(LANES)

    def head_norm_back(incoming, hat, scale, gains):
        inner = incoming * gains
        first = nn(inner.astype(BF), means)
        second = nn((inner * hat).astype(BF), means)
        return scale * (inner - first - hat * second)

    def one(t, carry):
        k_sum, v_sum = carry
        rows = chunk_at(t, step)
        grad_v, grad_k = 0.0, 0.0
        for h in (0, 1):
            key = half(k[rows, :], h)
            scores = nt(jnp.concatenate([key, extra_k[rows, :]], axis=1), queries[h])
            pulled = nt(jnp.concatenate([half(v[rows, :], h), v_extra], axis=1), grads[h])
            probs = jnp.exp2(scores * EXP_SCALE)
            grad_scores = (probs * pulled).astype(BF)
            grad_v += nn(probs.astype(BF), go_half[h])
            grad_k += nn(grad_scores, q_half[h])
            total[...] += tn(key, grad_scores)
        out_v = (grad_v + padding[rows, :] * go[rows, :].astype(F32)).astype(BF)
        packed[rows, v_at] = out_v
        grad_k = grad_k * HD**-0.5
        hat = k_hat[rows, :].astype(F32)
        back = head_norm_back(grad_k, hat, k_scale[rows, :].astype(F32), k_gain[...])
        packed[rows, k_at] = back.astype(BF)
        return k_sum + column_sum(grad_k * hat), v_sum + column_sum(out_v.astype(F32))

    zero = jnp.zeros((1, LANES), F32)
    k_sum, v_sum = lax.fori_loop(0, ROW // step, one, (zero, zero))
    gain_sum, bias_sum, shift_sum = zero, zero, zero
    for t in range(ROW // 256):
        rows = slice(t * 256, t * 256 + 256)
        grad_q = total[:, rows].T * HD**-0.5
        hat = q_hat[rows, :].astype(F32)
        back = head_norm_back(grad_q, hat, q_scale[rows, :].astype(F32), q_gain[...]).astype(BF)
        packed[rows, q_at] = back
        gain_sum += column_sum(grad_q * hat)
        bias_sum += column_sum(grad_q)
        shift_sum += column_sum(back.astype(F32))
    sums[...] = jnp.concatenate(
        [shift_sum, v_sum, gain_sum, bias_sum, k_sum, zero, zero, zero], axis=0
    )


def attend_back(q, k, v, go, att, extra_q, extra_k, padding, q_hat, k_hat, q_scale, k_scale,
                q_gain, k_gain):
    tokens, width = q.shape
    count = tokens // ROW
    block = pl.BlockSpec((ROW, LANES), lambda r, p: (r, p))
    fixed = pl.BlockSpec((ROW, LANES), lambda r, p: (r, 0))
    row = pl.BlockSpec((1, LANES), lambda r, p: (0, p))
    return call(
        functools.partial(attend_back_body, 512),
        (count, width // LANES),
        [block] * 5
        + [pl.BlockSpec((2, ROW, LANES), lambda r, p: (p, r, 0)), fixed, fixed]
        + [block] * 4
        + [row] * 2,
        [
            pl.BlockSpec((ROW, 6 * LANES), lambda r, p: (r, p // 2)),
            pl.BlockSpec((8, LANES), lambda r, p: (r, p)),
        ],
        [shape((tokens, 3 * width), BF), shape((8 * count, width), F32)],
        [pltpu.VMEM((LANES, ROW), F32)],
        40 * tokens * ROW * width,
        "attend_back",
    )(q, k, v, go, att, extra_q, extra_k, padding, q_hat, k_hat, q_scale, k_scale, q_gain, k_gain)


def mix_body(att, w_out, b_out, x, gain, bias, x2, a2):
    middle = x[...].astype(F32) + (nn(att[...], w_out[...]) + b_out[...])
    x2[...] = middle
    a2[...] = (normed(middle)[0] * gain[...] + bias[...]).astype(BF)


def mix(att, weights, b_out, x, gain, bias):
    tokens, width = x.shape
    last = weights.shape[1] // width - 1
    step = 256
    block = pl.BlockSpec((step, width), lambda t: (t, 0))
    row = pl.BlockSpec((1, width), lambda t: (0, 0))
    return call(
        mix_body,
        (tokens // step,),
        [block, pl.BlockSpec((width, width), lambda t: (0, last)), row, block, row, row],
        [block, block],
        [shape((tokens, width), F32), shape((tokens, width), BF)],
        [],
        2 * tokens * width * width,
        "mix",
    )(att, weights, b_out, x, gain, bias)


SLOPE = math.sqrt(2.0 / math.pi)
CUBE = 0.044715


def gelu_pair(values):
    square = values * values
    bent = jnp.tanh(SLOPE * (values + CUBE * (square * values)))
    share = 0.5 * (1.0 + bent)
    slope = share + (0.5 * SLOPE) * values * (1.0 - bent * bent) * (1.0 + (3 * CUBE) * square)
    return values * share, slope


def fold_pairs(owners, rows, folds, width):
    for o in range(owners):
        for w in range(folds):
            at = (o * folds + w) * rows
            yield slice(at, at + rows), slice(o * rows, o * rows + rows), slice(w * width, w * width + width)


def hidden_body(rows_each, step, a2, og, x2, down_in, up, b_up, b_down, gain, w_down, w_up, sum_up,
                mixed, gx2, gy, sums, y, ga, turned, act, grad, down, flat):
    tokens, width = a2.shape
    folds = down_in.shape[1] // width
    owners = down_in.shape[0] // rows_each

    @pl.when(pl.program_id(0) == 0)
    def _():
        turned[...] = a2[...].T
        y[...] = jnp.zeros_like(y)
        ga[...] = jnp.zeros_like(ga)

    for natural, rows, cols in fold_pairs(owners, rows_each, folds, width):
        down[natural, :] = down_in[rows, cols]

    def one(t, carry):
        rows = chunk_at(t, step)
        value, slope = gelu_pair(nn(a2[rows, :], up[...]) + b_up[...])
        value = value.astype(BF)
        act[rows, :] = value
        y[rows, :] += nn(value, down[...])
        pulled = (nt(og[rows, :], down[...]) * slope).astype(BF)
        grad[rows, :] = pulled
        ga[rows, :] += nt(pulled, up[...])
        return carry + column_sum(pulled.astype(F32))

    sum_up[...] = lax.fori_loop(0, tokens // step, one, jnp.zeros(sum_up.shape, F32))
    for part in range(0, act.shape[1], 256):
        cols = slice(part, part + 256)
        flat[cols, :] = tn(act[:, cols], og[...]).astype(BF)
    for natural, rows, cols in fold_pairs(owners, rows_each, folds, width):
        w_down[rows, cols] = flat[natural, :]
    for part in range(0, width, 256):
        rows = slice(part, part + 256)
        w_up[rows, :] = nn(turned[rows, :], grad[...]).astype(BF)

    @pl.when(pl.program_id(0) == pl.num_programs(0) - 1)
    def _():
        def end(t, carry):
            rows = chunk_at(t, step)
            middle = x2[rows, :]
            outer = og[rows, :].astype(F32)
            mixed[rows, :] = (middle + (y[rows, :] + b_down[...])).astype(BF)
            hat, scale = normed(middle)
            incoming = ga[rows, :]
            total = outer + norm_back(hat, scale, incoming * gain[...])
            gx2[rows, :] = total
            rounded = total.astype(BF)
            gy[rows, :] = rounded
            new = (incoming * hat, incoming, rounded.astype(F32), outer)
            return tuple(old + column_sum(n) for old, n in zip(carry, new))

        zero = jnp.zeros((1, width), F32)
        done = lax.fori_loop(0, tokens // step, end, (zero,) * 4)
        sums[...] = jnp.concatenate([*done, jnp.zeros((4, width), F32)], axis=0)


def hidden(a2, og, x2, weights, b_up, b_down, gain, rows_each):
    tokens, width = a2.shape
    units = (weights.shape[1] - width) // 2
    folds = units // width
    fixed = pl.BlockSpec((tokens, width), lambda j: (0, 0))
    once = pl.BlockSpec((tokens, width), lambda j: (0, 0), pipeline_mode=pl.Buffered(1))
    cols = pl.BlockSpec((width, width), lambda j: (0, j))
    rows = pl.BlockSpec((width // folds, units), lambda j: (j, 0))
    row = pl.BlockSpec((1, width), lambda j: (0, j))
    row_one = pl.BlockSpec((1, width), lambda j: (0, 0))
    return call(
        functools.partial(hidden_body, rows_each, 256),
        (folds,),
        [once, once, once, rows, pl.BlockSpec((width, width), lambda j: (0, folds + j)), row, row_one,
         row_one],
        [rows, cols, row, fixed, fixed, fixed, pl.BlockSpec((8, width), lambda j: (0, 0))],
        [
            shape((width, units), BF),
            shape((width, units), BF),
            shape((1, units), F32),
            shape((tokens, width), BF),
            shape((tokens, width), F32),
            shape((tokens, width), BF),
            shape((8, width), F32),
        ],
        [
            pltpu.VMEM((tokens, width), F32),
            pltpu.VMEM((tokens, width), F32),
            pltpu.VMEM((width, tokens), BF),
            pltpu.VMEM((tokens, width), BF),
            pltpu.VMEM((tokens, width), BF),
            pltpu.VMEM((width, width), BF),
            pltpu.VMEM((width, width), BF),
        ],
        12 * tokens * width * units,
        "hidden",
    )(a2, og, x2, weights, weights, b_up, b_down, gain)


def mix_back_body(gy, att, w_out, go, w_grad):
    go[...] = nt(gy[...], w_out[...]).astype(BF)
    w_grad[...] = tn(att[...], gy[...]).astype(BF)


def mix_back(gy, att, weights):
    tokens, width = gy.shape
    cols = 256
    last = weights.shape[1] // width - 1
    narrow = pl.BlockSpec((tokens, cols), lambda j: (0, j))
    rows = pl.BlockSpec((cols, width), lambda j: (j, 0))
    return call(
        mix_back_body,
        (width // cols,),
        [
            pl.BlockSpec((tokens, width), lambda j: (0, 0)),
            narrow,
            pl.BlockSpec((cols, width), lambda j: (j, last)),
        ],
        [narrow, rows],
        [shape((tokens, width), BF), shape((width, width), BF)],
        [],
        4 * tokens * width * width,
        "mix_back",
    )(gy, att, weights)


def project_grad_body(a1, grads, out, turned):
    @pl.when(pl.program_id(0) == 0)
    def _():
        turned[...] = a1[...].T

    for part in range(0, turned.shape[0], 256):
        rows = slice(part, part + 256)
        out[rows, :] = nn(turned[rows, :], grads[...]).astype(BF)


def project_grad(a1, grads):
    tokens, width = a1.shape
    return call(
        project_grad_body,
        (3,),
        [
            pl.BlockSpec((tokens, width), lambda j: (0, 0)),
            pl.BlockSpec((tokens, width), lambda j: (0, j)),
        ],
        [pl.BlockSpec((width, width), lambda j: (0, j))],
        [shape((width, 3 * width), BF)],
        [pltpu.VMEM((width, tokens), BF)],
        6 * tokens * width * width,
        "project_grad",
    )(a1, grads)[0]


def project_back_body(grads, weights, x, gx2, gain, out, sums):
    width = x.shape[1]
    incoming = nt(grads[...], weights[...])
    hat, scale = normed(x[...].astype(F32))
    out[...] = gx2[...] + norm_back(hat, scale, incoming * gain[...])
    new = jnp.concatenate(
        [column_sum(incoming * hat), column_sum(incoming), jnp.zeros((6, width), F32)], axis=0
    )

    @pl.when(pl.program_id(0) == 0)
    def _():
        sums[...] = new

    @pl.when(pl.program_id(0) > 0)
    def _():
        sums[...] += new


def project_back(grads, weights, x, gx2, gain):
    tokens, width = x.shape
    step = 256
    block = pl.BlockSpec((step, width), lambda t: (t, 0))
    return call(
        project_back_body,
        (tokens // step,),
        [
            pl.BlockSpec((step, 3 * width), lambda t: (t, 0)),
            pl.BlockSpec((width, 3 * width), lambda t: (0, 0)),
            block,
            block,
            pl.BlockSpec((1, width), lambda t: (0, 0)),
        ],
        [block, pl.BlockSpec((8, width), lambda t: (0, 0))],
        [shape((tokens, width), F32), shape((8, width), F32)],
        [],
        6 * tokens * width * width,
        "project_back",
    )(grads, weights, x, gx2, gain)


AXES = ("side", "front", "core", "fsdp")


def split_mesh(mesh):
    outer, inner = mesh.shape["dp"], mesh.shape["fsdp"]
    cores = 2 if outer % 2 == 0 else 1
    side = math.isqrt(outer // cores)
    while (outer // cores) % side:
        side -= 1
    sizes = (side, outer // cores // side, cores, inner)
    return Mesh(mesh.devices.reshape(sizes), AXES)


def shifted(values, axis, distance):
    size = lax.axis_size(axis)
    return lax.ppermute(values, axis, [(i, (i + distance) % size) for i in range(size)])


def direct(values, axis):
    return [values] + [shifted(values, axis, d) for d in range(1, lax.axis_size(axis))]


def joined(parts):
    return parts[0] if len(parts) == 1 else jnp.concatenate(parts, axis=0)


def place_body(count, owners, *refs):
    parts, out, sems = refs[:count], refs[count], refs[count + 1]
    copies = []
    for part in parts:
        for n in range(part.shape[0]):
            at = len(copies)
            copies.append(pltpu.make_async_copy(part.at[n], out.at[owners[at]], sems.at[at]))
    for copy in copies:
        copy.start()
    for copy in copies:
        copy.wait()


def place(parts, owners):
    total = sum(p.shape[0] for p in parts)
    _, rows, cols = parts[0].shape
    out = pl.pallas_call(
        functools.partial(place_body, len(parts)),
        in_specs=[pl.BlockSpec(memory_space=pltpu.SMEM)]
        + [pl.BlockSpec(memory_space=pl.ANY)] * len(parts),
        out_specs=pl.BlockSpec(memory_space=pltpu.VMEM),
        out_shape=shape((total, rows, cols), parts[0].dtype),
        scratch_shapes=[pltpu.SemaphoreType.DMA((total,))],
        compiler_params=pltpu.CompilerParams(vmem_limit_bytes=VMEM_LIMIT),
        name="place",
    )(owners, *parts)
    return out.reshape(total * rows, cols)


def gather(shard):
    side, front, cores, depth = (lax.axis_size(a) for a in AXES)
    here = [lax.axis_index(a) for a in AXES]

    def owner(a, b, c, z):
        place_a, place_b = (here[0] - a) % side, (here[1] - b) % front
        place_c, place_z = (here[2] - c) % cores, (here[3] - z) % depth
        return ((place_a * front + place_b) * cores + place_c) * depth + place_z

    line = direct(shard[None], "fsdp")
    cut = max(1, depth // 2)
    parts, owners = [], []
    for low, high, order in ((0, cut, (0, 1)), (cut, depth, (1, 0))):
        if low == high:
            continue
        block = joined(line[low:high])
        for axis in order:
            block = joined(direct(block, AXES[axis]))
        for c, piece in enumerate(direct(block, "core")):
            parts.append(piece)
            sizes = [(side, front)[axis] for axis in order]
            for second in range(sizes[1]):
                for first in range(sizes[0]):
                    step = [0, 0]
                    step[order[0]], step[order[1]] = first, second
                    owners += [owner(step[0], step[1], c, z) for z in range(low, high)]
    return place(parts, jnp.stack(owners).astype(jnp.int32))


def taken(values, index, dim):
    return lax.dynamic_index_in_dim(values, index, dim, keepdims=False)


def summed_over(values, axis, dim, last=False):
    size, here = lax.axis_size(axis), lax.axis_index(axis)
    total = taken(values, here, dim).astype(F32)
    for d in range(1, size):
        total += shifted(taken(values, (here + d) % size, dim), axis, d).astype(F32)
    return total if last else total.astype(BF)


def by_owner(grad):
    sizes = [lax.axis_size(a) for a in AXES]
    rows = grad.shape[0] // math.prod(sizes)
    return grad.reshape(*sizes, rows, grad.shape[1])


def over_cores(grads):
    parts = [summed_over(by_owner(g), "core", 2) for g in grads]
    return parts[0] if len(parts) == 1 else jnp.concatenate(parts, axis=-1)


def spread(values):
    depth = lax.axis_size("fsdp")
    cut = max(1, depth // 2)
    halves = []
    for low, high, order in ((0, cut, (0, 1)), (cut, depth, (1, 0))):
        if low == high:
            continue
        block = values[:, :, low:high]
        block = summed_over(block, AXES[order[0]], order[0])
        halves.append(summed_over(block, AXES[order[1]], 0))
    return summed_over(joined(halves), "fsdp", 0, last=True)


def spread_wide(values):
    flat = values.reshape(-1, values.shape[-1])
    flat = lax.psum_scatter(flat, AXES[:2], scatter_dimension=0, tiled=True)
    return lax.psum_scatter(flat, AXES[3], scatter_dimension=0, tiled=True).astype(F32)


def regrouped(values, outer, inner):
    rows, cols = values.shape
    size = cols // (outer * inner)
    return values.reshape(rows, outer, inner, size).transpose(0, 2, 1, 3).reshape(rows, cols)


def pack_columns(vectors, rows):
    flat = jnp.concatenate(vectors)
    columns = flat.reshape(-1, rows).T
    return jnp.pad(columns, ((0, 0), (0, LANES - columns.shape[1])))


def on_device(patches, picture_ids, norm1_gain, norm1_bias, qkv_weight, query_shift, value_shift,
              query_gain, query_bias, key_gain, out_weight, out_bias, norm2_gain, norm2_bias,
              up_weight, up_bias, down_weight, down_bias, out_grad):
    width = patches.shape[1]
    rows = qkv_weight.shape[0]
    units = up_weight.shape[1]
    folds = units // width
    groups = width // 256
    small = pack_columns(
        [norm1_gain, norm1_bias, query_shift, value_shift, query_gain, query_bias, key_gain,
         out_bias, norm2_gain, norm2_bias, down_bias, up_bias],
        rows,
    )
    first = gather(jnp.concatenate([regrouped(qkv_weight, 3, groups), small], axis=1))
    down_folded = down_weight.reshape(folds, rows, width).transpose(1, 0, 2).reshape(rows, units)
    second = gather_wide(jnp.concatenate([down_folded, up_weight, out_weight], axis=1))
    vectors = first[:, 3 * width :]
    b_up = vectors[:, 11 : 11 + folds].reshape(-1, rows, folds).transpose(0, 2, 1)
    b_up = b_up.reshape(1, -1).astype(F32)
    vectors = vectors.T.astype(F32)
    (gain_one, bias_one, q_shift, v_shift, q_gain, q_bias, k_gain, b_out, gain_two, bias_two,
     b_down) = [vectors[n : n + 1] for n in range(11)]

    extra_q, extra_k, padding = picture_lanes(picture_ids)
    a1, q, k, v, q_hat, k_hat, q_scale, k_scale = project(
        patches, gain_one, bias_one, first, q_shift, v_shift, q_gain, q_bias, k_gain
    )
    att, extra_back = attend(q, k, v, extra_q, extra_k, padding)
    x2, a2 = mix(att, second, b_out, patches, gain_two, bias_two)
    down_grad, up_grad, up_sum, mixed, gx2, gy, sums_two = hidden(
        a2, out_grad, x2, second, b_up, b_down, gain_two, rows
    )
    go, out_w_grad = mix_back(gy, att, second)
    half_sum = over_cores([down_grad, up_grad, out_w_grad])
    half_sum, go = lax.optimization_barrier((half_sum, go))
    wide_out = spread_wide(half_sum)
    grads, sums_att = attend_back(
        q, k, v, go, att, extra_back, extra_k, padding, q_hat, k_hat, q_scale, k_scale, q_gain,
        k_gain,
    )
    sums_att = sums_att.reshape(-1, 8, width).sum(axis=0)
    qkv_grad = project_grad(a1, grads)
    qkv_grad, gx2 = lax.optimization_barrier((qkv_grad, gx2))
    patches_grad, sums_one = project_back(grads, first, patches, gx2, gain_one)
    sums = jnp.concatenate([sums_one[:2], sums_att[:5], sums_two[:4]], axis=0)
    up_columns = up_sum.reshape(-1, folds, rows).transpose(0, 2, 1).reshape(width, folds)
    columns = jnp.concatenate([sums.T, up_columns], axis=1)
    columns = jnp.pad(columns, ((0, 0), (0, LANES - columns.shape[1]))).astype(BF)
    last = spread(over_cores([qkv_grad, columns]))
    qkv_out = regrouped(last[:, : 3 * width], groups, 3)
    final = last[:, 3 * width :].T
    (gain_one_out, bias_one_out, q_shift_out, v_shift_out, q_gain_out, q_bias_out, k_gain_out,
     gain_two_out, bias_two_out, out_bias_out, down_bias_out) = [final[n] for n in range(11)]
    down_out = wide_out[:, :units].reshape(rows, folds, width).transpose(1, 0, 2)
    return (
        mixed, patches_grad, gain_one_out, bias_one_out, qkv_out, q_shift_out, v_shift_out,
        q_gain_out, q_bias_out, k_gain_out, wide_out[:, 2 * units :], out_bias_out, gain_two_out,
        bias_two_out, wide_out[:, units : 2 * units], final[11 : 11 + folds].reshape(-1),
        down_out.reshape(rows * folds, width), down_bias_out,
    )


def gather_wide(shard):
    return lax.all_gather(shard, AXES, axis=0, tiled=True)


def solution(mesh):
    flat = P(AXES)
    wide = P(AXES, None)
    in_specs = (wide, flat, flat, flat, wide, flat, flat, flat, flat, flat, wide, flat, flat, flat,
                wide, flat, wide, flat, wide)
    out_specs = (wide, wide, flat, flat, wide, flat, flat, flat, flat, flat, wide, flat, flat, flat,
                 wide, flat, wide, flat)
    return jax.shard_map(
        on_device, mesh=split_mesh(mesh), in_specs=in_specs, out_specs=out_specs, check_vma=False
    )
```

```python
import functools
import math
import jax
import jax.numpy as jnp
from jax import lax
from jax.experimental import pallas as pl
from jax.experimental.pallas import tpu as pltpu
from jax.sharding import Mesh, PartitionSpec as P

HEADS = 12
HD = 64
ROW = 1024
EPSILON = 1e-06
BF = jnp.bfloat16
F32 = jnp.float32
EXP_SCALE = HD**-0.5 * math.log2(math.e)
VMEM_LIMIT = 56 << 20
LANES = 128


def nn(left, right):
    return jnp.dot(left, right, preferred_element_type=F32)


def nt(left, right):
    return lax.dot_general(left, right, (((1,), (1,)), ((), ())), preferred_element_type=F32)


def tn(left, right):
    return lax.dot_general(left, right, (((0,), (0,)), ((), ())), preferred_element_type=F32)


def call(body, grid, in_specs, out_specs, out_shape, scratch, flops, name, limit=VMEM_LIMIT):
    def run(*args):
        moved = sum(a.size * a.dtype.itemsize for a in args)
        moved += sum(math.prod(o.shape) * o.dtype.itemsize for o in out_shape)
        return pl.pallas_call(
            body,
            grid=grid,
            in_specs=in_specs,
            out_specs=out_specs,
            out_shape=out_shape,
            scratch_shapes=scratch,
            compiler_params=pltpu.CompilerParams(vmem_limit_bytes=limit),
            cost_estimate=pl.CostEstimate(flops=flops, bytes_accessed=moved, transcendentals=0),
            name=name,
        )(*args)

    return run


def shape(dims, kind):
    return jax.ShapeDtypeStruct(dims, kind)


def chunk_at(step, size):
    return pl.ds(pl.multiple_of(step * size, size), size)


def block_mean(size):
    rows_at = lax.broadcasted_iota(jnp.int32, (size, size), 0)
    cols_at = lax.broadcasted_iota(jnp.int32, (size, size), 1)
    return jnp.where(rows_at // HD == cols_at // HD, 1.0 / HD, 0.0).astype(BF)


def normed(values):
    average = jnp.mean(values, axis=-1, keepdims=True)
    centred = values - average
    variance = jnp.mean(centred * centred, axis=-1, keepdims=True)
    scale = lax.rsqrt(variance + EPSILON)
    return centred * scale, scale


def norm_back(hat, scale, grads):
    first = jnp.mean(grads, axis=-1, keepdims=True)
    second = jnp.mean(grads * hat, axis=-1, keepdims=True)
    return scale * (grads - first - hat * second)


def column_sum(values):
    return jnp.sum(values, axis=0, keepdims=True)


def project_body(x, gain, bias, weights, q_shift, v_shift, q_gain, q_bias, k_gain,
                 turned, q, k, v, q_hat, k_hat, q_scale, k_scale, a1):
    tokens = x.shape[0]
    step = 1024

    @pl.when(pl.program_id(0) == 0)
    def _():
        def first(t, carry):
            rows = chunk_at(t, 256)
            hat, scale = normed(x[rows, :].astype(F32))
            a1[rows, :] = (hat * gain[...] + bias[...]).astype(BF)
            return carry

        lax.fori_loop(0, tokens // 256, first, 0)
        turned[...] = a1[...].T

    cols = weights.shape[1] // 3
    means = block_mean(cols)

    def one(t, carry):
        rows = chunk_at(t, step)
        source = a1[rows, :]

        def head_norm(pre, out, hat_out, scale_out, gains, biases):
            high = pre.astype(BF)
            low = (pre - high.astype(F32)).astype(BF)
            centred = pre - (nn(high, means) + nn(low, means))
            variance = nn((centred * centred).astype(BF), means)
            scale = lax.rsqrt(variance + EPSILON)
            hat = centred * scale
            shifted = hat * gains
            out[rows, :] = (shifted if biases is None else shifted + biases).astype(BF)
            hat_out[rows, :] = hat.astype(BF)
            scale_out[rows, :] = scale.astype(BF)

        head_norm(nn(source, weights[:, :cols]) + q_shift[...], q, q_hat, q_scale, q_gain[...], q_bias[...])
        head_norm(nn(source, weights[:, cols : 2 * cols]), k, k_hat, k_scale, k_gain[...], None)
        v[rows, :] = (nn(source, weights[:, 2 * cols :]) + v_shift[...]).astype(BF)
        return carry

    lax.fori_loop(0, tokens // step, one, 0)


def project(x, gain, bias, weights, q_shift, v_shift, q_gain, q_bias, k_gain):
    tokens, width = x.shape
    cols = 256
    parts = width // cols
    whole = pl.BlockSpec((tokens, width), lambda j: (0, 0))
    wide = pl.BlockSpec((1, width), lambda j: (0, 0))
    row = pl.BlockSpec((1, cols), lambda j: (0, j))
    out = pl.BlockSpec((tokens, cols), lambda j: (0, j))
    return call(
        project_body,
        (parts,),
        [whole, wide, wide, pl.BlockSpec((width, 3 * cols), lambda j: (0, j))] + [row] * 5,
        [pl.BlockSpec((width, tokens), lambda j: (0, 0))] + [out] * 7,
        [shape((width, tokens), BF)] + [shape((tokens, width), BF)] * 7,
        [pltpu.VMEM((tokens, width), BF)],
        6 * tokens * width * width,
        "project",
    )(x, gain, bias, weights, q_shift, v_shift, q_gain, q_bias, k_gain)


def half(values, head):
    lane = lax.broadcasted_iota(jnp.int32, values.shape, 1)
    return jnp.where((lane < HD) if head == 0 else (lane >= HD), values, jnp.zeros_like(values))


def three_parts(values, lane):
    high = values.astype(BF).astype(F32)
    rest = values - high
    middle = rest.astype(BF).astype(F32)
    low = rest - middle
    return jnp.where(
        lane == 12, high, jnp.where(lane == 13, middle, jnp.where(lane == 14, low, 0.0))
    )


def picture_lanes(pic_ids):
    lane = lax.broadcasted_iota(jnp.int32, (pic_ids.shape[0], LANES), 1)
    same = (pic_ids[:, None] == lane + 1) & (lane < 10)
    for_q = jnp.where(same | (lane == 10), 32.0, 0.0).astype(BF)
    ones = jnp.where((lane >= 12) & (lane < 15), 1.0, 0.0)
    for_k = jnp.where(same, 64.0, jnp.where(lane == 10, -64.0, ones)).astype(BF)
    padding = jnp.broadcast_to((pic_ids == 0)[:, None], lane.shape).astype(F32)
    return for_q, for_k, padding


def attend_body(q, k, v, extra_q, extra_k, padding, att, extra_back):
    lane = lax.broadcasted_iota(jnp.int32, (ROW, LANES), 1)
    queries = jnp.concatenate([q[...], extra_q[...]], axis=1)
    results, totals = [], []
    for h in (0, 1):
        keys = jnp.concatenate([half(k[...], h), extra_k[...]], axis=1)
        powers = jnp.exp2(nt(keys, queries) * EXP_SCALE).astype(BF)
        mine = (lane < HD) if h == 0 else (lane >= HD)
        out = tn(jnp.where(mine, v[...], jnp.ones_like(v[...])), powers)
        low, high = out[:HD, :], out[HD:, :]
        results.append(low if h == 0 else high)
        totals.append(high if h == 0 else low)
    result = jnp.concatenate(results, axis=0).T
    pad = padding[...]
    total = jnp.concatenate(totals, axis=0).T + pad
    att[...] = ((result + pad * v[...].astype(F32)) / total).astype(BF)
    row_term = jnp.log(total) * -(HD**0.5)
    other = pltpu.roll(row_term, HD, 1)
    base = extra_q[...].astype(F32)
    for h in (0, 1):
        mine = row_term if h == 0 else other
        extra_back[h] = (base + three_parts(mine, lane)).astype(BF)


def attend(q, k, v, extra_q, extra_k, padding):
    tokens, width = q.shape
    pairs = width // LANES
    block = pl.BlockSpec((ROW, LANES), lambda r, p: (r, p))
    fixed = pl.BlockSpec((ROW, LANES), lambda r, p: (r, 0))
    return call(
        attend_body,
        (tokens // ROW, pairs),
        [block] * 3 + [fixed] * 3,
        [block, pl.BlockSpec((2, ROW, LANES), lambda r, p: (p, r, 0))],
        [shape((tokens, width), BF), shape((2 * pairs, tokens, LANES), BF)],
        [],
        16 * tokens * ROW * width,
        "attend",
    )(q, k, v, extra_q, extra_k, padding)


def attend_back_body(q, k, v, go, att, extra_q, extra_k, padding, q_hat, k_hat, q_scale, k_scale,
                     q_gain, k_gain, packed, sums):
    offset = lax.rem(pl.program_id(1), 2) * LANES
    q_at, k_at, v_at = [pl.ds(pl.multiple_of(offset + n, LANES), LANES) for n in (0, 256, 512)]
    lane = lax.broadcasted_iota(jnp.int32, (ROW, LANES), 1)
    rows_at = lax.broadcasted_iota(jnp.int32, (LANES, LANES), 0)
    cols_at = lax.broadcasted_iota(jnp.int32, (LANES, LANES), 1)
    terms = go[...].astype(F32) * att[...].astype(F32)
    high = terms.astype(BF)
    low = (terms - high.astype(F32)).astype(BF)
    v_extra = jnp.where((lane >= 12) & (lane < 15), 1.0, 0.0).astype(BF)
    q_half, k_half, go_half, probs_all, grads_all = [], [], [], [], []
    for h in (0, 1):
        mine = (rows_at < HD) if h == 0 else (rows_at >= HD)
        pick = jnp.where(mine & (cols_at >= 12) & (cols_at < 15), 1.0, 0.0).astype(BF)
        delta = nn(high, pick) + nn(low, pick)
        go_extra = jnp.concatenate([go[...], three_parts(-delta, lane).astype(BF)], axis=1)
        key = half(k[...], h)
        scores = nt(
            jnp.concatenate([q[...], extra_q[h]], axis=1),
            jnp.concatenate([key, extra_k[...]], axis=1),
        )
        pulled = nt(go_extra, jnp.concatenate([half(v[...], h), v_extra], axis=1))
        probs = jnp.exp2(scores * EXP_SCALE)
        q_half.append(half(q[...], h))
        k_half.append(key)
        go_half.append(half(go[...], h))
        probs_all.append(probs.astype(BF))
        grads_all.append((probs * pulled).astype(BF))
    grad_v = tn(jnp.concatenate(go_half, axis=0), jnp.concatenate(probs_all, axis=0)).T
    grad_k = tn(jnp.concatenate(q_half, axis=0), jnp.concatenate(grads_all, axis=0)).T * HD**-0.5
    keys_turned = jnp.concatenate([part.T for part in k_half], axis=1)
    grad_q = nt(keys_turned, jnp.concatenate(grads_all, axis=1)).T * HD**-0.5
    means = block_mean(LANES)

    def head_norm_back(incoming, hat, scale, gains):
        inner = incoming * gains
        first = nn(inner.astype(BF), means)
        second = nn((inner * hat).astype(BF), means)
        return (scale * (inner - first - hat * second)).astype(BF)

    out_v = (grad_v + padding[...] * go[...].astype(F32)).astype(BF)
    packed[:, v_at] = out_v
    hat = k_hat[...].astype(F32)
    packed[:, k_at] = head_norm_back(grad_k, hat, k_scale[...].astype(F32), k_gain[...])
    k_sum = column_sum(grad_k * hat)
    hat = q_hat[...].astype(F32)
    out_q = head_norm_back(grad_q, hat, q_scale[...].astype(F32), q_gain[...])
    packed[:, q_at] = out_q
    parts = [out_q.astype(F32), out_v.astype(F32), grad_q * hat, grad_q]
    zero = jnp.zeros((3, LANES), F32)
    sums[...] = jnp.concatenate([*map(column_sum, parts), k_sum, zero], axis=0)


def attend_back(q, k, v, go, att, extra_q, extra_k, padding, q_hat, k_hat, q_scale, k_scale,
                q_gain, k_gain):
    tokens, width = q.shape
    count = tokens // ROW
    block = pl.BlockSpec((ROW, LANES), lambda r, p: (r, p))
    fixed = pl.BlockSpec((ROW, LANES), lambda r, p: (r, 0))
    row = pl.BlockSpec((1, LANES), lambda r, p: (0, p))
    return call(
        attend_back_body,
        (count, width // LANES),
        [block] * 5
        + [pl.BlockSpec((2, ROW, LANES), lambda r, p: (p, r, 0)), fixed, fixed]
        + [block] * 4
        + [row] * 2,
        [
            pl.BlockSpec((ROW, 6 * LANES), lambda r, p: (r, p // 2)),
            pl.BlockSpec((8, LANES), lambda r, p: (r, p)),
        ],
        [shape((tokens, 3 * width), BF), shape((8 * count, width), F32)],
        [],
        40 * tokens * ROW * width,
        "attend_back",
    )(q, k, v, go, att, extra_q, extra_k, padding, q_hat, k_hat, q_scale, k_scale, q_gain, k_gain)


SLOPE = math.sqrt(2.0 / math.pi)
CUBE = 0.044715


def gelu_pair(values):
    square = values * values
    share = 0.5 + 0.5 * jnp.tanh(values * (SLOPE + (SLOPE * CUBE) * square))
    gelu = values * share
    return gelu, share + gelu * (1.0 - share) * (2 * SLOPE + (6 * SLOPE * CUBE) * square)


UP_LANE = 11


def hidden_body(counts, core, *refs):
    (att, w_out, patches, og, folded, up, b_out, b_up, b_down, gain, bias, mine_down, other_down, mine_up,
     other_up, sum_up, mixed, gx2, gy, sums, x2, a2, y, ga, turned, act, grad, down) = refs
    rows_each, groups = counts
    tokens, width = a2.shape
    folds = folded.shape[1] // width
    each = folded.shape[0] // rows_each
    step = pl.program_id(0)

    @pl.when(step == 0)
    def _():
        y[...] = jnp.zeros_like(y)
        ga[...] = jnp.zeros_like(ga)

        def mix(t, carry):
            rows = chunk_at(t, 512)
            middle = patches[rows, :].astype(F32) + (nn(att[rows, :], w_out[...]) + b_out[...])
            x2[rows, :] = middle
            a2[rows, :] = (normed(middle)[0] * gain[...] + bias[...]).astype(BF)
            return carry

        lax.fori_loop(0, tokens // 512, mix, 0)
        turned[...] = a2[...].T

    for o in range(each):
        for w in range(folds):
            at = (o * folds + w) * rows_each
            source = folded[o * rows_each : o * rows_each + rows_each, w * width : w * width + width]
            down[at : at + rows_each, :] = source

    value, slope = gelu_pair(nn(a2[...], up[...]) + b_up[...])
    act[...] = value.astype(BF)
    y[...] += nn(act[...], down[...])
    pulled = nt(og[...], down[...]) * slope
    grad[...] = pulled.astype(BF)
    ga[...] += nt(grad[...], up[...])
    summed = jnp.broadcast_to(column_sum(grad[...].astype(F32)), (LANES, width)).T
    lane = lax.broadcasted_iota(jnp.int32, (rows_each, LANES), 1)
    for o in range(each):
        columns = jnp.zeros((rows_each, LANES), F32)
        for w in range(folds):
            at = (o * folds + w) * rows_each
            columns = jnp.where(lane == UP_LANE + w, summed[at : at + rows_each, :], columns)
        sum_up[o * rows_each : o * rows_each + rows_each, :] = columns

    down_rows = tn(act[...], og[...]).astype(BF)
    up_rows = nn(turned[...], grad[...]).astype(BF)

    def emit(down_refs, up_refs):
        for o in range(each):
            block, inner = divmod(o, 2 * groups)
            c, z = divmod(inner, groups)
            rows = slice(z * rows_each, z * rows_each + rows_each)
            for w in range(folds):
                at = (o * folds + w) * rows_each
                down_refs[c][block, rows, w * width : w * width + width] = down_rows[
                    at : at + rows_each, :
                ]
        size = groups * rows_each
        for block in range(width // (2 * size)):
            for c in (0, 1):
                at = (2 * block + c) * size
                up_refs[c][block, :, :] = up_rows[at : at + size, :]

    @pl.when(core[0] == 0)
    def _():
        emit((mine_down, other_down), (mine_up, other_up))

    @pl.when(core[0] == 1)
    def _():
        emit((other_down, mine_down), (other_up, mine_up))

    @pl.when(step == pl.num_programs(0) - 1)
    def _():
        def end(t, carry):
            rows = chunk_at(t, 256)
            middle = x2[rows, :]
            outer = og[rows, :].astype(F32)
            mixed[rows, :] = (middle + (y[rows, :] + b_down[...])).astype(BF)
            hat, scale = normed(middle)
            incoming = ga[rows, :]
            total = outer + norm_back(hat, scale, incoming * gain[...])
            gx2[rows, :] = total
            rounded = total.astype(BF)
            gy[rows, :] = rounded
            new = (incoming * hat, incoming, rounded.astype(F32), outer)
            return tuple(old + column_sum(n) for old, n in zip(carry, new))

        zero = jnp.zeros((1, width), F32)
        done = lax.fori_loop(0, tokens // 256, end, (zero,) * 4)
        sums[...] = jnp.concatenate([*done, jnp.zeros((4, width), F32)], axis=0)


def hidden(core, att, patches, og, weights, b_out, b_up, b_down, gain, bias, rows_each, groups):
    tokens, width = patches.shape
    units = (weights.shape[1] - width) // 2
    folds = units // width
    last = weights.shape[1] // width - 1
    blocks = width // (2 * groups * rows_each)
    each = blocks // folds
    size = groups * rows_each
    smem = pl.BlockSpec(memory_space=pltpu.SMEM)
    single = dict(pipeline_mode=pl.Buffered(1))
    fixed = pl.BlockSpec((tokens, width), lambda j: (0, 0), **single)
    row = pl.BlockSpec((1, width), lambda j: (0, j))
    row_one = pl.BlockSpec((1, width), lambda j: (0, 0))
    by_rows = pl.BlockSpec((each, size, units), lambda j: (j, 0, 0))
    by_cols = pl.BlockSpec((blocks, size, width), lambda j: (0, 0, j))
    square = pltpu.VMEM((tokens, width), BF)
    return call(
        functools.partial(hidden_body, (rows_each, groups)),
        (folds,),
        [
            smem,
            fixed,
            pl.BlockSpec((width, width), lambda j: (0, last), **single),
            fixed,
            fixed,
            pl.BlockSpec((width // folds, units), lambda j: (j, 0)),
            pl.BlockSpec((width, width), lambda j: (0, folds + j)),
            row_one,
            row,
            row_one,
            row_one,
            row_one,
        ],
        [by_rows, by_rows, by_cols, by_cols, pl.BlockSpec((width // folds, LANES), lambda j: (j, 0)), fixed, fixed, fixed,
         pl.BlockSpec((8, width), lambda j: (0, 0))],
        [shape((blocks, size, units), BF)] * 4
        + [
            shape((width, LANES), F32),
            shape((tokens, width), BF),
            shape((tokens, width), F32),
            shape((tokens, width), BF),
            shape((8, width), F32),
        ],
        [
            pltpu.VMEM((tokens, width), F32),
            square,
            pltpu.VMEM((tokens, width), F32),
            pltpu.VMEM((tokens, width), F32),
            pltpu.VMEM((width, tokens), BF),
            square,
            square,
            pltpu.VMEM((width, width), BF),
        ],
        12 * tokens * width * units,
        "hidden",
    )(core, att, weights, patches, og, weights, weights, b_out, b_up, b_down, gain, bias)


def mix_back_body(core, gy, att, w_out, go, mine, other):
    go[...] = nt(gy[...], w_out[...]).astype(BF)
    grads = tn(att[...], gy[...]).astype(BF)
    blocks, size, _ = mine.shape

    def emit(refs):
        for n in range(2 * blocks):
            refs[n % 2][n // 2, :, :] = grads[n * size : n * size + size, :]

    @pl.when(core[0] == 0)
    def _():
        emit((mine, other))

    @pl.when(core[0] == 1)
    def _():
        emit((other, mine))


def mix_back(core, gy, att, weights, size):
    tokens, width = gy.shape
    last = weights.shape[1] // width - 1
    blocks = width // (2 * size)
    whole = pl.BlockSpec((tokens, width), lambda j: (0, 0))
    grads = pl.BlockSpec((blocks, size, width), lambda j: (0, 0, 0))
    return call(
        mix_back_body,
        (1,),
        [
            pl.BlockSpec(memory_space=pltpu.SMEM),
            whole,
            whole,
            pl.BlockSpec((width, width), lambda j: (0, last)),
        ],
        [whole, grads, grads],
        [shape((tokens, width), BF)] + [shape((blocks, size, width), BF)] * 2,
        [],
        4 * tokens * width * width,
        "mix_back",
    )(core, gy, att, weights)


def merge_body(count, *refs):
    out = refs[2 * count]
    at = 0
    for n in range(count):
        size = refs[n].shape[2]
        total = refs[n][...].astype(F32) + refs[count + n][...].astype(F32)
        out[:, :, at : at + size] = total.astype(BF)
        at += size


def merge(mine, received):
    blocks, size, _ = mine[0].shape
    widths = [m.shape[2] for m in mine]
    many = 2
    specs = [pl.BlockSpec((many, size, w), lambda j: (j, 0, 0)) for w in widths]
    return call(
        functools.partial(merge_body, len(mine)),
        (blocks // many,),
        specs + specs,
        [pl.BlockSpec((many, size, sum(widths)), lambda j: (j, 0, 0))],
        [shape((blocks, size, sum(widths)), BF)],
        [],
        2 * blocks * size * sum(widths),
        "merge",
        20 << 20,
    )(*mine, *received)[0]


def project_grad_body(core, turned, grads, weights, vectors, sums_att, sums_two, sum_up, mine,
                      other, mine_columns, other_columns, gain_sum, bias_sum):
    result = nn(turned[...], grads[...])
    blocks, size, _ = mine.shape
    width = turned.shape[0]
    step = pl.program_id(0)
    wide = (width, LANES)
    current = weights[...].astype(F32)
    new_gain = jnp.broadcast_to(jnp.sum(result * current, axis=1, keepdims=True), wide)
    grad_sum = column_sum(grads[...].astype(F32))
    new_bias = jnp.broadcast_to(jnp.sum(current * grad_sum, axis=1, keepdims=True), wide)
    rounded = result.astype(BF)

    def emit(values, refs):
        for n in range(2 * blocks):
            refs[n % 2][n // 2, :, :] = values[n * size : n * size + size, :]

    def by_core(values, first, second):
        @pl.when(core[0] == 0)
        def _():
            emit(values, (first, second))

        @pl.when(core[0] == 1)
        def _():
            emit(values, (second, first))

    by_core(rounded, mine, other)

    @pl.when(step == 0)
    def _():
        gain_sum[...] = new_gain
        bias_sum[...] = new_bias

    @pl.when(step > 0)
    def _():
        gain_sum[...] += new_gain
        bias_sum[...] += new_bias

    @pl.when(step == pl.num_programs(0) - 1)
    def _():
        lane = lax.broadcasted_iota(jnp.int32, wide, 1)
        pair = vectors[...].astype(F32)
        gain = jnp.sum(jnp.where(lane == 0, pair, 0.0), axis=1, keepdims=True)
        bias = jnp.sum(jnp.where(lane == 1, pair, 0.0), axis=1, keepdims=True)
        gain_grad = (gain_sum[...] - bias * bias_sum[...]) / gain
        used = [jnp.zeros((2, width), F32), sums_att[:5, :], sums_two[:4, :]]
        zeros = jnp.zeros((LANES - UP_LANE, width), F32)
        columns = jnp.concatenate([*used, zeros], axis=0).T + sum_up[...]
        columns = jnp.where(lane == 0, gain_grad, jnp.where(lane == 1, bias_sum[...], columns))
        by_core(columns.astype(BF), mine_columns, other_columns)


def project_grad(core, turned, grads, weights, sums_att, sums_two, sum_up, size):
    width, tokens = turned.shape
    blocks = width // (2 * size)
    out = pl.BlockSpec((blocks, size, width), lambda j: (0, 0, j))
    columns = pl.BlockSpec((blocks, size, LANES), lambda j: (0, 0, 0))
    eight = pl.BlockSpec((8, width), lambda j: (0, 0))
    last = 3 * width // LANES
    return call(
        project_grad_body,
        (3,),
        [
            pl.BlockSpec(memory_space=pltpu.SMEM),
            pl.BlockSpec((width, tokens), lambda j: (0, 0)),
            pl.BlockSpec((tokens, width), lambda j: (0, j)),
            pl.BlockSpec((width, width), lambda j: (0, j)),
            pl.BlockSpec((width, LANES), lambda j: (0, last)),
            eight,
            eight,
            pl.BlockSpec((width, LANES), lambda j: (0, 0)),
        ],
        [out, out, columns, columns],
        [shape((blocks, size, 3 * width), BF)] * 2 + [shape((blocks, size, LANES), BF)] * 2,
        [pltpu.VMEM((width, LANES), F32)] * 2,
        6 * tokens * width * width,
        "project_grad",
    )(core, turned, grads, weights, weights, sums_att, sums_two, sum_up)


def project_back_body(grads, weights, x, gx2, gain, out):
    incoming = nt(grads[...], weights[...])
    hat, scale = normed(x[...].astype(F32))
    out[...] = gx2[...] + norm_back(hat, scale, incoming * gain[...])


def project_back(grads, weights, x, gx2, gain):
    tokens, width = x.shape
    step = 256
    block = pl.BlockSpec((step, width), lambda t: (t, 0))
    return call(
        project_back_body,
        (tokens // step,),
        [
            pl.BlockSpec((step, 3 * width), lambda t: (t, 0)),
            pl.BlockSpec((width, 3 * width), lambda t: (0, 0)),
            block,
            block,
            pl.BlockSpec((1, width), lambda t: (0, 0)),
        ],
        [block],
        [shape((tokens, width), F32)],
        [],
        6 * tokens * width * width,
        "project_back",
    )(grads, weights, x, gx2, gain)[0]


AXES = ("side", "front", "core", "fsdp")


def split_mesh(mesh):
    outer, inner = mesh.shape["dp"], mesh.shape["fsdp"]
    cores = 2 if outer % 2 == 0 else 1
    side = math.isqrt(outer // cores)
    while (outer // cores) % side:
        side -= 1
    sizes = (side, outer // cores // side, cores, inner)
    return Mesh(mesh.devices.reshape(sizes), AXES)


def shifted(values, axis, distance):
    size = lax.axis_size(axis)
    return lax.ppermute(values, axis, [(i, (i + distance) % size) for i in range(size)])


def direct(values, axis):
    return [values] + [shifted(values, axis, d) for d in range(1, lax.axis_size(axis))]


def joined(parts):
    return parts[0] if len(parts) == 1 else jnp.concatenate(parts, axis=0)


def place_body(count, owners, *refs):
    parts, out, sems = refs[:count], refs[count], refs[count + 1]
    copies = []
    for part in parts:
        for n in range(part.shape[0]):
            at = len(copies)
            copies.append(pltpu.make_async_copy(part.at[n], out.at[owners[at]], sems.at[at]))
    for copy in copies:
        copy.start()
    for copy in copies:
        copy.wait()


def place(parts, owners):
    total = sum(p.shape[0] for p in parts)
    _, rows, cols = parts[0].shape
    out = pl.pallas_call(
        functools.partial(place_body, len(parts)),
        in_specs=[pl.BlockSpec(memory_space=pltpu.SMEM)]
        + [pl.BlockSpec(memory_space=pl.ANY)] * len(parts),
        out_specs=pl.BlockSpec(memory_space=pltpu.VMEM),
        out_shape=shape((total, rows, cols), parts[0].dtype),
        scratch_shapes=[pltpu.SemaphoreType.DMA((total,))],
        compiler_params=pltpu.CompilerParams(vmem_limit_bytes=VMEM_LIMIT),
        name="place",
    )(owners, *parts)
    return out.reshape(total * rows, cols)


def orders():
    depth = lax.axis_size("fsdp")
    cut = max(1, depth // 2)
    return [part for part in ((0, cut, (0, 1)), (cut, depth, (1, 0))) if part[0] < part[1]]


def begin(shard):
    line = direct(shard[None], "fsdp")
    return [joined(line[low:high]) for low, high, _ in orders()]


def across(blocks, stage):
    return [joined(direct(b, AXES[o[2][stage]])) for b, o in zip(blocks, orders())]


def over(blocks):
    return [part for b in blocks for part in direct(b, "core")]


def owner_table():
    sizes = [lax.axis_size(a) for a in AXES]
    here = [lax.axis_index(a) for a in AXES]
    steps = []
    for low, high, order in orders():
        for c in range(sizes[2]):
            for second in range(sizes[order[1]]):
                for first in range(sizes[order[0]]):
                    moved = {order[0]: first, order[1]: second}
                    steps += [(moved[0], moved[1], c, z) for z in range(low, high)]
    table = jnp.asarray(steps, jnp.int32)
    owner = jnp.zeros((len(steps),), jnp.int32)
    for n, size in enumerate(sizes):
        owner = owner * size + lax.rem(here[n] - table[:, n] + size, size)
    return owner


def taken(values, index, dim):
    return lax.dynamic_index_in_dim(values, index, dim, keepdims=False)


def summed_over(values, axis, dim, last=False):
    size, here = lax.axis_size(axis), lax.axis_index(axis)
    total = taken(values, here, dim).astype(F32)
    for d in range(1, size):
        total += shifted(taken(values, (here + d) % size, dim), axis, d).astype(F32)
    return total if last else total.astype(BF)


def added(left, right):
    return (left.astype(F32) + right.astype(F32)).astype(BF)


def joined_last(parts):
    return parts[0] if len(parts) == 1 else jnp.concatenate(parts, axis=-1)


def spread_chips(values, stage):
    if stage == 0:
        return [
            summed_over(values[:, :, low:high], AXES[order[0]], order[0])
            for low, high, order in orders()
        ]
    return [summed_over(v, AXES[o[2][1]], 0) for v, o in zip(values, orders())]


def regrouped(values, outer, inner):
    rows, cols = values.shape
    size = cols // (outer * inner)
    return values.reshape(rows, outer, inner, size).transpose(0, 2, 1, 3).reshape(rows, cols)


def pack_columns(vectors, rows):
    flat = jnp.concatenate(vectors)
    columns = flat.reshape(-1, rows).T
    return jnp.pad(columns, ((0, 0), (0, LANES - columns.shape[1])))


def on_device(patches, picture_ids, norm1_gain, norm1_bias, qkv_weight, query_shift, value_shift,
              query_gain, query_bias, key_gain, out_weight, out_bias, norm2_gain, norm2_bias,
              up_weight, up_bias, down_weight, down_bias, out_grad):
    width = patches.shape[1]
    rows = qkv_weight.shape[0]
    units = up_weight.shape[1]
    folds = units // width
    groups = width // 256
    small = pack_columns(
        [norm1_gain, norm1_bias, query_shift, value_shift, query_gain, query_bias, key_gain,
         out_bias, norm2_gain, norm2_bias, down_bias, up_bias],
        rows,
    )
    core = lax.axis_index("core").astype(jnp.int32).reshape(1)
    depth = lax.axis_size("fsdp")
    down_shard = down_weight.reshape(folds, rows, width).transpose(1, 0, 2).reshape(rows, units)
    second = lax.all_gather(
        jnp.concatenate([down_shard, up_weight, out_weight], axis=1), AXES, axis=0, tiled=True
    )
    one = begin(jnp.concatenate([regrouped(qkv_weight, 3, groups), small], axis=1))
    extras = (*picture_lanes(picture_ids), owner_table())
    one, extras = lax.optimization_barrier((one, extras))
    extra_q, extra_k, padding, owners = extras
    first = place(over(across(across(one, 0), 1)), owners)
    vectors = first[:, 3 * width :]
    b_up = vectors[:, 11 : 11 + folds].reshape(-1, rows, folds).transpose(0, 2, 1)
    b_up = b_up.reshape(1, -1).astype(F32)
    vectors = vectors.T.astype(F32)
    (gain_one, bias_one, q_shift, v_shift, q_gain, q_bias, k_gain, b_out, gain_two, bias_two,
     b_down) = [vectors[n : n + 1] for n in range(11)]

    turned, q, k, v, q_hat, k_hat, q_scale, k_scale = project(
        patches, gain_one, bias_one, first, q_shift, v_shift, q_gain, q_bias, k_gain
    )
    att, extra_back = attend(q, k, v, extra_q, extra_k, padding)
    (mine_down, other_down, mine_up, other_up, up_sum, mixed, gx2, gy, sums_two) = hidden(
        core, att, patches, out_grad, second, b_out, b_up, b_down, gain_two,
        bias_two, rows, depth
    )
    go, mine_out, other_out = mix_back(core, gy, att, second, depth * rows)
    received = [shifted(p, "core", 1) for p in (other_down, other_up, other_out)]
    merged = merge([mine_down, mine_up, mine_out], received)
    merged, go = lax.optimization_barrier((merged, go))
    flat = merged.reshape(-1, merged.shape[2])
    flat = lax.psum_scatter(flat, AXES[:2], scatter_dimension=0, tiled=True)
    grads, sums_att = attend_back(
        q, k, v, go, att, extra_back, extra_k, padding, q_hat, k_hat, q_scale, k_scale, q_gain,
        k_gain,
    )
    sums_att = sums_att.reshape(-1, 8, width).sum(axis=0)
    mine_qkv, other_qkv, mine_columns, other_columns = project_grad(
        core, turned, grads, first, sums_att, sums_two, up_sum, depth * rows
    )
    received_qkv = shifted(other_qkv, "core", 1)
    received_columns = shifted(other_columns, "core", 1)
    last = joined_last([added(mine_qkv, received_qkv), added(mine_columns, received_columns)])
    last, flat = lax.optimization_barrier((last, flat))
    wide_out = lax.psum_scatter(flat, AXES[3], scatter_dimension=0, tiled=True).astype(F32)
    sizes = [lax.axis_size(a) for a in AXES]
    last = last.reshape(sizes[0], sizes[1], depth, rows, -1)
    halves = spread_chips(spread_chips(last, 0), 1)
    halves, gx2 = lax.optimization_barrier((halves, gx2))
    last = summed_over(joined(halves), "fsdp", 0, last=True)
    patches_grad = project_back(grads, first, patches, gx2, gain_one)
    qkv_out = regrouped(last[:, : 3 * width], groups, 3)
    final = last[:, 3 * width :].T
    (gain_one_out, bias_one_out, q_shift_out, v_shift_out, q_gain_out, q_bias_out, k_gain_out,
     gain_two_out, bias_two_out, out_bias_out, down_bias_out) = [final[n] for n in range(11)]
    down_out = wide_out[:, :units].reshape(rows, folds, width).transpose(1, 0, 2)
    return (
        mixed, patches_grad, gain_one_out, bias_one_out, qkv_out, q_shift_out, v_shift_out,
        q_gain_out, q_bias_out, k_gain_out, wide_out[:, 2 * units :], out_bias_out, gain_two_out,
        bias_two_out, wide_out[:, units : 2 * units], final[11 : 11 + folds].reshape(-1),
        down_out.reshape(rows * folds, width), down_bias_out,
    )


def solution(mesh):
    flat = P(AXES)
    wide = P(AXES, None)
    in_specs = (wide, flat, flat, flat, wide, flat, flat, flat, flat, flat, wide, flat, flat, flat,
                wide, flat, wide, flat, wide)
    out_specs = (wide, wide, flat, flat, wide, flat, flat, flat, flat, flat, wide, flat, flat, flat,
                 wide, flat, wide, flat)
    return jax.shard_map(
        on_device, mesh=split_mesh(mesh), in_specs=in_specs, out_specs=out_specs, check_vma=False
    )
```

```python
import functools
import math
import jax
import jax.numpy as jnp
from jax import lax
from jax.experimental import pallas as pl
from jax.experimental.pallas import tpu as pltpu
from jax.sharding import Mesh, PartitionSpec as P

HEADS = 12
HD = 64
ROW = 1024
EPSILON = 1e-06
BF = jnp.bfloat16
F32 = jnp.float32
EXP_SCALE = HD**-0.5 * math.log2(math.e)
VMEM_LIMIT = 56 << 20
LANES = 128
GAIN_ONE, BIAS_ONE, Q_SHIFT, V_SHIFT, Q_GAIN, Q_BIAS, K_GAIN = range(7)
B_OUT, GAIN_TWO, BIAS_TWO, B_DOWN = range(7, 11)


def nn(left, right):
    return jnp.dot(left, right, preferred_element_type=F32)


def nt(left, right):
    return lax.dot_general(left, right, (((1,), (1,)), ((), ())), preferred_element_type=F32)


def tn(left, right):
    return lax.dot_general(left, right, (((0,), (0,)), ((), ())), preferred_element_type=F32)


def call(body, grid, in_specs, out_specs, out_shape, scratch, flops, name, limit=VMEM_LIMIT):
    def run(*args):
        moved = sum(a.size * a.dtype.itemsize for a in args)
        moved += sum(math.prod(o.shape) * o.dtype.itemsize for o in out_shape)
        return pl.pallas_call(
            body,
            grid=grid,
            in_specs=in_specs,
            out_specs=out_specs,
            out_shape=out_shape,
            scratch_shapes=scratch,
            compiler_params=pltpu.CompilerParams(vmem_limit_bytes=limit),
            cost_estimate=pl.CostEstimate(flops=flops, bytes_accessed=moved, transcendentals=0),
            name=name,
        )(*args)

    return run


def row_of(vectors, n):
    return vectors[n : n + 1, :]


def shape(dims, kind):
    return jax.ShapeDtypeStruct(dims, kind)


def chunk_at(step, size):
    return pl.ds(pl.multiple_of(step * size, size), size)


def block_mean(size):
    rows_at = lax.broadcasted_iota(jnp.int32, (size, size), 0)
    cols_at = lax.broadcasted_iota(jnp.int32, (size, size), 1)
    return jnp.where(rows_at // HD == cols_at // HD, 1.0 / HD, 0.0).astype(BF)


def normed(values):
    average = jnp.mean(values, axis=-1, keepdims=True)
    centred = values - average
    variance = jnp.mean(centred * centred, axis=-1, keepdims=True)
    scale = lax.rsqrt(variance + EPSILON)
    return centred * scale, scale


def norm_back(hat, scale, grads):
    first = jnp.mean(grads, axis=-1, keepdims=True)
    second = jnp.mean(grads * hat, axis=-1, keepdims=True)
    return scale * (grads - first - hat * second)


def column_sum(values):
    return jnp.sum(values, axis=0, keepdims=True)


def project_body(x, whole_rows, weights, own_rows,
                 turned, q, k, v, q_hat, k_hat, q_scale, k_scale, a1):
    tokens = x.shape[0]
    step = 1024

    @pl.when(pl.program_id(0) == 0)
    def _():
        def first(t, carry):
            rows = chunk_at(t, 256)
            hat, scale = normed(x[rows, :].astype(F32))
            a1[rows, :] = (hat * row_of(whole_rows, GAIN_ONE) + row_of(whole_rows, BIAS_ONE)).astype(BF)
            return carry

        lax.fori_loop(0, tokens // 256, first, 0)
        turned[...] = a1[...].T

    cols = weights.shape[1] // 3
    means = block_mean(cols)

    def one(t, carry):
        rows = chunk_at(t, step)
        source = a1[rows, :]

        def head_norm(pre, out, hat_out, scale_out, gains, biases):
            high = pre.astype(BF)
            low = (pre - high.astype(F32)).astype(BF)
            centred = pre - (nn(high, means) + nn(low, means))
            variance = nn((centred * centred).astype(BF), means)
            scale = lax.rsqrt(variance + EPSILON)
            hat = centred * scale
            shifted = hat * gains
            out[rows, :] = (shifted if biases is None else shifted + biases).astype(BF)
            hat_out[rows, :] = hat.astype(BF)
            scale_out[rows, :] = scale.astype(BF)

        pre = nn(source, weights[:, :cols]) + row_of(own_rows, Q_SHIFT)
        head_norm(pre, q, q_hat, q_scale, row_of(own_rows, Q_GAIN), row_of(own_rows, Q_BIAS))
        pre = nn(source, weights[:, cols : 2 * cols])
        head_norm(pre, k, k_hat, k_scale, row_of(own_rows, K_GAIN), None)
        pre = nn(source, weights[:, 2 * cols :])
        v[rows, :] = (pre + row_of(own_rows, V_SHIFT)).astype(BF)
        return carry

    lax.fori_loop(0, tokens // step, one, 0)


def project(x, weights, vectors):
    tokens, width = x.shape
    cols = 256
    parts = width // cols
    whole = pl.BlockSpec((tokens, width), lambda j: (0, 0))
    out = pl.BlockSpec((tokens, cols), lambda j: (0, j))
    return call(
        project_body,
        (parts,),
        [
            whole,
            pl.BlockSpec((8, width), lambda j: (0, 0)),
            pl.BlockSpec((width, 3 * cols), lambda j: (0, j)),
            pl.BlockSpec((8, cols), lambda j: (0, j)),
        ],
        [pl.BlockSpec((width, tokens), lambda j: (0, 0))] + [out] * 7,
        [shape((width, tokens), BF)] + [shape((tokens, width), BF)] * 7,
        [pltpu.VMEM((tokens, width), BF)],
        6 * tokens * width * width,
        "project",
    )(x, vectors, weights, vectors)


def half(values, head):
    lane = lax.broadcasted_iota(jnp.int32, values.shape, 1)
    return jnp.where((lane < HD) if head == 0 else (lane >= HD), values, jnp.zeros_like(values))


def three_parts(values, lane):
    high = values.astype(BF).astype(F32)
    rest = values - high
    middle = rest.astype(BF).astype(F32)
    low = rest - middle
    return jnp.where(
        lane == 12, high, jnp.where(lane == 13, middle, jnp.where(lane == 14, low, 0.0))
    )


def picture_lanes(pic_ids):
    lane = lax.broadcasted_iota(jnp.int32, (pic_ids.shape[0], LANES), 1)
    same = (pic_ids[:, None] == lane + 1) & (lane < 10)
    for_q = jnp.where(same | (lane == 10), 32.0, 0.0).astype(BF)
    ones = jnp.where((lane >= 12) & (lane < 15), 1.0, 0.0)
    for_k = jnp.where(same, 64.0, jnp.where(lane == 10, -64.0, ones)).astype(BF)
    padding = jnp.broadcast_to((pic_ids == 0)[:, None], lane.shape).astype(F32)
    return for_q, for_k, padding


def attend_body(q, k, v, extra_q, extra_k, padding, att, extra_back):
    lane = lax.broadcasted_iota(jnp.int32, (ROW, LANES), 1)
    queries = jnp.concatenate([q[...], extra_q[...]], axis=1)
    results, totals = [], []
    for h in (0, 1):
        keys = jnp.concatenate([half(k[...], h), extra_k[...]], axis=1)
        powers = jnp.exp2(nt(keys, queries) * EXP_SCALE).astype(BF)
        mine = (lane < HD) if h == 0 else (lane >= HD)
        out = tn(jnp.where(mine, v[...], jnp.ones_like(v[...])), powers)
        low, high = out[:HD, :], out[HD:, :]
        results.append(low if h == 0 else high)
        totals.append(high if h == 0 else low)
    result = jnp.concatenate(results, axis=0).T
    pad = padding[...]
    total = jnp.concatenate(totals, axis=0).T + pad
    att[...] = ((result + pad * v[...].astype(F32)) / total).astype(BF)
    row_term = jnp.log(total) * -(HD**0.5)
    other = pltpu.roll(row_term, HD, 1)
    base = extra_q[...].astype(F32)
    for h in (0, 1):
        mine = row_term if h == 0 else other
        extra_back[h] = (base + three_parts(mine, lane)).astype(BF)


def attend(q, k, v, extra_q, extra_k, padding):
    tokens, width = q.shape
    pairs = width // LANES
    block = pl.BlockSpec((ROW, LANES), lambda r, p: (r, p))
    fixed = pl.BlockSpec((ROW, LANES), lambda r, p: (r, 0))
    return call(
        attend_body,
        (tokens // ROW, pairs),
        [block] * 3 + [fixed] * 3,
        [block, pl.BlockSpec((2, ROW, LANES), lambda r, p: (p, r, 0))],
        [shape((tokens, width), BF), shape((2 * pairs, tokens, LANES), BF)],
        [],
        16 * tokens * ROW * width,
        "attend",
    )(q, k, v, extra_q, extra_k, padding)


def attend_back_body(q, k, v, go, att, extra_q, extra_k, padding, q_hat, k_hat, q_scale, k_scale,
                     vectors, packed, sums):
    offset = lax.rem(pl.program_id(1), 2) * LANES
    q_at, k_at, v_at = [pl.ds(pl.multiple_of(offset + n, LANES), LANES) for n in (0, 256, 512)]
    lane = lax.broadcasted_iota(jnp.int32, (ROW, LANES), 1)
    rows_at = lax.broadcasted_iota(jnp.int32, (LANES, LANES), 0)
    cols_at = lax.broadcasted_iota(jnp.int32, (LANES, LANES), 1)
    terms = go[...].astype(F32) * att[...].astype(F32)
    high = terms.astype(BF)
    low = (terms - high.astype(F32)).astype(BF)
    v_extra = jnp.where((lane >= 12) & (lane < 15), 1.0, 0.0).astype(BF)
    q_half, k_half, go_half, probs_all, grads_all = [], [], [], [], []
    for h in (0, 1):
        mine = (rows_at < HD) if h == 0 else (rows_at >= HD)
        pick = jnp.where(mine & (cols_at >= 12) & (cols_at < 15), 1.0, 0.0).astype(BF)
        delta = nn(high, pick) + nn(low, pick)
        go_extra = jnp.concatenate([go[...], three_parts(-delta, lane).astype(BF)], axis=1)
        key = half(k[...], h)
        scores = nt(
            jnp.concatenate([q[...], extra_q[h]], axis=1),
            jnp.concatenate([key, extra_k[...]], axis=1),
        )
        pulled = nt(go_extra, jnp.concatenate([half(v[...], h), v_extra], axis=1))
        probs = jnp.exp2(scores * EXP_SCALE)
        q_half.append(half(q[...], h))
        k_half.append(key)
        go_half.append(half(go[...], h))
        probs_all.append(probs.astype(BF))
        grads_all.append((probs * pulled).astype(BF))
    grad_v = tn(jnp.concatenate(go_half, axis=0), jnp.concatenate(probs_all, axis=0)).T
    grad_k = tn(jnp.concatenate(q_half, axis=0), jnp.concatenate(grads_all, axis=0)).T * HD**-0.5
    keys_turned = jnp.concatenate([part.T for part in k_half], axis=1)
    grad_q = nt(keys_turned, jnp.concatenate(grads_all, axis=1)).T * HD**-0.5
    means = block_mean(LANES)

    def head_norm_back(incoming, hat, scale, gains):
        inner = incoming * gains
        first = nn(inner.astype(BF), means)
        second = nn((inner * hat).astype(BF), means)
        return (scale * (inner - first - hat * second)).astype(BF)

    out_v = (grad_v + padding[...] * go[...].astype(F32)).astype(BF)
    packed[:, v_at] = out_v
    hat = k_hat[...].astype(F32)
    packed[:, k_at] = head_norm_back(grad_k, hat, k_scale[...].astype(F32), row_of(vectors, K_GAIN))
    k_sum = column_sum(grad_k * hat)
    hat = q_hat[...].astype(F32)
    out_q = head_norm_back(grad_q, hat, q_scale[...].astype(F32), row_of(vectors, Q_GAIN))
    packed[:, q_at] = out_q
    parts = [out_q.astype(F32), out_v.astype(F32), grad_q * hat, grad_q]
    zero = jnp.zeros((3, LANES), F32)
    sums[...] = jnp.concatenate([*map(column_sum, parts), k_sum, zero], axis=0)


def attend_back(q, k, v, go, att, extra_q, extra_k, padding, q_hat, k_hat, q_scale, k_scale,
                vectors):
    tokens, width = q.shape
    count = tokens // ROW
    block = pl.BlockSpec((ROW, LANES), lambda r, p: (r, p))
    fixed = pl.BlockSpec((ROW, LANES), lambda r, p: (r, 0))
    eight = pl.BlockSpec((8, LANES), lambda r, p: (0, p))
    return call(
        attend_back_body,
        (count, width // LANES),
        [block] * 5
        + [pl.BlockSpec((2, ROW, LANES), lambda r, p: (p, r, 0)), fixed, fixed]
        + [block] * 4
        + [eight],
        [
            pl.BlockSpec((ROW, 6 * LANES), lambda r, p: (r, p // 2)),
            pl.BlockSpec((8, LANES), lambda r, p: (r, p)),
        ],
        [shape((tokens, 3 * width), BF), shape((8 * count, width), F32)],
        [],
        40 * tokens * ROW * width,
        "attend_back",
    )(q, k, v, go, att, extra_q, extra_k, padding, q_hat, k_hat, q_scale, k_scale, vectors)


SLOPE = math.sqrt(2.0 / math.pi)
CUBE = 0.044715


def gelu_pair(values):
    square = values * values
    share = 0.5 + 0.5 * jnp.tanh(values * (SLOPE + (SLOPE * CUBE) * square))
    gelu = values * share
    return gelu, share + gelu * (1.0 - share) * (2 * SLOPE + (6 * SLOPE * CUBE) * square)


UP_LANE = 11


def hidden_body(counts, core, *refs):
    (att, w_out, patches, og_out, folded, up, vectors, b_up, mine_down, other_down, mine_up,
     other_up, sum_up, mixed, gx2, gy, sums, x2, a2, y, ga, turned, act, grad, down, og,
     sems) = refs
    rows_each, groups = counts
    tokens, width = a2.shape
    folds = folded.shape[1] // width
    each = folded.shape[0] // rows_each
    step = pl.program_id(0)

    @pl.when(step == 0)
    def _():
        fetch = pltpu.make_async_copy(og_out, og, sems.at[0])
        fetch.start()
        y[...] = jnp.zeros_like(y)
        ga[...] = jnp.zeros_like(ga)

        def mix(t, carry):
            rows = chunk_at(t, 512)
            middle = patches[rows, :].astype(F32) + (nn(att[rows, :], w_out[...]) + row_of(vectors, B_OUT))
            x2[rows, :] = middle
            scaled = normed(middle)[0] * row_of(vectors, GAIN_TWO)
            a2[rows, :] = (scaled + row_of(vectors, BIAS_TWO)).astype(BF)
            return carry

        lax.fori_loop(0, tokens // 512, mix, 0)
        turned[...] = a2[...].T
        fetch.wait()

    for o in range(each):
        for w in range(folds):
            at = (o * folds + w) * rows_each
            source = folded[o * rows_each : o * rows_each + rows_each, w * width : w * width + width]
            down[at : at + rows_each, :] = source

    value, slope = gelu_pair(nn(a2[...], up[...]) + b_up[...])
    act[...] = value.astype(BF)
    y[...] += nn(act[...], down[...])
    pulled = nt(og[...], down[...]) * slope
    grad[...] = pulled.astype(BF)
    ga[...] += nt(grad[...], up[...])
    summed = jnp.broadcast_to(column_sum(grad[...].astype(F32)), (LANES, width)).T
    lane = lax.broadcasted_iota(jnp.int32, (rows_each, LANES), 1)
    for o in range(each):
        columns = jnp.zeros((rows_each, LANES), F32)
        for w in range(folds):
            at = (o * folds + w) * rows_each
            columns = jnp.where(lane == UP_LANE + w, summed[at : at + rows_each, :], columns)
        sum_up[o * rows_each : o * rows_each + rows_each, :] = columns

    down_rows = tn(act[...], og[...]).astype(BF)
    up_rows = nn(turned[...], grad[...]).astype(BF)

    def emit(down_refs, up_refs):
        for o in range(each):
            block, inner = divmod(o, 2 * groups)
            c, z = divmod(inner, groups)
            rows = slice(z * rows_each, z * rows_each + rows_each)
            for w in range(folds):
                at = (o * folds + w) * rows_each
                down_refs[c][block, rows, w * width : w * width + width] = down_rows[
                    at : at + rows_each, :
                ]
        size = groups * rows_each
        for block in range(width // (2 * size)):
            for c in (0, 1):
                at = (2 * block + c) * size
                up_refs[c][block, :, :] = up_rows[at : at + size, :]

    @pl.when(core[0] == 0)
    def _():
        emit((mine_down, other_down), (mine_up, other_up))

    @pl.when(core[0] == 1)
    def _():
        emit((other_down, mine_down), (other_up, mine_up))

    @pl.when(step == pl.num_programs(0) - 1)
    def _():
        carry = (jnp.zeros((1, width), F32),) * 4
        copies = []
        for t in range(tokens // 256):
            rows = slice(t * 256, t * 256 + 256)
            middle = x2[rows, :]
            outer = og[rows, :].astype(F32)
            act[rows, :] = (middle + (y[rows, :] + row_of(vectors, B_DOWN))).astype(BF)
            hat, scale = normed(middle)
            incoming = ga[rows, :]
            total = outer + norm_back(hat, scale, incoming * row_of(vectors, GAIN_TWO))
            ga[rows, :] = total
            rounded = total.astype(BF)
            grad[rows, :] = rounded
            for n, (source, target) in enumerate(((act, mixed), (ga, gx2), (grad, gy))):
                sem = sems.at[1 + 3 * t + n]
                copies.append(pltpu.make_async_copy(source.at[rows], target.at[rows], sem))
                copies[-1].start()
            new = (incoming * hat, incoming, rounded.astype(F32), outer)
            carry = tuple(old + column_sum(n) for old, n in zip(carry, new))
        sums[...] = jnp.concatenate([*carry, jnp.zeros((4, width), F32)], axis=0)
        for copy in copies:
            copy.wait()


def hidden(core, att, patches, og, weights, vectors, b_up, rows_each, groups):
    tokens, width = patches.shape
    units = (weights.shape[1] - width) // 2
    folds = units // width
    blocks = width // (2 * groups * rows_each)
    each = blocks // folds
    size = groups * rows_each
    smem = pl.BlockSpec(memory_space=pltpu.SMEM)
    single = dict(pipeline_mode=pl.Buffered(1))
    fixed = pl.BlockSpec((tokens, width), lambda j: (0, 0), **single)
    row = pl.BlockSpec((1, width), lambda j: (0, j))
    by_rows = pl.BlockSpec((each, size, units), lambda j: (j, 0, 0))
    by_cols = pl.BlockSpec((blocks, size, width), lambda j: (0, 0, j))
    square = pltpu.VMEM((tokens, width), BF)
    anywhere = pl.BlockSpec(memory_space=pl.ANY)
    chunks = tokens // 256
    return call(
        functools.partial(hidden_body, (rows_each, groups)),
        (folds,),
        [
            smem,
            fixed,
            pl.BlockSpec((width, width), lambda j: (0, 2 * folds), **single),
            fixed,
            anywhere,
            pl.BlockSpec((width // folds, units), lambda j: (j, 0)),
            pl.BlockSpec((width, width), lambda j: (0, folds + j)),
            pl.BlockSpec((16, width), lambda j: (0, 0)),
            row,
        ],
        [by_rows, by_rows, by_cols, by_cols, pl.BlockSpec((width // folds, LANES), lambda j: (j, 0)), anywhere, anywhere, anywhere,
         pl.BlockSpec((8, width), lambda j: (0, 0))],
        [shape((blocks, size, units), BF)] * 4
        + [
            shape((width, LANES), F32),
            shape((tokens, width), BF),
            shape((tokens, width), F32),
            shape((tokens, width), BF),
            shape((8, width), F32),
        ],
        [
            pltpu.VMEM((tokens, width), F32),
            square,
            pltpu.VMEM((tokens, width), F32),
            pltpu.VMEM((tokens, width), F32),
            pltpu.VMEM((width, tokens), BF),
            square,
            square,
            pltpu.VMEM((width, width), BF),
            square,
            pltpu.SemaphoreType.DMA((1 + 3 * chunks,)),
        ],
        12 * tokens * width * units,
        "hidden",
    )(core, att, weights, patches, og, weights, weights, vectors, b_up)


def mix_back_body(core, gy, att, w_out, go, mine, other):
    go[...] = nt(gy[...], w_out[...]).astype(BF)
    grads = tn(att[...], gy[...]).astype(BF)
    blocks, size, _ = mine.shape

    def emit(refs):
        for n in range(2 * blocks):
            refs[n % 2][n // 2, :, :] = grads[n * size : n * size + size, :]

    @pl.when(core[0] == 0)
    def _():
        emit((mine, other))

    @pl.when(core[0] == 1)
    def _():
        emit((other, mine))


def mix_back(core, gy, att, weights, size):
    tokens, width = gy.shape
    last = weights.shape[1] // width - 1
    blocks = width // (2 * size)
    whole = pl.BlockSpec((tokens, width), lambda j: (0, 0))
    grads = pl.BlockSpec((blocks, size, width), lambda j: (0, 0, 0))
    return call(
        mix_back_body,
        (1,),
        [
            pl.BlockSpec(memory_space=pltpu.SMEM),
            whole,
            whole,
            pl.BlockSpec((width, width), lambda j: (0, last)),
        ],
        [whole, grads, grads],
        [shape((tokens, width), BF)] + [shape((blocks, size, width), BF)] * 2,
        [],
        4 * tokens * width * width,
        "mix_back",
    )(core, gy, att, weights)


def merge_body(count, *refs):
    out = refs[2 * count]
    at = 0
    for n in range(count):
        size = refs[n].shape[2]
        total = refs[n][...].astype(F32) + refs[count + n][...].astype(F32)
        out[:, :, at : at + size] = total.astype(BF)
        at += size


def merge(mine, received):
    blocks, size, _ = mine[0].shape
    widths = [m.shape[2] for m in mine]
    many = 2
    specs = [pl.BlockSpec((many, size, w), lambda j: (j, 0, 0)) for w in widths]
    return call(
        functools.partial(merge_body, len(mine)),
        (blocks // many,),
        specs + specs,
        [pl.BlockSpec((many, size, sum(widths)), lambda j: (j, 0, 0))],
        [shape((blocks, size, sum(widths)), BF)],
        [],
        2 * blocks * size * sum(widths),
        "merge",
        20 << 20,
    )(*mine, *received)[0]


def project_grad_body(core, turned, grads, weights, vectors, sums_att, sums_two, sum_up, mine,
                      other, mine_columns, other_columns, gain_sum, bias_sum):
    result = nn(turned[...], grads[...])
    blocks, size, _ = mine.shape
    width = turned.shape[0]
    step = pl.program_id(0)
    wide = (width, LANES)
    current = weights[...].astype(F32)
    new_gain = jnp.broadcast_to(jnp.sum(result * current, axis=1, keepdims=True), wide)
    grad_sum = column_sum(grads[...].astype(F32))
    new_bias = jnp.broadcast_to(jnp.sum(current * grad_sum, axis=1, keepdims=True), wide)
    rounded = result.astype(BF)

    def emit(values, refs):
        for n in range(2 * blocks):
            refs[n % 2][n // 2, :, :] = values[n * size : n * size + size, :]

    def by_core(values, first, second):
        @pl.when(core[0] == 0)
        def _():
            emit(values, (first, second))

        @pl.when(core[0] == 1)
        def _():
            emit(values, (second, first))

    by_core(rounded, mine, other)

    @pl.when(step == 0)
    def _():
        gain_sum[...] = new_gain
        bias_sum[...] = new_bias

    @pl.when(step > 0)
    def _():
        gain_sum[...] += new_gain
        bias_sum[...] += new_bias

    @pl.when(step == pl.num_programs(0) - 1)
    def _():
        lane = lax.broadcasted_iota(jnp.int32, wide, 1)
        pair = vectors[...].astype(F32)
        gain = jnp.sum(jnp.where(lane == 0, pair, 0.0), axis=1, keepdims=True)
        bias = jnp.sum(jnp.where(lane == 1, pair, 0.0), axis=1, keepdims=True)
        gain_grad = (gain_sum[...] - bias * bias_sum[...]) / gain
        used = [jnp.zeros((2, width), F32), sums_att[:5, :], sums_two[:4, :]]
        zeros = jnp.zeros((LANES - UP_LANE, width), F32)
        columns = jnp.concatenate([*used, zeros], axis=0).T + sum_up[...]
        columns = jnp.where(lane == 0, gain_grad, jnp.where(lane == 1, bias_sum[...], columns))
        by_core(columns.astype(BF), mine_columns, other_columns)


def project_grad(core, turned, grads, weights, sums_att, sums_two, sum_up, size):
    width, tokens = turned.shape
    blocks = width // (2 * size)
    out = pl.BlockSpec((blocks, size, width), lambda j: (0, 0, j))
    columns = pl.BlockSpec((blocks, size, LANES), lambda j: (0, 0, 0))
    eight = pl.BlockSpec((8, width), lambda j: (0, 0))
    last = 3 * width // LANES
    return call(
        project_grad_body,
        (3,),
        [
            pl.BlockSpec(memory_space=pltpu.SMEM),
            pl.BlockSpec((width, tokens), lambda j: (0, 0)),
            pl.BlockSpec((tokens, width), lambda j: (0, j)),
            pl.BlockSpec((width, width), lambda j: (0, j)),
            pl.BlockSpec((width, LANES), lambda j: (0, last)),
            eight,
            eight,
            pl.BlockSpec((width, LANES), lambda j: (0, 0)),
        ],
        [out, out, columns, columns],
        [shape((blocks, size, 3 * width), BF)] * 2 + [shape((blocks, size, LANES), BF)] * 2,
        [pltpu.VMEM((width, LANES), F32)] * 2,
        6 * tokens * width * width,
        "project_grad",
    )(core, turned, grads, weights, weights, sums_att, sums_two, sum_up)


def project_back_body(grads, weights, x, gx2, vectors, out):
    incoming = nt(grads[...], weights[...])
    hat, scale = normed(x[...].astype(F32))
    out[...] = gx2[...] + norm_back(hat, scale, incoming * row_of(vectors, GAIN_ONE))


def project_back(grads, weights, x, gx2, vectors):
    tokens, width = x.shape
    step = 256
    block = pl.BlockSpec((step, width), lambda t: (t, 0))
    return call(
        project_back_body,
        (tokens // step,),
        [
            pl.BlockSpec((step, 3 * width), lambda t: (t, 0)),
            pl.BlockSpec((width, 3 * width), lambda t: (0, 0)),
            block,
            block,
            pl.BlockSpec((8, width), lambda t: (0, 0)),
        ],
        [block],
        [shape((tokens, width), F32)],
        [],
        6 * tokens * width * width,
        "project_back",
    )(grads, weights, x, gx2, vectors)[0]


def chips_one_body(sizes, count, here, *refs):
    side, front, cut = sizes
    mine, received, outs = refs[:count], refs[count : 2 * count], refs[2 * count :]
    size = mine[0].shape[1]
    at = 0
    for m, r in zip(mine, received):
        cols = slice(at, at + m.shape[2])
        at += m.shape[2]
        for d in range(side):
            for b in range(front):
                n = lax.rem(here[0] + d, side) * front + b
                total = m[n, :cut, :].astype(F32) + r[n, :cut, :].astype(F32)
                outs[d][b, :, cols] = total.astype(BF)
        for d in range(front):
            for a in range(side):
                n = a * front + lax.rem(here[1] + d, front)
                total = m[n, cut:size, :].astype(F32) + r[n, cut:size, :].astype(F32)
                outs[side + d][a, :, cols] = total.astype(BF)


def chips_two_body(sizes, here, *refs):
    side, front, _ = sizes
    first, second, outs = refs[:side], refs[side : side + front], refs[side + front :]
    for parts, limit, coordinate, to in (
        (first, front, here[1], outs[:front]),
        (second, side, here[0], outs[front:]),
    ):
        for d in range(limit):
            n = lax.rem(coordinate + d, limit)
            to[d][...] = sum(p[n].astype(F32) for p in parts).astype(BF)


def chips_three_body(sizes, depth, here, *refs):
    side, front, cut = sizes
    first, second = refs[:front], refs[front : front + side]
    outs, kept = refs[front + side : -1], refs[-1]
    rows = kept.shape[1]
    for parts, begin_at in ((first, 0), (second, cut)):
        total = sum(p[...].astype(F32) for p in parts)
        for n in range(total.shape[0] // rows):
            kept[begin_at // rows + n] = total[n * rows : n * rows + rows, :].astype(BF)
    for d in range(depth):
        outs[d][...] = kept[lax.rem(here[3] + d, depth)]


def small_call(body, here, args, out_shape, scratch, name):
    whole = pl.BlockSpec(memory_space=pltpu.VMEM)
    moved = sum(math.prod(o.shape) * o.dtype.itemsize for o in [*args, *out_shape])
    return pl.pallas_call(
        body,
        in_specs=[pl.BlockSpec(memory_space=pltpu.SMEM)] + [whole] * len(args),
        out_specs=[whole] * len(out_shape),
        out_shape=out_shape,
        scratch_shapes=scratch,
        compiler_params=pltpu.CompilerParams(vmem_limit_bytes=24 << 20),
        cost_estimate=pl.CostEstimate(flops=moved, bytes_accessed=moved, transcendentals=0),
        name=name,
    )(here, *args)


def chips_one(here, mine, received, sizes):
    side, front, cut = sizes
    size, cols = mine[0].shape[1], sum(m.shape[2] for m in mine)
    outs = [shape((front, cut, cols), BF)] * side + [shape((side, size - cut, cols), BF)] * front
    body = functools.partial(chips_one_body, sizes, len(mine))
    done = small_call(body, here, [*mine, *received], outs, [], "chips_one")
    return done[:side], done[side:]


def chips_two(here, first, second, sizes):
    side, front, _ = sizes
    outs = [shape(first[0].shape[1:], BF)] * front + [shape(second[0].shape[1:], BF)] * side
    body = functools.partial(chips_two_body, sizes)
    done = small_call(body, here, [*first, *second], outs, [], "chips_two")
    return done[:front], done[front:]


def chips_three(here, first, second, sizes, depth):
    cols = first[0].shape[1]
    rows = (first[0].shape[0] + second[0].shape[0]) // depth
    body = functools.partial(chips_three_body, sizes, depth)
    scratch = [pltpu.VMEM((depth, rows, cols), BF)]
    outs = [shape((rows, cols), BF)] * depth
    return small_call(body, here, [*first, *second], outs, scratch, "chips_three")


def pack_first_body(qkv, vectors, packed, square):
    rows, third = qkv.shape[0], qkv.shape[1] // 3
    size = 256
    at = 0
    for group in range(third // size):
        for part in range(3):
            source = part * third + group * size
            packed[:, at : at + size] = qkv[:, source : source + size]
            at += size
    square[...] = jnp.zeros_like(square)
    square[: vectors.shape[0], : vectors.shape[1]] = vectors[...].astype(F32)
    packed[:, at:] = square[...].T[:rows, :].astype(BF)


def pack_first(qkv, vectors):
    rows, cols = qkv.shape
    whole = pl.BlockSpec(memory_space=pltpu.VMEM)
    return pl.pallas_call(
        pack_first_body,
        in_specs=[whole] * 2,
        out_specs=whole,
        out_shape=shape((rows, cols + LANES), BF),
        scratch_shapes=[pltpu.VMEM((LANES, LANES), F32)],
        name="pack_first",
    )(qkv, vectors)


def pack_rest_body(down, up, out, packed):
    rows, units = up.shape
    width = down.shape[1]
    for n in range(units // width):
        packed[:, n * width : n * width + width] = down[n * rows : n * rows + rows, :]
    packed[:, units : 2 * units] = up[...]
    packed[:, 2 * units :] = out[...]


def pack_rest(down, up, out):
    rows, units = up.shape
    whole = pl.BlockSpec(memory_space=pltpu.VMEM)
    return pl.pallas_call(
        pack_rest_body,
        in_specs=[whole] * 3,
        out_specs=whole,
        out_shape=shape((rows, 2 * units + out.shape[1]), BF),
        name="pack_rest",
    )(down, up, out)


AXES = ("side", "front", "core", "fsdp")


def split_mesh(mesh):
    outer, inner = mesh.shape["dp"], mesh.shape["fsdp"]
    cores = 2 if outer % 2 == 0 else 1
    side = math.isqrt(outer // cores)
    while (outer // cores) % side:
        side -= 1
    sizes = (side, outer // cores // side, cores, inner)
    return Mesh(mesh.devices.reshape(sizes), AXES)


def shifted(values, axis, distance):
    size = lax.axis_size(axis)
    return lax.ppermute(values, axis, [(i, (i + distance) % size) for i in range(size)])


def direct(values, axis):
    return [values] + [shifted(values, axis, d) for d in range(1, lax.axis_size(axis))]


def joined(parts):
    return parts[0] if len(parts) == 1 else jnp.concatenate(parts, axis=0)


def place_body(offsets, with_vectors, owners, *refs):
    count = len(offsets)
    parts, out, rest = refs[:count], refs[count], refs[count + 1 :]
    sems, rows = rest[-1], out.shape[1]
    copies = []
    for part, offset in zip(parts, offsets):
        for n in range(part.shape[0]):
            at = len(copies)
            target = out.at[owners[at], :, offset : offset + part.shape[2]]
            copies.append(pltpu.make_async_copy(part.at[n], target, sems.at[at]))
    for copy in copies:
        copy.start()
    for copy in copies:
        copy.wait()
    if with_vectors:
        vectors, columns = rest[:2]
        for n in range(out.shape[0]):
            columns[n * rows : n * rows + rows, :] = out[n, :, out.shape[2] - LANES :]
        vectors[...] = columns[...].astype(F32).T


def place(parts, offsets, owners, total, cols, with_vectors=False):
    rows = parts[0].shape[1]
    whole = pl.BlockSpec(memory_space=pltpu.VMEM)
    copies = sum(p.shape[0] for p in parts)
    out_shape = [shape((total, rows, cols), BF)]
    scratch = [pltpu.SemaphoreType.DMA((copies,))]
    if with_vectors:
        out_shape.append(shape((LANES, total * rows), F32))
        scratch = [pltpu.VMEM((total * rows, LANES), BF)] + scratch
    moved = 2 * total * rows * cols
    done = pl.pallas_call(
        functools.partial(place_body, tuple(offsets), with_vectors),
        in_specs=[pl.BlockSpec(memory_space=pltpu.SMEM)]
        + [pl.BlockSpec(memory_space=pl.ANY)] * len(parts),
        out_specs=[whole] * len(out_shape),
        out_shape=out_shape,
        scratch_shapes=scratch,
        compiler_params=pltpu.CompilerParams(vmem_limit_bytes=VMEM_LIMIT),
        cost_estimate=pl.CostEstimate(flops=0, bytes_accessed=2 * moved, transcendentals=0),
        name="place",
    )(owners, *parts)
    return done[0].reshape(total * rows, cols), done[1:]


def orders():
    depth = lax.axis_size("fsdp")
    cut = max(1, depth // 2)
    return [part for part in ((0, cut, (0, 1)), (cut, depth, (1, 0))) if part[0] < part[1]]


def begin(shard):
    line = direct(shard[None], "fsdp")
    return [joined(line[low:high]) for low, high, _ in orders()]


def across(blocks, stage):
    return [joined(direct(b, AXES[o[2][stage]])) for b, o in zip(blocks, orders())]


def over(blocks):
    return [part for b in blocks for part in direct(b, "core")]


def owners_of(steps):
    sizes = [lax.axis_size(a) for a in AXES]
    here = [lax.axis_index(a) for a in AXES]
    table = jnp.asarray(steps, jnp.int32)
    owner = jnp.zeros((len(steps),), jnp.int32)
    for n, size in enumerate(sizes):
        owner = owner * size + lax.rem(here[n] - table[:, n] + size, size)
    return owner


def owner_table():
    sizes = [lax.axis_size(a) for a in AXES]
    steps = []
    for low, high, order in orders():
        for c in range(sizes[2]):
            for second in range(sizes[order[1]]):
                for first in range(sizes[order[0]]):
                    moved = {order[0]: first, order[1]: second}
                    steps += [(moved[0], moved[1], c, z) for z in range(low, high)]
    return owners_of(steps)


def exchanged(parts, axis):
    return [parts[0]] + [shifted(p, axis, d) for d, p in enumerate(parts) if d > 0]


def regrouped(values, outer, inner):
    rows, cols = values.shape
    size = cols // (outer * inner)
    return values.reshape(rows, outer, inner, size).transpose(0, 2, 1, 3).reshape(rows, cols)


def on_device(patches, picture_ids, norm1_gain, norm1_bias, qkv_weight, query_shift, value_shift,
              query_gain, query_bias, key_gain, out_weight, out_bias, norm2_gain, norm2_bias,
              up_weight, up_bias, down_weight, down_bias, out_grad):
    width = patches.shape[1]
    rows = qkv_weight.shape[0]
    units = up_weight.shape[1]
    folds = units // width
    groups = width // 256
    side, front, cores, depth = (lax.axis_size(a) for a in AXES)
    total = side * front * cores * depth
    vectors_here = [norm1_gain, norm1_bias, query_shift, value_shift, query_gain, query_bias,
                    key_gain, out_bias, norm2_gain, norm2_bias, down_bias, up_bias]
    count = sum(v.shape[0] for v in vectors_here)
    small, at = 0.0, 0
    for v in vectors_here:
        small += jnp.pad(v.astype(F32), (at, count - at - v.shape[0]))
        at += v.shape[0]
    small = small.reshape(-1, rows)
    here = jnp.stack([lax.axis_index(a) for a in AXES]).astype(jnp.int32)
    core = here[2:3]

    second = lax.all_gather(
        pack_rest(down_weight, up_weight, out_weight), AXES, axis=0, tiled=True
    )
    one = begin(pack_first(qkv_weight, small))
    extras = (*picture_lanes(picture_ids), owner_table())
    one, extras = lax.optimization_barrier((one, extras))
    extra_q, extra_k, padding, owners = extras
    one = over(across(across(one, 0), 1))
    offsets = [0] * len(one)
    first, (vectors,) = place(one, offsets, owners, total, 3 * width + LANES, with_vectors=True)
    b_up = vectors[UP_LANE : UP_LANE + folds].reshape(folds, -1, rows).transpose(1, 0, 2)
    b_up = b_up.reshape(1, -1)

    turned, q, k, v, q_hat, k_hat, q_scale, k_scale = project(patches, first, vectors)
    att, extra_back = attend(q, k, v, extra_q, extra_k, padding)
    (mine_down, other_down, mine_up, other_up, up_sum, mixed, gx2, gy, sums_two) = hidden(
        core, att, patches, out_grad, second, vectors, b_up, rows, depth
    )
    go, mine_out, other_out = mix_back(core, gy, att, second, depth * rows)
    received = [shifted(p, "core", 1) for p in (other_down, other_up, other_out)]
    merged = merge([mine_down, mine_up, mine_out], received)
    merged, go = lax.optimization_barrier((merged, go))
    flat = merged.reshape(-1, merged.shape[2])
    flat = lax.psum_scatter(flat, AXES[:2], scatter_dimension=0, tiled=True)
    grads, sums_att = attend_back(
        q, k, v, go, att, extra_back, extra_k, padding, q_hat, k_hat, q_scale, k_scale, vectors
    )
    sums_att = sums_att.reshape(-1, 8, width).sum(axis=0)
    mine_qkv, other_qkv, mine_columns, other_columns = project_grad(
        core, turned, grads, first, sums_att, sums_two, up_sum, depth * rows
    )
    received = [shifted(p, "core", 1) for p in (other_qkv, other_columns)]
    sizes = (side, front, depth // 2 * rows)
    last = chips_one(here, [mine_qkv, mine_columns], received, sizes)
    last, flat = lax.optimization_barrier((last, flat))
    wide_out = lax.psum_scatter(flat, AXES[3], scatter_dimension=0, tiled=True).astype(F32)
    last = exchanged(last[0], "side"), exchanged(last[1], "front")
    last = chips_two(here, *last, sizes)
    last = exchanged(last[0], "front"), exchanged(last[1], "side")
    last = chips_three(here, *last, sizes, depth)
    last, gx2 = lax.optimization_barrier((last, gx2))
    last = exchanged(last, "fsdp")
    patches_grad = project_back(grads, first, patches, gx2, vectors)
    last = sum(part.astype(F32) for part in last)
    qkv_out = regrouped(last[:, : 3 * width], groups, 3)
    final = last[:, 3 * width :].T
    (gain_one_out, bias_one_out, q_shift_out, v_shift_out, q_gain_out, q_bias_out, k_gain_out,
     gain_two_out, bias_two_out, out_bias_out, down_bias_out) = [final[n] for n in range(11)]
    down_out = wide_out[:, :units].reshape(rows, folds, width).transpose(1, 0, 2)
    return (
        mixed, patches_grad, gain_one_out, bias_one_out, qkv_out, q_shift_out, v_shift_out,
        q_gain_out, q_bias_out, k_gain_out, wide_out[:, 2 * units :], out_bias_out, gain_two_out,
        bias_two_out, wide_out[:, units : 2 * units], final[11 : 11 + folds].reshape(-1),
        down_out.reshape(rows * folds, width), down_bias_out,
    )


def solution(mesh):
    flat = P(AXES)
    wide = P(AXES, None)
    in_specs = (wide, flat, flat, flat, wide, flat, flat, flat, flat, flat, wide, flat, flat, flat,
                wide, flat, wide, flat, wide)
    out_specs = (wide, wide, flat, flat, wide, flat, flat, flat, flat, flat, wide, flat, flat, flat,
                 wide, flat, wide, flat)
    return jax.shard_map(
        on_device, mesh=split_mesh(mesh), in_specs=in_specs, out_specs=out_specs, check_vma=False
    )
```

```python
import functools
import math
import jax
import jax.numpy as jnp
from jax import lax
from jax.experimental import pallas as pl
from jax.experimental.pallas import tpu as pltpu
from jax.sharding import Mesh, PartitionSpec as P

HEADS = 12
HD = 64
ROW = 1024
EPSILON = 1e-06
BF = jnp.bfloat16
F32 = jnp.float32
EXP_SCALE = HD**-0.5 * math.log2(math.e)
VMEM_LIMIT = 56 << 20
LANES = 128
GAIN_ONE, BIAS_ONE, Q_SHIFT, V_SHIFT, Q_GAIN, Q_BIAS, K_GAIN = range(7)
B_OUT, GAIN_TWO, BIAS_TWO, B_DOWN = range(7, 11)


def nn(left, right):
    return jnp.dot(left, right, preferred_element_type=F32)


def nt(left, right):
    return lax.dot_general(left, right, (((1,), (1,)), ((), ())), preferred_element_type=F32)


def tn(left, right):
    return lax.dot_general(left, right, (((0,), (0,)), ((), ())), preferred_element_type=F32)


def call(body, grid, in_specs, out_specs, out_shape, scratch, flops, name, limit=VMEM_LIMIT):
    def run(*args):
        moved = sum(a.size * a.dtype.itemsize for a in args)
        moved += sum(math.prod(o.shape) * o.dtype.itemsize for o in out_shape)
        return pl.pallas_call(
            body,
            grid=grid,
            in_specs=in_specs,
            out_specs=out_specs,
            out_shape=out_shape,
            scratch_shapes=scratch,
            compiler_params=pltpu.CompilerParams(vmem_limit_bytes=limit),
            cost_estimate=pl.CostEstimate(flops=flops, bytes_accessed=moved, transcendentals=0),
            name=name,
        )(*args)

    return run


def row_of(vectors, n):
    return vectors[n : n + 1, :]


def shape(dims, kind):
    return jax.ShapeDtypeStruct(dims, kind)


def chunk_at(step, size):
    return pl.ds(pl.multiple_of(step * size, size), size)


def block_mean(size):
    rows_at = lax.broadcasted_iota(jnp.int32, (size, size), 0)
    cols_at = lax.broadcasted_iota(jnp.int32, (size, size), 1)
    return jnp.where(rows_at // HD == cols_at // HD, 1.0 / HD, 0.0).astype(BF)


def normed(values):
    average = jnp.mean(values, axis=-1, keepdims=True)
    centred = values - average
    variance = jnp.mean(centred * centred, axis=-1, keepdims=True)
    scale = lax.rsqrt(variance + EPSILON)
    return centred * scale, scale


def norm_back(hat, scale, grads):
    first = jnp.mean(grads, axis=-1, keepdims=True)
    second = jnp.mean(grads * hat, axis=-1, keepdims=True)
    return scale * (grads - first - hat * second)


def column_sum(values):
    return jnp.sum(values, axis=0, keepdims=True)


def project_body(x, whole_rows, weights, own_rows,
                 turned, q, k, v, q_hat, k_hat, q_scale, k_scale, a1):
    tokens = x.shape[0]
    step = 1024

    @pl.when(pl.program_id(0) == 0)
    def _():
        def first(t, carry):
            rows = chunk_at(t, 256)
            hat, scale = normed(x[rows, :].astype(F32))
            a1[rows, :] = (hat * row_of(whole_rows, GAIN_ONE) + row_of(whole_rows, BIAS_ONE)).astype(BF)
            return carry

        lax.fori_loop(0, tokens // 256, first, 0)
        turned[...] = a1[...].T

    cols = weights.shape[1] // 3
    means = block_mean(cols)

    def one(t, carry):
        rows = chunk_at(t, step)
        source = a1[rows, :]

        def head_norm(pre, out, hat_out, scale_out, gains, biases):
            high = pre.astype(BF)
            low = (pre - high.astype(F32)).astype(BF)
            centred = pre - (nn(high, means) + nn(low, means))
            variance = nn((centred * centred).astype(BF), means)
            scale = lax.rsqrt(variance + EPSILON)
            hat = centred * scale
            shifted = hat * gains
            out[rows, :] = (shifted if biases is None else shifted + biases).astype(BF)
            hat_out[rows, :] = hat.astype(BF)
            scale_out[rows, :] = scale.astype(BF)

        pre = nn(source, weights[:, :cols]) + row_of(own_rows, Q_SHIFT)
        head_norm(pre, q, q_hat, q_scale, row_of(own_rows, Q_GAIN), row_of(own_rows, Q_BIAS))
        pre = nn(source, weights[:, cols : 2 * cols])
        head_norm(pre, k, k_hat, k_scale, row_of(own_rows, K_GAIN), None)
        pre = nn(source, weights[:, 2 * cols :])
        v[rows, :] = (pre + row_of(own_rows, V_SHIFT)).astype(BF)
        return carry

    lax.fori_loop(0, tokens // step, one, 0)


def project(x, weights, vectors):
    tokens, width = x.shape
    cols = 256
    parts = width // cols
    whole = pl.BlockSpec((tokens, width), lambda j: (0, 0))
    out = pl.BlockSpec((tokens, cols), lambda j: (0, j))
    return call(
        project_body,
        (parts,),
        [
            whole,
            pl.BlockSpec((8, width), lambda j: (0, 0)),
            pl.BlockSpec((width, 3 * cols), lambda j: (0, j)),
            pl.BlockSpec((8, cols), lambda j: (0, j)),
        ],
        [pl.BlockSpec((width, tokens), lambda j: (0, 0))] + [out] * 7,
        [shape((width, tokens), BF)] + [shape((tokens, width), BF)] * 7,
        [pltpu.VMEM((tokens, width), BF)],
        6 * tokens * width * width,
        "project",
    )(x, vectors, weights, vectors)


def half(values, head):
    lane = lax.broadcasted_iota(jnp.int32, values.shape, 1)
    return jnp.where((lane < HD) if head == 0 else (lane >= HD), values, jnp.zeros_like(values))


def three_parts(values, lane):
    high = values.astype(BF).astype(F32)
    rest = values - high
    middle = rest.astype(BF).astype(F32)
    low = rest - middle
    return jnp.where(
        lane == 12, high, jnp.where(lane == 13, middle, jnp.where(lane == 14, low, 0.0))
    )


def picture_lanes(pic_ids):
    lane = lax.broadcasted_iota(jnp.int32, (pic_ids.shape[0], LANES), 1)
    same = (pic_ids[:, None] == lane + 1) & (lane < 10)
    for_q = jnp.where(same | (lane == 10), 32.0, 0.0).astype(BF)
    ones = jnp.where((lane >= 12) & (lane < 15), 1.0, 0.0)
    for_k = jnp.where(same, 64.0, jnp.where(lane == 10, -64.0, ones)).astype(BF)
    padding = jnp.broadcast_to((pic_ids == 0)[:, None], lane.shape).astype(F32)
    return for_q, for_k, padding


def attend_body(q, k, v, extra_q, extra_k, padding, att, extra_back):
    lane = lax.broadcasted_iota(jnp.int32, (ROW, LANES), 1)
    queries = jnp.concatenate([q[...], extra_q[...]], axis=1)
    results, totals = [], []
    for h in (0, 1):
        keys = jnp.concatenate([half(k[...], h), extra_k[...]], axis=1)
        powers = jnp.exp2(nt(keys, queries) * EXP_SCALE).astype(BF)
        mine = (lane < HD) if h == 0 else (lane >= HD)
        out = tn(jnp.where(mine, v[...], jnp.ones_like(v[...])), powers)
        low, high = out[:HD, :], out[HD:, :]
        results.append(low if h == 0 else high)
        totals.append(high if h == 0 else low)
    result = jnp.concatenate(results, axis=0).T
    pad = padding[...]
    total = jnp.concatenate(totals, axis=0).T + pad
    att[...] = ((result + pad * v[...].astype(F32)) / total).astype(BF)
    row_term = jnp.log(total) * -(HD**0.5)
    other = pltpu.roll(row_term, HD, 1)
    base = extra_q[...].astype(F32)
    for h in (0, 1):
        mine = row_term if h == 0 else other
        extra_back[h] = (base + three_parts(mine, lane)).astype(BF)


def attend(q, k, v, extra_q, extra_k, padding):
    tokens, width = q.shape
    pairs = width // LANES
    block = pl.BlockSpec((ROW, LANES), lambda r, p: (r, p))
    fixed = pl.BlockSpec((ROW, LANES), lambda r, p: (r, 0))
    return call(
        attend_body,
        (tokens // ROW, pairs),
        [block] * 3 + [fixed] * 3,
        [block, pl.BlockSpec((2, ROW, LANES), lambda r, p: (p, r, 0))],
        [shape((tokens, width), BF), shape((2 * pairs, tokens, LANES), BF)],
        [],
        16 * tokens * ROW * width,
        "attend",
    )(q, k, v, extra_q, extra_k, padding)


def attend_back_body(q, k, v, go, att, extra_q, extra_k, padding, q_hat, k_hat, q_scale, k_scale,
                     vectors, packed, sums):
    offset = lax.rem(pl.program_id(1), 2) * LANES
    q_at, k_at, v_at = [pl.ds(pl.multiple_of(offset + n, LANES), LANES) for n in (0, 256, 512)]
    lane = lax.broadcasted_iota(jnp.int32, (ROW, LANES), 1)
    rows_at = lax.broadcasted_iota(jnp.int32, (LANES, LANES), 0)
    cols_at = lax.broadcasted_iota(jnp.int32, (LANES, LANES), 1)
    terms = go[...].astype(F32) * att[...].astype(F32)
    high = terms.astype(BF)
    low = (terms - high.astype(F32)).astype(BF)
    v_extra = jnp.where((lane >= 12) & (lane < 15), 1.0, 0.0).astype(BF)
    q_half, k_half, go_half, probs_all, grads_all = [], [], [], [], []
    for h in (0, 1):
        mine = (rows_at < HD) if h == 0 else (rows_at >= HD)
        pick = jnp.where(mine & (cols_at >= 12) & (cols_at < 15), 1.0, 0.0).astype(BF)
        delta = nn(high, pick) + nn(low, pick)
        go_extra = jnp.concatenate([go[...], three_parts(-delta, lane).astype(BF)], axis=1)
        key = half(k[...], h)
        scores = nt(
            jnp.concatenate([q[...], extra_q[h]], axis=1),
            jnp.concatenate([key, extra_k[...]], axis=1),
        )
        pulled = nt(go_extra, jnp.concatenate([half(v[...], h), v_extra], axis=1))
        probs = jnp.exp2(scores * EXP_SCALE)
        q_half.append(half(q[...], h))
        k_half.append(key)
        go_half.append(half(go[...], h))
        probs_all.append(probs.astype(BF))
        grads_all.append((probs * pulled).astype(BF))
    grad_v = tn(jnp.concatenate(go_half, axis=0), jnp.concatenate(probs_all, axis=0)).T
    grad_k = tn(jnp.concatenate(q_half, axis=0), jnp.concatenate(grads_all, axis=0)).T * HD**-0.5
    keys_turned = jnp.concatenate([part.T for part in k_half], axis=1)
    grad_q = nt(keys_turned, jnp.concatenate(grads_all, axis=1)).T * HD**-0.5
    means = block_mean(LANES)

    def head_norm_back(incoming, hat, scale, gains):
        inner = incoming * gains
        first = nn(inner.astype(BF), means)
        second = nn((inner * hat).astype(BF), means)
        return (scale * (inner - first - hat * second)).astype(BF)

    out_v = (grad_v + padding[...] * go[...].astype(F32)).astype(BF)
    packed[:, v_at] = out_v
    hat = k_hat[...].astype(F32)
    packed[:, k_at] = head_norm_back(grad_k, hat, k_scale[...].astype(F32), row_of(vectors, K_GAIN))
    k_sum = column_sum(grad_k * hat)
    hat = q_hat[...].astype(F32)
    out_q = head_norm_back(grad_q, hat, q_scale[...].astype(F32), row_of(vectors, Q_GAIN))
    packed[:, q_at] = out_q
    parts = [out_q.astype(F32), out_v.astype(F32), grad_q * hat, grad_q]
    zero = jnp.zeros((3, LANES), F32)
    sums[...] = jnp.concatenate([*map(column_sum, parts), k_sum, zero], axis=0)


def attend_back(q, k, v, go, att, extra_q, extra_k, padding, q_hat, k_hat, q_scale, k_scale,
                vectors):
    tokens, width = q.shape
    count = tokens // ROW
    block = pl.BlockSpec((ROW, LANES), lambda r, p: (r, p))
    fixed = pl.BlockSpec((ROW, LANES), lambda r, p: (r, 0))
    eight = pl.BlockSpec((8, LANES), lambda r, p: (0, p))
    return call(
        attend_back_body,
        (count, width // LANES),
        [block] * 5
        + [pl.BlockSpec((2, ROW, LANES), lambda r, p: (p, r, 0)), fixed, fixed]
        + [block] * 4
        + [eight],
        [
            pl.BlockSpec((ROW, 6 * LANES), lambda r, p: (r, p // 2)),
            pl.BlockSpec((8, LANES), lambda r, p: (r, p)),
        ],
        [shape((tokens, 3 * width), BF), shape((8 * count, width), F32)],
        [],
        40 * tokens * ROW * width,
        "attend_back",
    )(q, k, v, go, att, extra_q, extra_k, padding, q_hat, k_hat, q_scale, k_scale, vectors)


SLOPE = math.sqrt(2.0 / math.pi)
CUBE = 0.044715


def gelu_pair(values):
    square = values * values
    share = 0.5 + 0.5 * jnp.tanh(values * (SLOPE + (SLOPE * CUBE) * square))
    gelu = values * share
    return gelu, share + gelu * (1.0 - share) * (2 * SLOPE + (6 * SLOPE * CUBE) * square)


UP_LANE = 11


def hidden_body(counts, core, *refs):
    (att, w_out, patches, og_out, folded, up, vectors, b_up, mine_down, other_down, mine_up,
     other_up, sum_up, mixed, gx2, gy, sums, x2, a2, y, ga, turned, act, grad, down, og,
     flat_down, flat_up, held_gy, sems) = refs
    held_mixed = a2
    rows_each, groups = counts
    tokens, width = a2.shape
    folds = folded.shape[1] // width
    each = folded.shape[0] // rows_each
    step = pl.program_id(0)

    @pl.when(step == 0)
    def _():
        fetch = pltpu.make_async_copy(og_out, og, sems.at[0])
        fetch.start()
        y[...] = jnp.zeros_like(y)
        ga[...] = jnp.zeros_like(ga)

        def mix(t, carry):
            rows = chunk_at(t, 1024)
            middle = patches[rows, :].astype(F32) + (nn(att[rows, :], w_out[...]) + row_of(vectors, B_OUT))
            x2[rows, :] = middle
            scaled = normed(middle)[0] * row_of(vectors, GAIN_TWO)
            a2[rows, :] = (scaled + row_of(vectors, BIAS_TWO)).astype(BF)
            return carry

        lax.fori_loop(0, tokens // 1024, mix, 0)
        turned[...] = a2[...].T
        fetch.wait()

    for o in range(each):
        for w in range(folds):
            at = (o * folds + w) * rows_each
            source = folded[o * rows_each : o * rows_each + rows_each, w * width : w * width + width]
            down[at : at + rows_each, :] = source

    value, slope = gelu_pair(nn(a2[...], up[...]) + b_up[...])
    act[...] = value.astype(BF)
    y[...] += nn(act[...], down[...])
    pulled = nt(og[...], down[...]) * slope
    grad[...] = pulled.astype(BF)
    ga[...] += nt(grad[...], up[...])
    summed = jnp.broadcast_to(column_sum(grad[...].astype(F32)), (LANES, width)).T
    lane = lax.broadcasted_iota(jnp.int32, (rows_each, LANES), 1)
    for o in range(each):
        columns = jnp.zeros((rows_each, LANES), F32)
        for w in range(folds):
            at = (o * folds + w) * rows_each
            columns = jnp.where(lane == UP_LANE + w, summed[at : at + rows_each, :], columns)
        sum_up[o * rows_each : o * rows_each + rows_each, :] = columns

    def weight_grads():
        flat_down[...] = tn(act[...], og[...]).astype(BF)
        flat_up[...] = nn(turned[...], grad[...]).astype(BF)

    def end():
        carry = (jnp.zeros((1, width), F32),) * 4
        for t in range(tokens // 256):
            rows = slice(t * 256, t * 256 + 256)
            middle = x2[rows, :]
            outer = og[rows, :].astype(F32)
            held_mixed[rows, :] = (middle + (y[rows, :] + row_of(vectors, B_DOWN))).astype(BF)
            hat, scale = normed(middle)
            incoming = ga[rows, :]
            total = outer + norm_back(hat, scale, incoming * row_of(vectors, GAIN_TWO))
            ga[rows, :] = total
            rounded = total.astype(BF)
            held_gy[rows, :] = rounded
            for copy in sends(t):
                copy.start()
            new = (incoming * hat, incoming, rounded.astype(F32), outer)
            carry = tuple(old + column_sum(n) for old, n in zip(carry, new))
        sums[...] = jnp.concatenate([*carry, jnp.zeros((4, width), F32)], axis=0)

    def sends(t):
        rows = slice(t * 256, t * 256 + 256)
        return [
            pltpu.make_async_copy(source.at[rows], target.at[rows], sems.at[1 + 3 * t + n])
            for n, (source, target) in enumerate(
                ((held_mixed, mixed), (ga, gx2), (held_gy, gy))
            )
        ]

    last_step = pl.num_programs(0) - 1

    @pl.when(step < last_step)
    def _():
        weight_grads()

    @pl.when(step == last_step)
    def _():
        weight_grads()
        end()

    def emit(down_refs, up_refs):
        for o in range(each):
            block, inner = divmod(o, 2 * groups)
            c, z = divmod(inner, groups)
            rows = slice(z * rows_each, z * rows_each + rows_each)
            for w in range(folds):
                at = (o * folds + w) * rows_each
                down_refs[c][block, rows, w * width : w * width + width] = flat_down[
                    at : at + rows_each, :
                ]
        size = groups * rows_each
        for block in range(width // (2 * size)):
            for c in (0, 1):
                at = (2 * block + c) * size
                up_refs[c][block, :, :] = flat_up[at : at + size, :]

    @pl.when(core[0] == 0)
    def _():
        emit((mine_down, other_down), (mine_up, other_up))

    @pl.when(core[0] == 1)
    def _():
        emit((other_down, mine_down), (other_up, mine_up))

    @pl.when(step == last_step)
    def _():
        for t in range(tokens // 256):
            for copy in sends(t):
                copy.wait()


def hidden(core, att, patches, og, weights, vectors, b_up, rows_each, groups):
    tokens, width = patches.shape
    units = (weights.shape[1] - width) // 2
    folds = units // width
    blocks = width // (2 * groups * rows_each)
    each = blocks // folds
    size = groups * rows_each
    smem = pl.BlockSpec(memory_space=pltpu.SMEM)
    single = dict(pipeline_mode=pl.Buffered(1))
    fixed = pl.BlockSpec((tokens, width), lambda j: (0, 0), **single)
    row = pl.BlockSpec((1, width), lambda j: (0, j))
    by_rows = pl.BlockSpec((each, size, units), lambda j: (j, 0, 0))
    by_cols = pl.BlockSpec((blocks, size, width), lambda j: (0, 0, j))
    square = pltpu.VMEM((tokens, width), BF)
    anywhere = pl.BlockSpec(memory_space=pl.ANY)
    chunks = tokens // 256
    return call(
        functools.partial(hidden_body, (rows_each, groups)),
        (folds,),
        [
            smem,
            fixed,
            pl.BlockSpec((width, width), lambda j: (0, 2 * folds), **single),
            fixed,
            anywhere,
            pl.BlockSpec((width // folds, units), lambda j: (j, 0)),
            pl.BlockSpec((width, width), lambda j: (0, folds + j)),
            pl.BlockSpec((16, width), lambda j: (0, 0)),
            row,
        ],
        [by_rows, by_rows, by_cols, by_cols, pl.BlockSpec((width // folds, LANES), lambda j: (j, 0)), anywhere, anywhere, anywhere,
         pl.BlockSpec((8, width), lambda j: (0, 0))],
        [shape((blocks, size, units), BF)] * 4
        + [
            shape((width, LANES), F32),
            shape((tokens, width), BF),
            shape((tokens, width), F32),
            shape((tokens, width), BF),
            shape((8, width), F32),
        ],
        [
            pltpu.VMEM((tokens, width), F32),
            square,
            pltpu.VMEM((tokens, width), F32),
            pltpu.VMEM((tokens, width), F32),
            pltpu.VMEM((width, tokens), BF),
            square,
            square,
            pltpu.VMEM((width, width), BF),
            square,
            pltpu.VMEM((width, width), BF),
            pltpu.VMEM((width, width), BF),
            square,
            pltpu.SemaphoreType.DMA((1 + 3 * chunks,)),
        ],
        12 * tokens * width * units,
        "hidden",
    )(core, att, weights, patches, og, weights, weights, vectors, b_up)


def mix_back_body(core, gy, att, w_out, go, mine, other):
    go[...] = nt(gy[...], w_out[...]).astype(BF)
    grads = tn(att[...], gy[...]).astype(BF)
    blocks, size, _ = mine.shape

    def emit(refs):
        for n in range(2 * blocks):
            refs[n % 2][n // 2, :, :] = grads[n * size : n * size + size, :]

    @pl.when(core[0] == 0)
    def _():
        emit((mine, other))

    @pl.when(core[0] == 1)
    def _():
        emit((other, mine))


def mix_back(core, gy, att, weights, size):
    tokens, width = gy.shape
    last = weights.shape[1] // width - 1
    blocks = width // (2 * size)
    whole = pl.BlockSpec((tokens, width), lambda j: (0, 0))
    grads = pl.BlockSpec((blocks, size, width), lambda j: (0, 0, 0))
    return call(
        mix_back_body,
        (1,),
        [
            pl.BlockSpec(memory_space=pltpu.SMEM),
            whole,
            whole,
            pl.BlockSpec((width, width), lambda j: (0, last)),
        ],
        [whole, grads, grads],
        [shape((tokens, width), BF)] + [shape((blocks, size, width), BF)] * 2,
        [],
        4 * tokens * width * width,
        "mix_back",
    )(core, gy, att, weights)


def merge_body(count, *refs):
    out = refs[2 * count]
    at = 0
    for n in range(count):
        size = refs[n].shape[2]
        total = refs[n][...].astype(F32) + refs[count + n][...].astype(F32)
        out[:, :, at : at + size] = total.astype(BF)
        at += size


def merge(mine, received):
    blocks, size, _ = mine[0].shape
    widths = [m.shape[2] for m in mine]
    many = 2
    specs = [pl.BlockSpec((many, size, w), lambda j: (j, 0, 0)) for w in widths]
    return call(
        functools.partial(merge_body, len(mine)),
        (blocks // many,),
        specs + specs,
        [pl.BlockSpec((many, size, sum(widths)), lambda j: (j, 0, 0))],
        [shape((blocks, size, sum(widths)), BF)],
        [],
        2 * blocks * size * sum(widths),
        "merge",
        20 << 20,
    )(*mine, *received)[0]


def project_grad_body(core, turned, grads, weights, vectors, sums_att, sums_two, sum_up, mine,
                      other, mine_columns, other_columns, gain_sum, bias_sum):
    result = nn(turned[...], grads[...])
    blocks, size, _ = mine.shape
    width = turned.shape[0]
    step = pl.program_id(0)
    wide = (width, LANES)
    current = weights[...].astype(F32)
    new_gain = jnp.broadcast_to(jnp.sum(result * current, axis=1, keepdims=True), wide)
    grad_sum = column_sum(grads[...].astype(F32))
    new_bias = jnp.broadcast_to(jnp.sum(current * grad_sum, axis=1, keepdims=True), wide)
    rounded = result.astype(BF)

    def emit(values, refs):
        for n in range(2 * blocks):
            refs[n % 2][n // 2, :, :] = values[n * size : n * size + size, :]

    def by_core(values, first, second):
        @pl.when(core[0] == 0)
        def _():
            emit(values, (first, second))

        @pl.when(core[0] == 1)
        def _():
            emit(values, (second, first))

    by_core(rounded, mine, other)

    @pl.when(step == 0)
    def _():
        gain_sum[...] = new_gain
        bias_sum[...] = new_bias

    @pl.when(step > 0)
    def _():
        gain_sum[...] += new_gain
        bias_sum[...] += new_bias

    @pl.when(step == pl.num_programs(0) - 1)
    def _():
        lane = lax.broadcasted_iota(jnp.int32, wide, 1)
        pair = vectors[...].astype(F32)
        gain = jnp.sum(jnp.where(lane == 0, pair, 0.0), axis=1, keepdims=True)
        bias = jnp.sum(jnp.where(lane == 1, pair, 0.0), axis=1, keepdims=True)
        gain_grad = (gain_sum[...] - bias * bias_sum[...]) / gain
        used = [jnp.zeros((2, width), F32), sums_att[:5, :], sums_two[:4, :]]
        zeros = jnp.zeros((LANES - UP_LANE, width), F32)
        columns = jnp.concatenate([*used, zeros], axis=0).T + sum_up[...]
        columns = jnp.where(lane == 0, gain_grad, jnp.where(lane == 1, bias_sum[...], columns))
        by_core(columns.astype(BF), mine_columns, other_columns)


def project_grad(core, turned, grads, weights, sums_att, sums_two, sum_up, size):
    width, tokens = turned.shape
    blocks = width // (2 * size)
    out = pl.BlockSpec((blocks, size, width), lambda j: (0, 0, j))
    columns = pl.BlockSpec((blocks, size, LANES), lambda j: (0, 0, 0))
    eight = pl.BlockSpec((8, width), lambda j: (0, 0))
    last = 3 * width // LANES
    return call(
        project_grad_body,
        (3,),
        [
            pl.BlockSpec(memory_space=pltpu.SMEM),
            pl.BlockSpec((width, tokens), lambda j: (0, 0)),
            pl.BlockSpec((tokens, width), lambda j: (0, j)),
            pl.BlockSpec((width, width), lambda j: (0, j)),
            pl.BlockSpec((width, LANES), lambda j: (0, last)),
            eight,
            eight,
            pl.BlockSpec((width, LANES), lambda j: (0, 0)),
        ],
        [out, out, columns, columns],
        [shape((blocks, size, 3 * width), BF)] * 2 + [shape((blocks, size, LANES), BF)] * 2,
        [pltpu.VMEM((width, LANES), F32)] * 2,
        6 * tokens * width * width,
        "project_grad",
    )(core, turned, grads, weights, weights, sums_att, sums_two, sum_up)


def project_back_body(grads, weights, x, gx2, vectors, out):
    incoming = nt(grads[...], weights[...])
    hat, scale = normed(x[...].astype(F32))
    out[...] = gx2[...] + norm_back(hat, scale, incoming * row_of(vectors, GAIN_ONE))


def project_back(grads, weights, x, gx2, vectors):
    tokens, width = x.shape
    step = 256
    block = pl.BlockSpec((step, width), lambda t: (t, 0))
    return call(
        project_back_body,
        (tokens // step,),
        [
            pl.BlockSpec((step, 3 * width), lambda t: (t, 0)),
            pl.BlockSpec((width, 3 * width), lambda t: (0, 0)),
            block,
            block,
            pl.BlockSpec((8, width), lambda t: (0, 0)),
        ],
        [block],
        [shape((tokens, width), F32)],
        [],
        6 * tokens * width * width,
        "project_back",
    )(grads, weights, x, gx2, vectors)[0]


def chips_one_body(sizes, count, here, *refs):
    side, front, cut = sizes
    mine, received, outs = refs[:count], refs[count : 2 * count], refs[2 * count :]
    size = mine[0].shape[1]
    at = 0
    for m, r in zip(mine, received):
        cols = slice(at, at + m.shape[2])
        at += m.shape[2]
        for d in range(side):
            for b in range(front):
                n = lax.rem(here[0] + d, side) * front + b
                total = m[n, :cut, :].astype(F32) + r[n, :cut, :].astype(F32)
                outs[d][b, :, cols] = total.astype(BF)
        for d in range(front):
            for a in range(side):
                n = a * front + lax.rem(here[1] + d, front)
                total = m[n, cut:size, :].astype(F32) + r[n, cut:size, :].astype(F32)
                outs[side + d][a, :, cols] = total.astype(BF)


def chips_two_body(sizes, here, *refs):
    side, front, _ = sizes
    first, second, outs = refs[:side], refs[side : side + front], refs[side + front :]
    for parts, limit, coordinate, to in (
        (first, front, here[1], outs[:front]),
        (second, side, here[0], outs[front:]),
    ):
        for d in range(limit):
            n = lax.rem(coordinate + d, limit)
            to[d][...] = sum(p[n].astype(F32) for p in parts).astype(BF)


def chips_three_body(sizes, depth, here, *refs):
    side, front, cut = sizes
    first, second = refs[:front], refs[front : front + side]
    outs, kept = refs[front + side : -1], refs[-1]
    rows = kept.shape[1]
    for parts, begin_at in ((first, 0), (second, cut)):
        total = sum(p[...].astype(F32) for p in parts)
        for n in range(total.shape[0] // rows):
            kept[begin_at // rows + n] = total[n * rows : n * rows + rows, :].astype(BF)
    for d in range(depth):
        outs[d][...] = kept[lax.rem(here[3] + d, depth)]


def small_call(body, here, args, out_shape, scratch, name):
    whole = pl.BlockSpec(memory_space=pltpu.VMEM)
    moved = sum(math.prod(o.shape) * o.dtype.itemsize for o in [*args, *out_shape])
    return pl.pallas_call(
        body,
        in_specs=[pl.BlockSpec(memory_space=pltpu.SMEM)] + [whole] * len(args),
        out_specs=[whole] * len(out_shape),
        out_shape=out_shape,
        scratch_shapes=scratch,
        compiler_params=pltpu.CompilerParams(vmem_limit_bytes=24 << 20),
        cost_estimate=pl.CostEstimate(flops=moved, bytes_accessed=moved, transcendentals=0),
        name=name,
    )(here, *args)


def chips_one(here, mine, received, sizes):
    side, front, cut = sizes
    size, cols = mine[0].shape[1], sum(m.shape[2] for m in mine)
    outs = [shape((front, cut, cols), BF)] * side + [shape((side, size - cut, cols), BF)] * front
    body = functools.partial(chips_one_body, sizes, len(mine))
    done = small_call(body, here, [*mine, *received], outs, [], "chips_one")
    return done[:side], done[side:]


def chips_two(here, first, second, sizes):
    side, front, _ = sizes
    outs = [shape(first[0].shape[1:], BF)] * front + [shape(second[0].shape[1:], BF)] * side
    body = functools.partial(chips_two_body, sizes)
    done = small_call(body, here, [*first, *second], outs, [], "chips_two")
    return done[:front], done[front:]


def chips_three(here, first, second, sizes, depth):
    cols = first[0].shape[1]
    rows = (first[0].shape[0] + second[0].shape[0]) // depth
    body = functools.partial(chips_three_body, sizes, depth)
    scratch = [pltpu.VMEM((depth, rows, cols), BF)]
    outs = [shape((rows, cols), BF)] * depth
    return small_call(body, here, [*first, *second], outs, scratch, "chips_three")


def pack_first_body(qkv, vectors, packed, square):
    rows, third = qkv.shape[0], qkv.shape[1] // 3
    size = 256
    at = 0
    for group in range(third // size):
        for part in range(3):
            source = part * third + group * size
            packed[:, at : at + size] = qkv[:, source : source + size]
            at += size
    square[...] = jnp.zeros_like(square)
    square[: vectors.shape[0], : vectors.shape[1]] = vectors[...].astype(F32)
    packed[:, at:] = square[...].T[:rows, :].astype(BF)


def pack_first(qkv, vectors):
    rows, cols = qkv.shape
    whole = pl.BlockSpec(memory_space=pltpu.VMEM)
    return pl.pallas_call(
        pack_first_body,
        in_specs=[whole] * 2,
        out_specs=whole,
        out_shape=shape((rows, cols + LANES), BF),
        scratch_shapes=[pltpu.VMEM((LANES, LANES), F32)],
        name="pack_first",
    )(qkv, vectors)


def pack_rest_body(down, up, out, packed):
    rows, units = up.shape
    width = down.shape[1]
    for n in range(units // width):
        packed[:, n * width : n * width + width] = down[n * rows : n * rows + rows, :]
    packed[:, units : 2 * units] = up[...]
    packed[:, 2 * units :] = out[...]


def pack_rest(down, up, out):
    rows, units = up.shape
    whole = pl.BlockSpec(memory_space=pltpu.VMEM)
    return pl.pallas_call(
        pack_rest_body,
        in_specs=[whole] * 3,
        out_specs=whole,
        out_shape=shape((rows, 2 * units + out.shape[1]), BF),
        name="pack_rest",
    )(down, up, out)


def finish_body(count, vectors, *refs):
    parts, wide, refs = refs[:count], refs[count], refs[count + 1 :]
    qkv, out, up, down, up_bias = refs[:5]
    singles, square = refs[5 : 5 + vectors], refs[-1]
    rows, width = out.shape
    units = up.shape[1]
    size = 256
    total = sum(p[...].astype(F32) for p in parts)
    at = 0
    for group in range(width // size):
        for part in range(3):
            target = part * width + group * size
            qkv[:, target : target + size] = total[:, at : at + size]
            at += size
    square[...] = jnp.zeros_like(square)
    square[:rows, :] = total[:, at:]
    turned = square[...].T
    for n in range(vectors):
        singles[n][...] = turned[n : n + 1, :rows]
    for n in range(units // width):
        up_bias[n : n + 1, :] = turned[vectors + n : vectors + n + 1, :rows]
        down[n * rows : n * rows + rows, :] = wide[:, n * width : n * width + width].astype(F32)
    up[...] = wide[:, units : 2 * units].astype(F32)
    out[...] = wide[:, 2 * units :].astype(F32)


def finish(parts, wide, width, vectors):
    rows = wide.shape[0]
    units = (wide.shape[1] - width) // 2
    folds = units // width
    whole = pl.BlockSpec(memory_space=pltpu.VMEM)
    out_shape = [
        shape((rows, 3 * width), F32),
        shape((rows, width), F32),
        shape((rows, units), F32),
        shape((rows * folds, width), F32),
        shape((folds, rows), F32),
    ] + [shape((1, rows), F32)] * vectors
    return pl.pallas_call(
        functools.partial(finish_body, len(parts), vectors),
        in_specs=[whole] * (len(parts) + 1),
        out_specs=[whole] * len(out_shape),
        out_shape=out_shape,
        scratch_shapes=[pltpu.VMEM((LANES, LANES), F32)],
        compiler_params=pltpu.CompilerParams(vmem_limit_bytes=24 << 20),
        name="finish",
    )(*parts, wide)


AXES = ("side", "front", "core", "fsdp")


def split_mesh(mesh):
    outer, inner = mesh.shape["dp"], mesh.shape["fsdp"]
    cores = 2 if outer % 2 == 0 else 1
    side = math.isqrt(outer // cores)
    while (outer // cores) % side:
        side -= 1
    sizes = (side, outer // cores // side, cores, inner)
    return Mesh(mesh.devices.reshape(sizes), AXES)


def shifted(values, axis, distance):
    size = lax.axis_size(axis)
    return lax.ppermute(values, axis, [(i, (i + distance) % size) for i in range(size)])


def direct(values, axis):
    return [values] + [shifted(values, axis, d) for d in range(1, lax.axis_size(axis))]


def joined(parts):
    return parts[0] if len(parts) == 1 else jnp.concatenate(parts, axis=0)


def place_body(offsets, with_vectors, owners, *refs):
    count = len(offsets)
    parts, out, rest = refs[:count], refs[count], refs[count + 1 :]
    sems, rows = rest[-1], out.shape[1]
    copies = []
    for part, offset in zip(parts, offsets):
        for n in range(part.shape[0]):
            at = len(copies)
            target = out.at[owners[at], :, offset : offset + part.shape[2]]
            copies.append(pltpu.make_async_copy(part.at[n], target, sems.at[at]))
    for copy in copies:
        copy.start()
    for copy in copies:
        copy.wait()
    if with_vectors:
        vectors, columns = rest[:2]
        for n in range(out.shape[0]):
            columns[n * rows : n * rows + rows, :] = out[n, :, out.shape[2] - LANES :]
        vectors[...] = columns[...].astype(F32).T


def place(parts, offsets, owners, total, cols, with_vectors=False):
    rows = parts[0].shape[1]
    whole = pl.BlockSpec(memory_space=pltpu.VMEM)
    copies = sum(p.shape[0] for p in parts)
    out_shape = [shape((total, rows, cols), BF)]
    scratch = [pltpu.SemaphoreType.DMA((copies,))]
    if with_vectors:
        out_shape.append(shape((LANES, total * rows), F32))
        scratch = [pltpu.VMEM((total * rows, LANES), BF)] + scratch
    moved = 2 * total * rows * cols
    done = pl.pallas_call(
        functools.partial(place_body, tuple(offsets), with_vectors),
        in_specs=[pl.BlockSpec(memory_space=pltpu.SMEM)]
        + [pl.BlockSpec(memory_space=pl.ANY)] * len(parts),
        out_specs=[whole] * len(out_shape),
        out_shape=out_shape,
        scratch_shapes=scratch,
        compiler_params=pltpu.CompilerParams(vmem_limit_bytes=VMEM_LIMIT),
        cost_estimate=pl.CostEstimate(flops=0, bytes_accessed=2 * moved, transcendentals=0),
        name="place",
    )(owners, *parts)
    return done[0].reshape(total * rows, cols), done[1:]


def orders():
    depth = lax.axis_size("fsdp")
    cut = max(1, depth // 2)
    return [part for part in ((0, cut, (0, 1)), (cut, depth, (1, 0))) if part[0] < part[1]]


def begin(shard):
    line = direct(shard[None], "fsdp")
    return [joined(line[low:high]) for low, high, _ in orders()]


def across(blocks, stage):
    return [joined(direct(b, AXES[o[2][stage]])) for b, o in zip(blocks, orders())]


def over(blocks):
    return [part for b in blocks for part in direct(b, "core")]


def owners_of(steps):
    sizes = [lax.axis_size(a) for a in AXES]
    here = [lax.axis_index(a) for a in AXES]
    table = jnp.asarray(steps, jnp.int32)
    owner = jnp.zeros((len(steps),), jnp.int32)
    for n, size in enumerate(sizes):
        owner = owner * size + lax.rem(here[n] - table[:, n] + size, size)
    return owner


def owner_table():
    sizes = [lax.axis_size(a) for a in AXES]
    steps = []
    for low, high, order in orders():
        for c in range(sizes[2]):
            for second in range(sizes[order[1]]):
                for first in range(sizes[order[0]]):
                    moved = {order[0]: first, order[1]: second}
                    steps += [(moved[0], moved[1], c, z) for z in range(low, high)]
    return owners_of(steps)


def exchanged(parts, axis):
    return [parts[0]] + [shifted(p, axis, d) for d, p in enumerate(parts) if d > 0]


def on_device(patches, picture_ids, norm1_gain, norm1_bias, qkv_weight, query_shift, value_shift,
              query_gain, query_bias, key_gain, out_weight, out_bias, norm2_gain, norm2_bias,
              up_weight, up_bias, down_weight, down_bias, out_grad):
    width = patches.shape[1]
    rows = qkv_weight.shape[0]
    units = up_weight.shape[1]
    folds = units // width
    side, front, cores, depth = (lax.axis_size(a) for a in AXES)
    total = side * front * cores * depth
    vectors_here = [norm1_gain, norm1_bias, query_shift, value_shift, query_gain, query_bias,
                    key_gain, out_bias, norm2_gain, norm2_bias, down_bias, up_bias]
    count = sum(v.shape[0] for v in vectors_here)
    small, at = 0.0, 0
    for v in vectors_here:
        small += jnp.pad(v.astype(F32), (at, count - at - v.shape[0]))
        at += v.shape[0]
    small = small.reshape(-1, rows)
    here = jnp.stack([lax.axis_index(a) for a in AXES]).astype(jnp.int32)
    core = here[2:3]

    second = lax.all_gather(
        pack_rest(down_weight, up_weight, out_weight), AXES, axis=0, tiled=True
    )
    one = begin(pack_first(qkv_weight, small))
    extras = (*picture_lanes(picture_ids), owner_table())
    one, extras = lax.optimization_barrier((one, extras))
    extra_q, extra_k, padding, owners = extras
    one = over(across(across(one, 0), 1))
    offsets = [0] * len(one)
    first, (vectors,) = place(one, offsets, owners, total, 3 * width + LANES, with_vectors=True)
    b_up = vectors[UP_LANE : UP_LANE + folds].reshape(folds, -1, rows).transpose(1, 0, 2)
    b_up = b_up.reshape(1, -1)

    turned, q, k, v, q_hat, k_hat, q_scale, k_scale = project(patches, first, vectors)
    att, extra_back = attend(q, k, v, extra_q, extra_k, padding)
    (mine_down, other_down, mine_up, other_up, up_sum, mixed, gx2, gy, sums_two) = hidden(
        core, att, patches, out_grad, second, vectors, b_up, rows, depth
    )
    go, mine_out, other_out = mix_back(core, gy, att, second, depth * rows)
    received = [shifted(p, "core", 1) for p in (other_down, other_up, other_out)]
    merged = merge([mine_down, mine_up, mine_out], received)
    merged, go = lax.optimization_barrier((merged, go))
    flat = merged.reshape(-1, merged.shape[2])
    flat = lax.psum_scatter(flat, AXES[:2], scatter_dimension=0, tiled=True)
    grads, sums_att = attend_back(
        q, k, v, go, att, extra_back, extra_k, padding, q_hat, k_hat, q_scale, k_scale, vectors
    )
    sums_att = sums_att.reshape(-1, 8, width).sum(axis=0)
    mine_qkv, other_qkv, mine_columns, other_columns = project_grad(
        core, turned, grads, first, sums_att, sums_two, up_sum, depth * rows
    )
    received = [shifted(p, "core", 1) for p in (other_qkv, other_columns)]
    sizes = (side, front, depth // 2 * rows)
    last = chips_one(here, [mine_qkv, mine_columns], received, sizes)
    last, flat = lax.optimization_barrier((last, flat))
    wide_out = lax.psum_scatter(flat, AXES[3], scatter_dimension=0, tiled=True)
    last = exchanged(last[0], "side"), exchanged(last[1], "front")
    last = chips_two(here, *last, sizes)
    last = exchanged(last[0], "front"), exchanged(last[1], "side")
    last = chips_three(here, *last, sizes, depth)
    last, gx2 = lax.optimization_barrier((last, gx2))
    last = exchanged(last, "fsdp")
    patches_grad = project_back(grads, first, patches, gx2, vectors)
    qkv_out, out_out, up_out, down_out, up_bias_out, *singles = finish(
        last, wide_out, width, UP_LANE
    )
    (gain_one_out, bias_one_out, q_shift_out, v_shift_out, q_gain_out, q_bias_out, k_gain_out,
     gain_two_out, bias_two_out, out_bias_out, down_bias_out) = [v.reshape(-1) for v in singles]
    return (
        mixed, patches_grad, gain_one_out, bias_one_out, qkv_out, q_shift_out, v_shift_out,
        q_gain_out, q_bias_out, k_gain_out, out_out, out_bias_out, gain_two_out, bias_two_out,
        up_out, up_bias_out.reshape(-1), down_out, down_bias_out,
    )


def solution(mesh):
    flat = P(AXES)
    wide = P(AXES, None)
    in_specs = (wide, flat, flat, flat, wide, flat, flat, flat, flat, flat, wide, flat, flat, flat,
                wide, flat, wide, flat, wide)
    out_specs = (wide, wide, flat, flat, wide, flat, flat, flat, flat, flat, wide, flat, flat, flat,
                 wide, flat, wide, flat)
    return jax.shard_map(
        on_device, mesh=split_mesh(mesh), in_specs=in_specs, out_specs=out_specs, check_vma=False
    )
```

```python
import functools
import math
import jax
import jax.numpy as jnp
from jax import lax
from jax.experimental import pallas as pl
from jax.experimental.pallas import tpu as pltpu
from jax.sharding import Mesh, PartitionSpec as P

HEADS = 12
HD = 64
ROW = 1024
EPSILON = 1e-06
BF = jnp.bfloat16
F32 = jnp.float32
EXP_SCALE = HD**-0.5 * math.log2(math.e)
VMEM_LIMIT = 56 << 20
LANES = 128
GAIN_ONE, BIAS_ONE, Q_SHIFT, V_SHIFT, Q_GAIN, Q_BIAS, K_GAIN = range(7)
B_OUT, GAIN_TWO, BIAS_TWO, B_DOWN = range(7, 11)


def nn(left, right):
    return jnp.dot(left, right, preferred_element_type=F32)


def nt(left, right):
    return lax.dot_general(left, right, (((1,), (1,)), ((), ())), preferred_element_type=F32)


def tn(left, right):
    return lax.dot_general(left, right, (((0,), (0,)), ((), ())), preferred_element_type=F32)


def call(body, grid, in_specs, out_specs, out_shape, scratch, flops, name, limit=VMEM_LIMIT):
    def run(*args):
        moved = sum(a.size * a.dtype.itemsize for a in args)
        moved += sum(math.prod(o.shape) * o.dtype.itemsize for o in out_shape)
        return pl.pallas_call(
            body,
            grid=grid,
            in_specs=in_specs,
            out_specs=out_specs,
            out_shape=out_shape,
            scratch_shapes=scratch,
            compiler_params=pltpu.CompilerParams(vmem_limit_bytes=limit),
            cost_estimate=pl.CostEstimate(flops=flops, bytes_accessed=moved, transcendentals=0),
            name=name,
        )(*args)

    return run


def row_of(vectors, n):
    return vectors[n : n + 1, :]


def shape(dims, kind):
    return jax.ShapeDtypeStruct(dims, kind)


def chunk_at(step, size):
    return pl.ds(pl.multiple_of(step * size, size), size)


def block_mean(size):
    rows_at = lax.broadcasted_iota(jnp.int32, (size, size), 0)
    cols_at = lax.broadcasted_iota(jnp.int32, (size, size), 1)
    return jnp.where(rows_at // HD == cols_at // HD, 1.0 / HD, 0.0).astype(BF)


def normed(values):
    average = jnp.mean(values, axis=-1, keepdims=True)
    centred = values - average
    variance = jnp.mean(centred * centred, axis=-1, keepdims=True)
    scale = lax.rsqrt(variance + EPSILON)
    return centred * scale, scale


def norm_back(hat, scale, grads):
    first = jnp.mean(grads, axis=-1, keepdims=True)
    second = jnp.mean(grads * hat, axis=-1, keepdims=True)
    return scale * (grads - first - hat * second)


def column_sum(values):
    return jnp.sum(values, axis=0, keepdims=True)


def project_body(x, whole_rows, weights, own_rows,
                 turned, q, k, v, q_hat, k_hat, q_scale, k_scale, a1):
    tokens = x.shape[0]
    step = 1024

    @pl.when(pl.program_id(0) == 0)
    def _():
        def first(t, carry):
            rows = chunk_at(t, 256)
            hat, scale = normed(x[rows, :].astype(F32))
            a1[rows, :] = (hat * row_of(whole_rows, GAIN_ONE) + row_of(whole_rows, BIAS_ONE)).astype(BF)
            return carry

        lax.fori_loop(0, tokens // 256, first, 0)
        turned[...] = a1[...].T

    cols = weights.shape[1] // 3
    means = block_mean(cols)

    def one(t, carry):
        rows = chunk_at(t, step)
        source = a1[rows, :]

        def head_norm(pre, out, hat_out, scale_out, gains, biases):
            high = pre.astype(BF)
            low = (pre - high.astype(F32)).astype(BF)
            centred = pre - (nn(high, means) + nn(low, means))
            variance = nn((centred * centred).astype(BF), means)
            scale = lax.rsqrt(variance + EPSILON)
            hat = centred * scale
            shifted = hat * gains
            out[rows, :] = (shifted if biases is None else shifted + biases).astype(BF)
            hat_out[rows, :] = hat.astype(BF)
            scale_out[rows, :] = scale.astype(BF)

        pre = nn(source, weights[:, :cols]) + row_of(own_rows, Q_SHIFT)
        head_norm(pre, q, q_hat, q_scale, row_of(own_rows, Q_GAIN), row_of(own_rows, Q_BIAS))
        pre = nn(source, weights[:, cols : 2 * cols])
        head_norm(pre, k, k_hat, k_scale, row_of(own_rows, K_GAIN), None)
        pre = nn(source, weights[:, 2 * cols :])
        v[rows, :] = (pre + row_of(own_rows, V_SHIFT)).astype(BF)
        return carry

    lax.fori_loop(0, tokens // step, one, 0)


def project(x, weights, vectors):
    tokens, width = x.shape
    cols = 256
    parts = width // cols
    whole = pl.BlockSpec((tokens, width), lambda j: (0, 0))
    out = pl.BlockSpec((tokens, cols), lambda j: (0, j))
    return call(
        project_body,
        (parts,),
        [
            whole,
            pl.BlockSpec((8, width), lambda j: (0, 0)),
            pl.BlockSpec((width, 3 * cols), lambda j: (0, j)),
            pl.BlockSpec((8, cols), lambda j: (0, j)),
        ],
        [pl.BlockSpec((width, tokens), lambda j: (0, 0))] + [out] * 7,
        [shape((width, tokens), BF)] + [shape((tokens, width), BF)] * 7,
        [pltpu.VMEM((tokens, width), BF)],
        6 * tokens * width * width,
        "project",
    )(x, vectors, weights, vectors)


def half(values, head):
    lane = lax.broadcasted_iota(jnp.int32, values.shape, 1)
    return jnp.where((lane < HD) if head == 0 else (lane >= HD), values, jnp.zeros_like(values))


def three_parts(values, lane):
    high = values.astype(BF).astype(F32)
    rest = values - high
    middle = rest.astype(BF).astype(F32)
    low = rest - middle
    return jnp.where(
        lane == 12, high, jnp.where(lane == 13, middle, jnp.where(lane == 14, low, 0.0))
    )


def picture_lanes(pic_ids):
    lane = lax.broadcasted_iota(jnp.int32, (pic_ids.shape[0], LANES), 1)
    same = (pic_ids[:, None] == lane + 1) & (lane < 10)
    for_q = jnp.where(same | (lane == 10), 32.0, 0.0).astype(BF)
    ones = jnp.where((lane >= 12) & (lane < 15), 1.0, 0.0)
    for_k = jnp.where(same, 64.0, jnp.where(lane == 10, -64.0, ones)).astype(BF)
    padding = jnp.broadcast_to((pic_ids == 0)[:, None], lane.shape).astype(F32)
    return for_q, for_k, padding


def attend_body(q, k, v, extra_q, extra_k, padding, att, extra_back):
    lane = lax.broadcasted_iota(jnp.int32, (ROW, LANES), 1)
    queries = jnp.concatenate([q[...], extra_q[...]], axis=1)
    results, totals = [], []
    for h in (0, 1):
        keys = jnp.concatenate([half(k[...], h), extra_k[...]], axis=1)
        powers = jnp.exp2(nt(keys, queries) * EXP_SCALE).astype(BF)
        mine = (lane < HD) if h == 0 else (lane >= HD)
        out = tn(jnp.where(mine, v[...], jnp.ones_like(v[...])), powers)
        low, high = out[:HD, :], out[HD:, :]
        results.append(low if h == 0 else high)
        totals.append(high if h == 0 else low)
    result = jnp.concatenate(results, axis=0).T
    pad = padding[...]
    total = jnp.concatenate(totals, axis=0).T + pad
    att[...] = ((result + pad * v[...].astype(F32)) / total).astype(BF)
    row_term = jnp.log(total) * -(HD**0.5)
    other = pltpu.roll(row_term, HD, 1)
    base = extra_q[...].astype(F32)
    for h in (0, 1):
        mine = row_term if h == 0 else other
        extra_back[h] = (base + three_parts(mine, lane)).astype(BF)


def attend(q, k, v, extra_q, extra_k, padding):
    tokens, width = q.shape
    pairs = width // LANES
    block = pl.BlockSpec((ROW, LANES), lambda r, p: (r, p))
    fixed = pl.BlockSpec((ROW, LANES), lambda r, p: (r, 0))
    return call(
        attend_body,
        (tokens // ROW, pairs),
        [block] * 3 + [fixed] * 3,
        [block, pl.BlockSpec((2, ROW, LANES), lambda r, p: (p, r, 0))],
        [shape((tokens, width), BF), shape((2 * pairs, tokens, LANES), BF)],
        [],
        16 * tokens * ROW * width,
        "attend",
    )(q, k, v, extra_q, extra_k, padding)


def attend_back_body(q, k, v, go, att, extra_q, extra_k, padding, q_hat, k_hat, q_scale, k_scale,
                     vectors, packed, sums):
    offset = lax.rem(pl.program_id(1), 2) * LANES
    q_at, k_at, v_at = [pl.ds(pl.multiple_of(offset + n, LANES), LANES) for n in (0, 256, 512)]
    lane = lax.broadcasted_iota(jnp.int32, (ROW, LANES), 1)
    rows_at = lax.broadcasted_iota(jnp.int32, (LANES, LANES), 0)
    cols_at = lax.broadcasted_iota(jnp.int32, (LANES, LANES), 1)
    terms = go[...].astype(F32) * att[...].astype(F32)
    high = terms.astype(BF)
    low = (terms - high.astype(F32)).astype(BF)
    v_extra = jnp.where((lane >= 12) & (lane < 15), 1.0, 0.0).astype(BF)
    q_half, k_half, go_half, probs_all, grads_all = [], [], [], [], []
    for h in (0, 1):
        mine = (rows_at < HD) if h == 0 else (rows_at >= HD)
        pick = jnp.where(mine & (cols_at >= 12) & (cols_at < 15), 1.0, 0.0).astype(BF)
        delta = nn(high, pick) + nn(low, pick)
        go_extra = jnp.concatenate([go[...], three_parts(-delta, lane).astype(BF)], axis=1)
        key = half(k[...], h)
        scores = nt(
            jnp.concatenate([q[...], extra_q[h]], axis=1),
            jnp.concatenate([key, extra_k[...]], axis=1),
        )
        pulled = nt(go_extra, jnp.concatenate([half(v[...], h), v_extra], axis=1))
        probs = jnp.exp2(scores * EXP_SCALE)
        q_half.append(half(q[...], h))
        k_half.append(key)
        go_half.append(half(go[...], h))
        probs_all.append(probs.astype(BF))
        grads_all.append((probs * pulled).astype(BF))
    grad_v = tn(jnp.concatenate(go_half, axis=0), jnp.concatenate(probs_all, axis=0)).T
    grad_k = tn(jnp.concatenate(q_half, axis=0), jnp.concatenate(grads_all, axis=0)).T * HD**-0.5
    keys_turned = jnp.concatenate([part.T for part in k_half], axis=1)
    grad_q = nt(keys_turned, jnp.concatenate(grads_all, axis=1)).T * HD**-0.5
    means = block_mean(LANES)

    def head_norm_back(incoming, hat, scale, gains):
        inner = incoming * gains
        first = nn(inner.astype(BF), means)
        second = nn((inner * hat).astype(BF), means)
        return (scale * (inner - first - hat * second)).astype(BF)

    out_v = (grad_v + padding[...] * go[...].astype(F32)).astype(BF)
    packed[:, v_at] = out_v
    hat = k_hat[...].astype(F32)
    packed[:, k_at] = head_norm_back(grad_k, hat, k_scale[...].astype(F32), row_of(vectors, K_GAIN))
    k_sum = column_sum(grad_k * hat)
    hat = q_hat[...].astype(F32)
    out_q = head_norm_back(grad_q, hat, q_scale[...].astype(F32), row_of(vectors, Q_GAIN))
    packed[:, q_at] = out_q
    parts = [out_q.astype(F32), out_v.astype(F32), grad_q * hat, grad_q]
    zero = jnp.zeros((3, LANES), F32)
    sums[...] = jnp.concatenate([*map(column_sum, parts), k_sum, zero], axis=0)


def attend_back(q, k, v, go, att, extra_q, extra_k, padding, q_hat, k_hat, q_scale, k_scale,
                vectors):
    tokens, width = q.shape
    count = tokens // ROW
    block = pl.BlockSpec((ROW, LANES), lambda r, p: (r, p))
    fixed = pl.BlockSpec((ROW, LANES), lambda r, p: (r, 0))
    eight = pl.BlockSpec((8, LANES), lambda r, p: (0, p))
    return call(
        attend_back_body,
        (count, width // LANES),
        [block] * 5
        + [pl.BlockSpec((2, ROW, LANES), lambda r, p: (p, r, 0)), fixed, fixed]
        + [block] * 4
        + [eight],
        [
            pl.BlockSpec((ROW, 6 * LANES), lambda r, p: (r, p // 2)),
            pl.BlockSpec((8, LANES), lambda r, p: (r, p)),
        ],
        [shape((tokens, 3 * width), BF), shape((8 * count, width), F32)],
        [],
        40 * tokens * ROW * width,
        "attend_back",
    )(q, k, v, go, att, extra_q, extra_k, padding, q_hat, k_hat, q_scale, k_scale, vectors)


SLOPE = math.sqrt(2.0 / math.pi)
CUBE = 0.044715


def gelu_pair(values):
    square = values * values
    share = 0.5 + 0.5 * jnp.tanh(values * (SLOPE + (SLOPE * CUBE) * square))
    gelu = values * share
    return gelu, share + gelu * (1.0 - share) * (2 * SLOPE + (6 * SLOPE * CUBE) * square)


UP_LANE = 11


def hidden_body(counts, core, *refs):
    (att, w_out, patches, og_out, folded, up, vectors, b_up, mine_down, other_down, mine_up,
     other_up, sum_up, mixed, gx2, gy, sums, x2, a2, y, ga, turned, act, grad, down, og,
     sems) = refs
    rows_each, groups = counts
    tokens, width = a2.shape
    folds = folded.shape[1] // width
    each = folded.shape[0] // rows_each
    step = pl.program_id(0)

    @pl.when(step == 0)
    def _():
        fetch = pltpu.make_async_copy(og_out, og, sems.at[0])
        fetch.start()
        y[...] = jnp.zeros_like(y)
        ga[...] = jnp.zeros_like(ga)

        def mix(t, carry):
            rows = chunk_at(t, 512)
            middle = patches[rows, :].astype(F32) + (nn(att[rows, :], w_out[...]) + row_of(vectors, B_OUT))
            x2[rows, :] = middle
            scaled = normed(middle)[0] * row_of(vectors, GAIN_TWO)
            a2[rows, :] = (scaled + row_of(vectors, BIAS_TWO)).astype(BF)
            return carry

        lax.fori_loop(0, tokens // 512, mix, 0)
        turned[...] = a2[...].T
        fetch.wait()

    for o in range(each):
        for w in range(folds):
            at = (o * folds + w) * rows_each
            source = folded[o * rows_each : o * rows_each + rows_each, w * width : w * width + width]
            down[at : at + rows_each, :] = source

    value, slope = gelu_pair(nn(a2[...], up[...]) + b_up[...])
    act[...] = value.astype(BF)
    y[...] += nn(act[...], down[...])
    pulled = nt(og[...], down[...]) * slope
    grad[...] = pulled.astype(BF)
    ga[...] += nt(grad[...], up[...])
    summed = jnp.broadcast_to(column_sum(grad[...].astype(F32)), (LANES, width)).T
    lane = lax.broadcasted_iota(jnp.int32, (rows_each, LANES), 1)
    for o in range(each):
        columns = jnp.zeros((rows_each, LANES), F32)
        for w in range(folds):
            at = (o * folds + w) * rows_each
            columns = jnp.where(lane == UP_LANE + w, summed[at : at + rows_each, :], columns)
        sum_up[o * rows_each : o * rows_each + rows_each, :] = columns

    down_rows = tn(act[...], og[...]).astype(BF)
    up_rows = nn(turned[...], grad[...]).astype(BF)

    def emit(down_refs, up_refs):
        for o in range(each):
            block, inner = divmod(o, 2 * groups)
            c, z = divmod(inner, groups)
            rows = slice(z * rows_each, z * rows_each + rows_each)
            for w in range(folds):
                at = (o * folds + w) * rows_each
                down_refs[c][block, rows, w * width : w * width + width] = down_rows[
                    at : at + rows_each, :
                ]
        size = groups * rows_each
        for block in range(width // (2 * size)):
            for c in (0, 1):
                at = (2 * block + c) * size
                up_refs[c][block, :, :] = up_rows[at : at + size, :]

    @pl.when(core[0] == 0)
    def _():
        emit((mine_down, other_down), (mine_up, other_up))

    @pl.when(core[0] == 1)
    def _():
        emit((other_down, mine_down), (other_up, mine_up))

    @pl.when(step == pl.num_programs(0) - 1)
    def _():
        carry = (jnp.zeros((1, width), F32),) * 4
        copies = []
        for t in range(tokens // 256):
            rows = slice(t * 256, t * 256 + 256)
            middle = x2[rows, :]
            outer = og[rows, :].astype(F32)
            act[rows, :] = (middle + (y[rows, :] + row_of(vectors, B_DOWN))).astype(BF)
            hat, scale = normed(middle)
            incoming = ga[rows, :]
            total = outer + norm_back(hat, scale, incoming * row_of(vectors, GAIN_TWO))
            ga[rows, :] = total
            rounded = total.astype(BF)
            grad[rows, :] = rounded
            for n, (source, target) in enumerate(((act, mixed), (ga, gx2), (grad, gy))):
                sem = sems.at[1 + 3 * t + n]
                copies.append(pltpu.make_async_copy(source.at[rows], target.at[rows], sem))
                copies[-1].start()
            new = (incoming * hat, incoming, rounded.astype(F32), outer)
            carry = tuple(old + column_sum(n) for old, n in zip(carry, new))
        sums[...] = jnp.concatenate([*carry, jnp.zeros((4, width), F32)], axis=0)
        for copy in copies:
            copy.wait()


def hidden(core, att, patches, og, weights, vectors, b_up, rows_each, groups):
    tokens, width = patches.shape
    units = (weights.shape[1] - width) // 2
    folds = units // width
    blocks = width // (2 * groups * rows_each)
    each = blocks // folds
    size = groups * rows_each
    smem = pl.BlockSpec(memory_space=pltpu.SMEM)
    single = dict(pipeline_mode=pl.Buffered(1))
    fixed = pl.BlockSpec((tokens, width), lambda j: (0, 0), **single)
    row = pl.BlockSpec((1, width), lambda j: (0, j))
    by_rows = pl.BlockSpec((each, size, units), lambda j: (j, 0, 0))
    by_cols = pl.BlockSpec((blocks, size, width), lambda j: (0, 0, j))
    square = pltpu.VMEM((tokens, width), BF)
    anywhere = pl.BlockSpec(memory_space=pl.ANY)
    chunks = tokens // 256
    return call(
        functools.partial(hidden_body, (rows_each, groups)),
        (folds,),
        [
            smem,
            fixed,
            pl.BlockSpec((width, width), lambda j: (0, 2 * folds), **single),
            fixed,
            anywhere,
            pl.BlockSpec((width // folds, units), lambda j: (j, 0)),
            pl.BlockSpec((width, width), lambda j: (0, folds + j)),
            pl.BlockSpec((16, width), lambda j: (0, 0)),
            row,
        ],
        [by_rows, by_rows, by_cols, by_cols, pl.BlockSpec((width // folds, LANES), lambda j: (j, 0)), anywhere, anywhere, anywhere,
         pl.BlockSpec((8, width), lambda j: (0, 0))],
        [shape((blocks, size, units), BF)] * 4
        + [
            shape((width, LANES), F32),
            shape((tokens, width), BF),
            shape((tokens, width), F32),
            shape((tokens, width), BF),
            shape((8, width), F32),
        ],
        [
            pltpu.VMEM((tokens, width), F32),
            square,
            pltpu.VMEM((tokens, width), F32),
            pltpu.VMEM((tokens, width), F32),
            pltpu.VMEM((width, tokens), BF),
            square,
            square,
            pltpu.VMEM((width, width), BF),
            square,
            pltpu.SemaphoreType.DMA((1 + 3 * chunks,)),
        ],
        12 * tokens * width * units,
        "hidden",
    )(core, att, weights, patches, og, weights, weights, vectors, b_up)


def mix_back_body(core, gy, att, w_out, go, mine, other):
    go[...] = nt(gy[...], w_out[...]).astype(BF)
    grads = tn(att[...], gy[...]).astype(BF)
    blocks, size, _ = mine.shape

    def emit(refs):
        for n in range(2 * blocks):
            refs[n % 2][n // 2, :, :] = grads[n * size : n * size + size, :]

    @pl.when(core[0] == 0)
    def _():
        emit((mine, other))

    @pl.when(core[0] == 1)
    def _():
        emit((other, mine))


def mix_back(core, gy, att, weights, size):
    tokens, width = gy.shape
    last = weights.shape[1] // width - 1
    blocks = width // (2 * size)
    whole = pl.BlockSpec((tokens, width), lambda j: (0, 0))
    grads = pl.BlockSpec((blocks, size, width), lambda j: (0, 0, 0))
    return call(
        mix_back_body,
        (1,),
        [
            pl.BlockSpec(memory_space=pltpu.SMEM),
            whole,
            whole,
            pl.BlockSpec((width, width), lambda j: (0, last)),
        ],
        [whole, grads, grads],
        [shape((tokens, width), BF)] + [shape((blocks, size, width), BF)] * 2,
        [],
        4 * tokens * width * width,
        "mix_back",
    )(core, gy, att, weights)


def merge_body(count, *refs):
    out = refs[2 * count]
    at = 0
    for n in range(count):
        size = refs[n].shape[2]
        total = refs[n][...].astype(F32) + refs[count + n][...].astype(F32)
        out[:, :, at : at + size] = total.astype(BF)
        at += size


def merge(mine, received):
    blocks, size, _ = mine[0].shape
    widths = [m.shape[2] for m in mine]
    many = 2
    specs = [pl.BlockSpec((many, size, w), lambda j: (j, 0, 0)) for w in widths]
    return call(
        functools.partial(merge_body, len(mine)),
        (blocks // many,),
        specs + specs,
        [pl.BlockSpec((many, size, sum(widths)), lambda j: (j, 0, 0))],
        [shape((blocks, size, sum(widths)), BF)],
        [],
        2 * blocks * size * sum(widths),
        "merge",
        20 << 20,
    )(*mine, *received)[0]


def project_grad_body(core, turned, grads, weights, vectors, sums_att, sums_two, sum_up, mine,
                      other, mine_columns, other_columns, gain_sum, bias_sum):
    result = nn(turned[...], grads[...])
    blocks, size, _ = mine.shape
    width = turned.shape[0]
    step = pl.program_id(0)
    wide = (width, LANES)
    current = weights[...].astype(F32)
    new_gain = jnp.broadcast_to(jnp.sum(result * current, axis=1, keepdims=True), wide)
    grad_sum = column_sum(grads[...].astype(F32))
    new_bias = jnp.broadcast_to(jnp.sum(current * grad_sum, axis=1, keepdims=True), wide)
    rounded = result.astype(BF)

    def emit(values, refs):
        for n in range(2 * blocks):
            refs[n % 2][n // 2, :, :] = values[n * size : n * size + size, :]

    def by_core(values, first, second):
        @pl.when(core[0] == 0)
        def _():
            emit(values, (first, second))

        @pl.when(core[0] == 1)
        def _():
            emit(values, (second, first))

    by_core(rounded, mine, other)

    @pl.when(step == 0)
    def _():
        gain_sum[...] = new_gain
        bias_sum[...] = new_bias

    @pl.when(step > 0)
    def _():
        gain_sum[...] += new_gain
        bias_sum[...] += new_bias

    @pl.when(step == pl.num_programs(0) - 1)
    def _():
        lane = lax.broadcasted_iota(jnp.int32, wide, 1)
        pair = vectors[...].astype(F32)
        gain = jnp.sum(jnp.where(lane == 0, pair, 0.0), axis=1, keepdims=True)
        bias = jnp.sum(jnp.where(lane == 1, pair, 0.0), axis=1, keepdims=True)
        gain_grad = (gain_sum[...] - bias * bias_sum[...]) / gain
        used = [jnp.zeros((2, width), F32), sums_att[:5, :], sums_two[:4, :]]
        zeros = jnp.zeros((LANES - UP_LANE, width), F32)
        columns = jnp.concatenate([*used, zeros], axis=0).T + sum_up[...]
        columns = jnp.where(lane == 0, gain_grad, jnp.where(lane == 1, bias_sum[...], columns))
        by_core(columns.astype(BF), mine_columns, other_columns)


def project_grad(core, turned, grads, weights, sums_att, sums_two, sum_up, size):
    width, tokens = turned.shape
    blocks = width // (2 * size)
    out = pl.BlockSpec((blocks, size, width), lambda j: (0, 0, j))
    columns = pl.BlockSpec((blocks, size, LANES), lambda j: (0, 0, 0))
    eight = pl.BlockSpec((8, width), lambda j: (0, 0))
    last = 3 * width // LANES
    return call(
        project_grad_body,
        (3,),
        [
            pl.BlockSpec(memory_space=pltpu.SMEM),
            pl.BlockSpec((width, tokens), lambda j: (0, 0)),
            pl.BlockSpec((tokens, width), lambda j: (0, j)),
            pl.BlockSpec((width, width), lambda j: (0, j)),
            pl.BlockSpec((width, LANES), lambda j: (0, last)),
            eight,
            eight,
            pl.BlockSpec((width, LANES), lambda j: (0, 0)),
        ],
        [out, out, columns, columns],
        [shape((blocks, size, 3 * width), BF)] * 2 + [shape((blocks, size, LANES), BF)] * 2,
        [pltpu.VMEM((width, LANES), F32)] * 2,
        6 * tokens * width * width,
        "project_grad",
    )(core, turned, grads, weights, weights, sums_att, sums_two, sum_up)


def project_back_body(grads, weights, x, gx2, vectors, out):
    incoming = nt(grads[...], weights[...])
    hat, scale = normed(x[...].astype(F32))
    out[...] = gx2[...] + norm_back(hat, scale, incoming * row_of(vectors, GAIN_ONE))


def project_back(grads, weights, x, gx2, vectors):
    tokens, width = x.shape
    step = 256
    block = pl.BlockSpec((step, width), lambda t: (t, 0))
    return call(
        project_back_body,
        (tokens // step,),
        [
            pl.BlockSpec((step, 3 * width), lambda t: (t, 0)),
            pl.BlockSpec((width, 3 * width), lambda t: (0, 0)),
            block,
            block,
            pl.BlockSpec((8, width), lambda t: (0, 0)),
        ],
        [block],
        [shape((tokens, width), F32)],
        [],
        6 * tokens * width * width,
        "project_back",
    )(grads, weights, x, gx2, vectors)[0]


def chips_one_body(sizes, count, here, *refs):
    side, front, cut = sizes
    mine, received, outs = refs[:count], refs[count : 2 * count], refs[2 * count :]
    size = mine[0].shape[1]
    at = 0
    for m, r in zip(mine, received):
        cols = slice(at, at + m.shape[2])
        at += m.shape[2]
        for d in range(side):
            for b in range(front):
                n = lax.rem(here[0] + d, side) * front + b
                total = m[n, :cut, :].astype(F32) + r[n, :cut, :].astype(F32)
                outs[d][b, :, cols] = total.astype(BF)
        for d in range(front):
            for a in range(side):
                n = a * front + lax.rem(here[1] + d, front)
                total = m[n, cut:size, :].astype(F32) + r[n, cut:size, :].astype(F32)
                outs[side + d][a, :, cols] = total.astype(BF)


def chips_two_body(sizes, here, *refs):
    side, front, _ = sizes
    first, second, outs = refs[:side], refs[side : side + front], refs[side + front :]
    for parts, limit, coordinate, to in (
        (first, front, here[1], outs[:front]),
        (second, side, here[0], outs[front:]),
    ):
        for d in range(limit):
            n = lax.rem(coordinate + d, limit)
            to[d][...] = sum(p[n].astype(F32) for p in parts).astype(BF)


def chips_three_body(sizes, depth, here, *refs):
    side, front, cut = sizes
    first, second = refs[:front], refs[front : front + side]
    outs, kept = refs[front + side : -1], refs[-1]
    rows = kept.shape[1]
    for parts, begin_at in ((first, 0), (second, cut)):
        total = sum(p[...].astype(F32) for p in parts)
        for n in range(total.shape[0] // rows):
            kept[begin_at // rows + n] = total[n * rows : n * rows + rows, :].astype(BF)
    for d in range(depth):
        outs[d][...] = kept[lax.rem(here[3] + d, depth)]


def small_call(body, here, args, out_shape, scratch, name):
    whole = pl.BlockSpec(memory_space=pltpu.VMEM)
    moved = sum(math.prod(o.shape) * o.dtype.itemsize for o in [*args, *out_shape])
    return pl.pallas_call(
        body,
        in_specs=[pl.BlockSpec(memory_space=pltpu.SMEM)] + [whole] * len(args),
        out_specs=[whole] * len(out_shape),
        out_shape=out_shape,
        scratch_shapes=scratch,
        compiler_params=pltpu.CompilerParams(vmem_limit_bytes=24 << 20),
        cost_estimate=pl.CostEstimate(flops=moved, bytes_accessed=moved, transcendentals=0),
        name=name,
    )(here, *args)


def chips_one(here, mine, received, sizes):
    side, front, cut = sizes
    size, cols = mine[0].shape[1], sum(m.shape[2] for m in mine)
    outs = [shape((front, cut, cols), BF)] * side + [shape((side, size - cut, cols), BF)] * front
    body = functools.partial(chips_one_body, sizes, len(mine))
    done = small_call(body, here, [*mine, *received], outs, [], "chips_one")
    return done[:side], done[side:]


def chips_two(here, first, second, sizes):
    side, front, _ = sizes
    outs = [shape(first[0].shape[1:], BF)] * front + [shape(second[0].shape[1:], BF)] * side
    body = functools.partial(chips_two_body, sizes)
    done = small_call(body, here, [*first, *second], outs, [], "chips_two")
    return done[:front], done[front:]


def chips_three(here, first, second, sizes, depth):
    cols = first[0].shape[1]
    rows = (first[0].shape[0] + second[0].shape[0]) // depth
    body = functools.partial(chips_three_body, sizes, depth)
    scratch = [pltpu.VMEM((depth, rows, cols), BF)]
    outs = [shape((rows, cols), BF)] * depth
    return small_call(body, here, [*first, *second], outs, scratch, "chips_three")


def pack_first_body(qkv, vectors, packed, square):
    rows, third = qkv.shape[0], qkv.shape[1] // 3
    size = 256
    at = 0
    for group in range(third // size):
        for part in range(3):
            source = part * third + group * size
            packed[:, at : at + size] = qkv[:, source : source + size]
            at += size
    square[...] = jnp.zeros_like(square)
    square[: vectors.shape[0], : vectors.shape[1]] = vectors[...].astype(F32)
    packed[:, at:] = square[...].T[:rows, :].astype(BF)


def pack_first(qkv, vectors):
    rows, cols = qkv.shape
    whole = pl.BlockSpec(memory_space=pltpu.VMEM)
    return pl.pallas_call(
        pack_first_body,
        in_specs=[whole] * 2,
        out_specs=whole,
        out_shape=shape((rows, cols + LANES), BF),
        scratch_shapes=[pltpu.VMEM((LANES, LANES), F32)],
        name="pack_first",
    )(qkv, vectors)


def pack_rest_body(down, up, out, packed):
    rows, units = up.shape
    width = down.shape[1]
    for n in range(units // width):
        packed[:, n * width : n * width + width] = down[n * rows : n * rows + rows, :]
    packed[:, units : 2 * units] = up[...]
    packed[:, 2 * units :] = out[...]


def pack_rest(down, up, out):
    rows, units = up.shape
    whole = pl.BlockSpec(memory_space=pltpu.VMEM)
    return pl.pallas_call(
        pack_rest_body,
        in_specs=[whole] * 3,
        out_specs=whole,
        out_shape=shape((rows, 2 * units + out.shape[1]), BF),
        name="pack_rest",
    )(down, up, out)


def finish_body(count, *refs):
    parts, wide, (qkv, out, up, down, rest) = refs[:count], refs[count], refs[count + 1 :]
    rows, width = out.shape
    units = up.shape[1]
    size = 256
    total = sum(p[...].astype(F32) for p in parts)
    at = 0
    for group in range(width // size):
        for part in range(3):
            target = part * width + group * size
            qkv[:, target : target + size] = total[:, at : at + size]
            at += size
    rest[...] = total[:, at:]
    for n in range(units // width):
        down[n * rows : n * rows + rows, :] = wide[:, n * width : n * width + width].astype(F32)
    up[...] = wide[:, units : 2 * units].astype(F32)
    out[...] = wide[:, 2 * units :].astype(F32)


def finish(parts, wide, width):
    rows = wide.shape[0]
    units = (wide.shape[1] - width) // 2
    whole = pl.BlockSpec(memory_space=pltpu.VMEM)
    out_shape = [
        shape((rows, 3 * width), F32),
        shape((rows, width), F32),
        shape((rows, units), F32),
        shape((rows * units // width, width), F32),
        shape((rows, LANES), F32),
    ]
    return pl.pallas_call(
        functools.partial(finish_body, len(parts)),
        in_specs=[whole] * (len(parts) + 1),
        out_specs=[whole] * len(out_shape),
        out_shape=out_shape,
        compiler_params=pltpu.CompilerParams(vmem_limit_bytes=24 << 20),
        name="finish",
    )(*parts, wide)


AXES = ("side", "front", "core", "fsdp")


def split_mesh(mesh):
    outer, inner = mesh.shape["dp"], mesh.shape["fsdp"]
    cores = 2 if outer % 2 == 0 else 1
    side = math.isqrt(outer // cores)
    while (outer // cores) % side:
        side -= 1
    sizes = (side, outer // cores // side, cores, inner)
    return Mesh(mesh.devices.reshape(sizes), AXES)


def shifted(values, axis, distance):
    size = lax.axis_size(axis)
    return lax.ppermute(values, axis, [(i, (i + distance) % size) for i in range(size)])


def direct(values, axis):
    return [values] + [shifted(values, axis, d) for d in range(1, lax.axis_size(axis))]


def joined(parts):
    return parts[0] if len(parts) == 1 else jnp.concatenate(parts, axis=0)


def place_body(offsets, with_vectors, owners, *refs):
    count = len(offsets)
    parts, out, rest = refs[:count], refs[count], refs[count + 1 :]
    sems, rows = rest[-1], out.shape[1]
    copies = []
    for part, offset in zip(parts, offsets):
        for n in range(part.shape[0]):
            at = len(copies)
            target = out.at[owners[at], :, offset : offset + part.shape[2]]
            copies.append(pltpu.make_async_copy(part.at[n], target, sems.at[at]))
    for copy in copies:
        copy.start()
    for copy in copies:
        copy.wait()
    if with_vectors:
        vectors, columns = rest[:2]
        for n in range(out.shape[0]):
            columns[n * rows : n * rows + rows, :] = out[n, :, out.shape[2] - LANES :]
        vectors[...] = columns[...].astype(F32).T


def place(parts, offsets, owners, total, cols, with_vectors=False):
    rows = parts[0].shape[1]
    whole = pl.BlockSpec(memory_space=pltpu.VMEM)
    copies = sum(p.shape[0] for p in parts)
    out_shape = [shape((total, rows, cols), BF)]
    scratch = [pltpu.SemaphoreType.DMA((copies,))]
    if with_vectors:
        out_shape.append(shape((LANES, total * rows), F32))
        scratch = [pltpu.VMEM((total * rows, LANES), BF)] + scratch
    moved = 2 * total * rows * cols
    done = pl.pallas_call(
        functools.partial(place_body, tuple(offsets), with_vectors),
        in_specs=[pl.BlockSpec(memory_space=pltpu.SMEM)]
        + [pl.BlockSpec(memory_space=pl.ANY)] * len(parts),
        out_specs=[whole] * len(out_shape),
        out_shape=out_shape,
        scratch_shapes=scratch,
        compiler_params=pltpu.CompilerParams(vmem_limit_bytes=VMEM_LIMIT),
        cost_estimate=pl.CostEstimate(flops=0, bytes_accessed=2 * moved, transcendentals=0),
        name="place",
    )(owners, *parts)
    return done[0].reshape(total * rows, cols), done[1:]


def orders():
    depth = lax.axis_size("fsdp")
    cut = max(1, depth // 2)
    return [part for part in ((0, cut, (0, 1)), (cut, depth, (1, 0))) if part[0] < part[1]]


def begin(shard):
    line = direct(shard[None], "fsdp")
    return [joined(line[low:high]) for low, high, _ in orders()]


def across(blocks, stage):
    return [joined(direct(b, AXES[o[2][stage]])) for b, o in zip(blocks, orders())]


def over(blocks):
    return [part for b in blocks for part in direct(b, "core")]


def owners_of(steps):
    sizes = [lax.axis_size(a) for a in AXES]
    here = [lax.axis_index(a) for a in AXES]
    table = jnp.asarray(steps, jnp.int32)
    owner = jnp.zeros((len(steps),), jnp.int32)
    for n, size in enumerate(sizes):
        owner = owner * size + lax.rem(here[n] - table[:, n] + size, size)
    return owner


def owner_table():
    sizes = [lax.axis_size(a) for a in AXES]
    steps = []
    for low, high, order in orders():
        for c in range(sizes[2]):
            for second in range(sizes[order[1]]):
                for first in range(sizes[order[0]]):
                    moved = {order[0]: first, order[1]: second}
                    steps += [(moved[0], moved[1], c, z) for z in range(low, high)]
    return owners_of(steps)


def exchanged(parts, axis):
    return [parts[0]] + [shifted(p, axis, d) for d, p in enumerate(parts) if d > 0]


def on_device(patches, picture_ids, norm1_gain, norm1_bias, qkv_weight, query_shift, value_shift,
              query_gain, query_bias, key_gain, out_weight, out_bias, norm2_gain, norm2_bias,
              up_weight, up_bias, down_weight, down_bias, out_grad):
    width = patches.shape[1]
    rows = qkv_weight.shape[0]
    units = up_weight.shape[1]
    folds = units // width
    side, front, cores, depth = (lax.axis_size(a) for a in AXES)
    total = side * front * cores * depth
    vectors_here = [norm1_gain, norm1_bias, query_shift, value_shift, query_gain, query_bias,
                    key_gain, out_bias, norm2_gain, norm2_bias, down_bias, up_bias]
    count = sum(v.shape[0] for v in vectors_here)
    small, at = 0.0, 0
    for v in vectors_here:
        small += jnp.pad(v.astype(F32), (at, count - at - v.shape[0]))
        at += v.shape[0]
    small = small.reshape(-1, rows)
    here = jnp.stack([lax.axis_index(a) for a in AXES]).astype(jnp.int32)
    core = here[2:3]

    second = lax.all_gather(
        pack_rest(down_weight, up_weight, out_weight), AXES, axis=0, tiled=True
    )
    one = begin(pack_first(qkv_weight, small))
    extras = (*picture_lanes(picture_ids), owner_table())
    one, extras = lax.optimization_barrier((one, extras))
    extra_q, extra_k, padding, owners = extras
    one = over(across(across(one, 0), 1))
    offsets = [0] * len(one)
    first, (vectors,) = place(one, offsets, owners, total, 3 * width + LANES, with_vectors=True)
    b_up = vectors[UP_LANE : UP_LANE + folds].reshape(folds, -1, rows).transpose(1, 0, 2)
    b_up = b_up.reshape(1, -1)

    turned, q, k, v, q_hat, k_hat, q_scale, k_scale = project(patches, first, vectors)
    att, extra_back = attend(q, k, v, extra_q, extra_k, padding)
    (mine_down, other_down, mine_up, other_up, up_sum, mixed, gx2, gy, sums_two) = hidden(
        core, att, patches, out_grad, second, vectors, b_up, rows, depth
    )
    go, mine_out, other_out = mix_back(core, gy, att, second, depth * rows)
    received = [shifted(p, "core", 1) for p in (other_down, other_up, other_out)]
    merged = merge([mine_down, mine_up, mine_out], received)
    merged, go = lax.optimization_barrier((merged, go))
    flat = merged.reshape(-1, merged.shape[2])
    flat = lax.psum_scatter(flat, AXES[:2], scatter_dimension=0, tiled=True)
    grads, sums_att = attend_back(
        q, k, v, go, att, extra_back, extra_k, padding, q_hat, k_hat, q_scale, k_scale, vectors
    )
    sums_att = sums_att.reshape(-1, 8, width).sum(axis=0)
    mine_qkv, other_qkv, mine_columns, other_columns = project_grad(
        core, turned, grads, first, sums_att, sums_two, up_sum, depth * rows
    )
    received = [shifted(p, "core", 1) for p in (other_qkv, other_columns)]
    sizes = (side, front, depth // 2 * rows)
    last = chips_one(here, [mine_qkv, mine_columns], received, sizes)
    last, flat = lax.optimization_barrier((last, flat))
    wide_out = lax.psum_scatter(flat, AXES[3], scatter_dimension=0, tiled=True)
    last = exchanged(last[0], "side"), exchanged(last[1], "front")
    last = chips_two(here, *last, sizes)
    last = exchanged(last[0], "front"), exchanged(last[1], "side")
    last = chips_three(here, *last, sizes, depth)
    last, gx2 = lax.optimization_barrier((last, gx2))
    last = exchanged(last, "fsdp")
    patches_grad = project_back(grads, first, patches, gx2, vectors)
    qkv_out, out_out, up_out, down_out, final = finish(last, wide_out, width)
    final = final.T
    (gain_one_out, bias_one_out, q_shift_out, v_shift_out, q_gain_out, q_bias_out, k_gain_out,
     gain_two_out, bias_two_out, out_bias_out, down_bias_out) = [final[n] for n in range(UP_LANE)]
    return (
        mixed, patches_grad, gain_one_out, bias_one_out, qkv_out, q_shift_out, v_shift_out,
        q_gain_out, q_bias_out, k_gain_out, out_out, out_bias_out, gain_two_out, bias_two_out,
        up_out, final[UP_LANE : UP_LANE + folds].reshape(-1), down_out, down_bias_out,
    )


def solution(mesh):
    flat = P(AXES)
    wide = P(AXES, None)
    in_specs = (wide, flat, flat, flat, wide, flat, flat, flat, flat, flat, wide, flat, flat, flat,
                wide, flat, wide, flat, wide)
    out_specs = (wide, wide, flat, flat, wide, flat, flat, flat, flat, flat, wide, flat, flat, flat,
                 wide, flat, wide, flat)
    return jax.shard_map(
        on_device, mesh=split_mesh(mesh), in_specs=in_specs, out_specs=out_specs, check_vma=False
    )
```
